512 devices in a mesh: sub: 32 (over z, y_hi, core), hgt: 16 (over y_lo, x).
Axes of the slice: x: 4, y: 8 (y_hi: 2, y_lo: 4; y = y_hi * 4 + y_lo), z: 8, core: 2. Of those that a mesh axis runs over, the one named last changes fastest.
Arguments:
- polar_beams: bfloat16 [16, 2, 512, 4096], P('hgt', None, 'sub'), may hold values from -6 to 6
- band_start: int32 [3, 2, 2, 16], replicated, may hold values from 0 to 8, as said below
- band_weight: bfloat16 [3, 2, 2, 16, 8], replicated, may hold values from -1.5 to 1.5
- phase_rate: float32 [3, 2, 2, 16], replicated, may hold values from -6 to 6
- layer_wave: float32 [16], P('hgt'), may hold values from 0.5 to 2
- beam_map: int32 [64, 2048], replicated, may hold values from 0 to 126, as said below
- range_map: int32 [64, 2048], replicated, may hold values from 0 to 4094
- pixel_frac: bfloat16 [3, 64, 2048], replicated, may hold values from 0 to 1
Outputs:
- image: float32 [64, 16, 2, 2048], P('sub', 'hgt')
The draws below stay inside these ranges and needn't reach their ends.
Inputs may be any that keep to these rules, and one draw needn't show every extreme that they name: band_start[l,k,h,j] + t for t < 8 lies within h * 8 - 8 to h * 8 + 16 / 2 + 7. beam_map[y, x] differs from x * 128 // 2048 by at most 2.
All inputs are finite; a program needn't handle non-finite values.
Results may differ from the reference program's by a relative error of at most 0.0041.
Values may be sent and summed in bfloat16 or wider, within the bound.
No kernel may reach another device: no remote copies, remote signals or barrier semaphores. Data moves between devices by JAX's collectives and lax.ppermute only.
A program may use at most 192 MiB of HBM per device.

```python
import math
import jax
import jax.numpy as jnp
import numpy as np
from jax import lax

RANGE = 4096
BEAMS = 16
TAPS = 8
LEVELS = 3
IMG_COLS = 2048
HEIGHTS = 16
TOTAL_BEAMS = 512
IMG_ROWS = 64
MERGED = 128
N_SUB = 32


def draw_band_start(key, part):
    beam_ids = jnp.arange(BEAMS, dtype=jnp.int32)
    halves = jnp.arange(2, dtype=jnp.int32)
    centre = halves[:, None] * (BEAMS // 2) + beam_ids[None, :] // 2 - TAPS // 2
    jitter = jax.random.randint(key, (LEVELS, 2, 2, BEAMS), -1, 2, dtype=jnp.int32)
    return jnp.clip(centre[None, None] + jitter, 0, BEAMS - TAPS).astype(jnp.int32)


def draw_beam_map(key, part):
    merged_count = BEAMS * 2 ** LEVELS
    columns = jnp.arange(IMG_COLS, dtype=jnp.int32)
    centre = columns * merged_count // IMG_COLS
    jitter = jax.random.randint(key, (IMG_ROWS, IMG_COLS), -2, 3, dtype=jnp.int32)
    chosen = jnp.clip(centre[None, :] + jitter, 0, merged_count - 2)
    chosen = chosen.at[0, 0].set(0).at[0, IMG_COLS - 1].set(merged_count - 2)
    return chosen.astype(jnp.int32)


def draw_range_map(key, part):
    chosen = jax.random.randint(key, (IMG_ROWS, IMG_COLS), 0, RANGE - 1, dtype=jnp.int32)
    chosen = chosen.at[0, 0].set(0).at[0, IMG_COLS - 1].set(RANGE - 2)
    return chosen.astype(jnp.int32)


def level_of(stream_key, dims, pieces, smallest, largest):
    factor_of, own = 1.0, jax.random.fold_in(stream_key, 6)
    for dim, parts in pieces:
        heights = jnp.exp(jax.random.uniform(jax.random.fold_in(own, dim), (parts,), jnp.float32, smallest / len(pieces), largest / len(pieces)))
        factor_of = factor_of * jnp.repeat(heights, dims[dim] // parts).reshape([-1 if axis == dim else 1 for axis in range(len(dims))])
    return factor_of


def bell_draw(rng, shape, scale, limit, pieces=(), kind=jnp.bfloat16):
    entries = jax.random.normal(rng, shape, jnp.float32) * scale
    if len(pieces) > 0:
        entries = level_of(rng, shape, pieces, -0.22, 0.18) * entries
    return jnp.clip(entries, min=-limit, max=limit).astype(kind)


def setup_inputs(seed: int = 0) -> dict:
    streams_of = jax.random.split(jax.random.key(seed), 9)
    polar_beams = bell_draw(streams_of[0], (HEIGHTS, 2, TOTAL_BEAMS, RANGE), 1.0, 6.0, ((0, 16), (2, 32)))
    band_start = draw_band_start(jax.random.fold_in(streams_of[8], 71), 0)
    band_weight = bell_draw(streams_of[2], (LEVELS, 2, 2, BEAMS, TAPS), 0.25, 1.5)
    phase_rate = jnp.clip(jax.random.uniform(streams_of[3], (LEVELS, 2, 2, BEAMS), jnp.float32, -6.0, 6.0), -6.0, 6.0)
    layer_wave = jnp.clip(jnp.exp(math.log(2.0) - 1.3862944 * jax.random.uniform(streams_of[4], (HEIGHTS,), jnp.float32) ** level_of(streams_of[4], (HEIGHTS,), ((0, 16),), -0.2, 0.2)), 0.5, 2.0)
    beam_map = draw_beam_map(jax.random.fold_in(streams_of[8], 71), 0)
    range_map = draw_range_map(jax.random.fold_in(streams_of[8], 71), 0)
    pixel_frac = jnp.clip(jax.random.uniform(streams_of[7], (3, IMG_ROWS, IMG_COLS), jnp.float32, 0.0, 1.0), 0.0, 1.0).astype(jnp.bfloat16)
    return dict(polar_beams=polar_beams, band_start=band_start, band_weight=band_weight, phase_rate=phase_rate, layer_wave=layer_wave, beam_map=beam_map, range_map=range_map, pixel_frac=pixel_frac)


range_phase = 0.003


def rotate(real_part, imag_part, angles):
    cosine = jnp.cos(angles)
    sine_part = jnp.sin(angles)
    return cosine * real_part - sine_part * imag_part, sine_part * real_part + cosine * imag_part


def reverse_bits(value, width):
    result = 0
    for bit_idx in range(width):
        result = result * 2 + ((value >> bit_idx) & 1)
    return result


def band_apply(values, starts, weights):
    accumulated = jnp.zeros(values.shape[:3] + (BEAMS, RANGE), jnp.float32)
    for tap_idx in range(TAPS):
        accumulated = accumulated + weights[:, tap_idx][:, None] * jnp.take(values, (starts + tap_idx).astype(jnp.int32), axis=3)
    return accumulated


def reference(polar_beams, band_start, band_weight, phase_rate, layer_wave, beam_map, range_map, pixel_frac):
    range_pos = (jnp.arange(RANGE, dtype=jnp.float32) + 0.5) / RANGE
    beam_frac = pixel_frac[0].astype(jnp.float32)
    range_fr = pixel_frac[1].astype(jnp.float32)
    height_frac = pixel_frac[2].astype(jnp.float32)
    groups = N_SUB // 2 ** LEVELS
    sector_device = np.array([reverse_bits(sector, LEVELS) for sector in range(2 ** LEVELS)], dtype=np.int32)

    def merge_section(current, section, wavenumber):
        values = current.astype(jnp.float32).reshape(2, N_SUB // 2 ** (section + 1), 2, 2 ** section, BEAMS, RANGE)
        halves = []
        for my_half in range(2):
            summed = None
            for child in range(2):
                shifted = band_apply(values[:, :, child], band_start[section, child, my_half], band_weight[section, child, my_half].astype(jnp.float32))
                angles = wavenumber * phase_rate[section, child, my_half][:, None] * range_pos[None, :]
                real_part, imag_part = rotate(shifted[0], shifted[1], angles[None, None])
                term = jnp.stack([real_part, imag_part])
                summed = term if child == 0 else summed + term
            halves.append(summed)
        return jnp.stack(halves, axis=2).reshape(2, N_SUB, BEAMS, RANGE)

    def one_layer(inputs):
        layer_beams, wavenumber = inputs
        current = layer_beams.reshape(2, N_SUB, BEAMS, RANGE)
        for section in range(LEVELS):
            merged_out = merge_section(current, section, wavenumber)
            current = merged_out.astype(jnp.bfloat16) if section + 1 < LEVELS else merged_out
        ordered = current.reshape(2, groups, 2 ** LEVELS, BEAMS, RANGE)[:, :, sector_device]
        flat_polar = ordered.reshape(2, groups, MERGED * RANGE)
        summed = jnp.zeros((2, IMG_ROWS, IMG_COLS), jnp.float32)
        for beam_step in range(2):
            beam_part = beam_frac if beam_step else 1.0 - beam_frac
            for range_step in range(2):
                pair_weight = beam_part * (range_fr if range_step else 1.0 - range_fr)
                flat_index = ((beam_map + beam_step) * RANGE + range_map + range_step).reshape(-1).astype(jnp.int32)
                sampled = jnp.sum(jnp.take(flat_polar, flat_index, axis=2), axis=1).reshape(2, IMG_ROWS, IMG_COLS)
                summed = summed + pair_weight[None] * sampled
        angles = wavenumber * range_phase * (range_map.astype(jnp.float32) + range_fr)
        real_part, imag_part = rotate(summed[0], summed[1], angles)
        return jnp.stack([real_part, imag_part])

    cart = lax.map(one_layer, (polar_beams, layer_wave))
    upper_layers = jnp.concatenate([cart[1:], jnp.zeros_like(cart[:1])], axis=0)
    blended = (1.0 - height_frac)[None, None] * cart + height_frac[None, None] * upper_layers
    return jnp.transpose(blended, (2, 0, 1, 3))
```

```python
import functools

import jax
import jax.numpy as jnp
from jax import lax
from jax.experimental import pallas as pl
from jax.experimental.pallas import tpu as pltpu
from jax.sharding import PartitionSpec as P

range_phase = 0.003
LANES = 128
WINDOW = 16
HALO = 4
BLOCK = 256


def merge_kernel(
    place_ref, wave_ref, data_ref, params_ref, out_ref, padded_ref, *, levels, groups, range_count
):
    beams = data_ref.shape[2]
    members = 2**levels
    wave = wave_ref[0]
    params = params_ref[...]
    matrices = levels * 4
    lane = lax.broadcasted_iota(jnp.int32, (1, LANES), 1)
    position = ((place_ref[0] * LANES + lane).astype(jnp.float32) + 0.5) / range_count
    taps = (params.shape[1] - 2 * matrices) // matrices
    cosines, sines, bands = {}, {}, []
    col_ids = lax.broadcasted_iota(jnp.int32, (beams, 2 * beams), 1).astype(jnp.float32)
    for level in range(levels):
        blocks = []
        for half in range(2):
            for child in range(2):
                i = (level * 2 + child) * 2 + half
                angles = (wave * params[:, i : i + 1]) * position
                cosines[level, child, half] = jnp.cos(angles)
                sines[level, child, half] = jnp.sin(angles)
                offsets = col_ids - (params[:, matrices + i : matrices + i + 1] + child * beams)
                block = jnp.zeros((beams, 2 * beams), jnp.float32)
                for tap in range(taps):
                    c = 2 * matrices + i * taps + tap
                    block = jnp.where(offsets == tap, params[:, c : c + 1], block)
                blocks.append(block)
        bands.append(jnp.concatenate(blocks, axis=0).astype(jnp.bfloat16))
    total = [None] * members
    for group in range(groups):
        current = [
            [data_ref[group * members + s, part] for part in range(2)] for s in range(members)
        ]
        for level in range(levels):
            lows = [s for s in range(members) if not s >> level & 1]
            highs = [s | 1 << level for s in lows]
            stacked = jnp.concatenate(
                [
                    jnp.concatenate([current[s][part] for s in rows for part in range(2)], axis=1)
                    for rows in (lows, highs)
                ],
                axis=0,
            )
            product = jnp.dot(bands[level], stacked, preferred_element_type=jnp.float32)
            following = [None] * members
            for pair, s in enumerate(lows):
                for half in range(2):
                    summed = None
                    for child in range(2):
                        row = (half * 2 + child) * beams
                        real = product[row : row + beams, pair * 2 * LANES : (pair * 2 + 1) * LANES]
                        imag = product[
                            row : row + beams, (pair * 2 + 1) * LANES : (pair * 2 + 2) * LANES
                        ]
                        cosine, sine = cosines[level, child, half], sines[level, child, half]
                        term = (cosine * real - sine * imag, sine * real + cosine * imag)
                        summed = term if child == 0 else (summed[0] + term[0], summed[1] + term[1])
                    if level + 1 < levels:
                        summed = tuple(v.astype(jnp.bfloat16) for v in summed)
                    following[s | half << level] = summed
            current = following
        for s in range(members):
            total[s] = (
                current[s]
                if group == 0
                else (total[s][0] + current[s][0], total[s][1] + current[s][1])
            )
    merged = beams * members
    padding = padded_ref.shape[1] - HALO - merged
    for part in range(2):
        padded_ref[part, 0:HALO, :] = jnp.zeros((HALO, LANES), jnp.float32)
        padded_ref[part, HALO + merged :, :] = jnp.zeros((padding, LANES), jnp.float32)
        for s in range(members):
            sector = 0
            for bit in range(levels):
                sector = sector * 2 + (s >> bit & 1)
            start = HALO + sector * beams
            padded_ref[part, start : start + beams, :] = total[s][part]
    for block in range(out_ref.shape[0] // 2):
        low = 4 * (block >> 1) + (block & 1)
        for part in range(2):
            rows = padded_ref[part, 8 * block : 8 * block + WINDOW, :].astype(jnp.bfloat16)
            out_ref[low, part] = rows
            out_ref[low + 2, part] = rows


def sample_kernel(
    place_ref,
    wave_ref,
    table_ref,
    beam_ref,
    range_ref,
    frac_ref,
    out_ref,
    lhs_ref,
    frac_scratch,
    cart_ref,
):
    slices = table_ref.shape[0]
    per_block = BLOCK // LANES
    blocks = slices // per_block
    lane = lax.broadcasted_iota(jnp.int32, (WINDOW, LANES), 1)
    for part in range(2):
        rolled = [
            pltpu.roll(table_ref[i, part].astype(jnp.float32), LANES - 1, 1) for i in range(slices)
        ]
        for i in range(slices):
            shifted = jnp.where(lane < LANES - 1, rolled[i], rolled[(i + 1) % slices])
            row = (i // per_block) * 4 * WINDOW + part * WINDOW
            col = (i % per_block) * LANES
            lhs_ref[row : row + WINDOW, col : col + LANES] = table_ref[i, part]
            row = row + 2 * WINDOW
            lhs_ref[row : row + WINDOW, col : col + LANES] = shifted.astype(jnp.bfloat16)
    frac_scratch[...] = frac_ref[...].astype(jnp.float32)
    column_block = place_ref[1]
    row_half = place_ref[2]
    first_beam = column_block * 8 - HALO
    pixels = 4 * LANES
    rows_iota = lax.broadcasted_iota(jnp.int32, (BLOCK, pixels), 0)
    beam_iota = lax.broadcasted_iota(jnp.int32, (WINDOW, pixels), 0)

    def flat(value):
        return jnp.concatenate([value[i : i + 1, :] for i in range(4)], axis=1)

    def chunk(step, carry):
        start = step * 8 + row_half * 4
        samples = flat(range_ref[pl.ds(start, 4), :])
        beam = flat(beam_ref[pl.ds(start, 4), :]) - first_beam
        frac0 = flat(frac_scratch[0, pl.ds(start, 4), :])
        frac1 = flat(frac_scratch[1, pl.ds(start, 4), :])
        inner = samples & (BLOCK - 1)
        outer = samples >> (BLOCK.bit_length() - 1)
        hot = jnp.where(rows_iota == inner, 1.0, 0.0).astype(jnp.bfloat16)
        product = jnp.dot(lhs_ref[...], hot, preferred_element_type=jnp.float32)
        picked = product[0 : 4 * WINDOW]
        for k in range(1, blocks):
            picked = jnp.where(
                outer == k, product[k * 4 * WINDOW : (k + 1) * 4 * WINDOW], picked
            )
        weights = jnp.where(
            beam_iota == beam, 1.0 - frac0, jnp.where(beam_iota == beam + 1, frac0, 0.0)
        )
        low_weights = weights * (1.0 - frac1)
        high_weights = weights * frac1
        for part in range(2):
            low = picked[part * WINDOW : (part + 1) * WINDOW]
            high = picked[(2 + part) * WINDOW : (3 + part) * WINDOW]
            summed = jnp.sum(low_weights * low + high_weights * high, axis=0, keepdims=True)
            for i in range(4):
                cart_ref[part, pl.ds(step * 4 + i, 1), :] = summed[:, i * LANES : (i + 1) * LANES]
        angle_scale = wave_ref[0] * range_phase
        angles = angle_scale * (samples.astype(jnp.float32) + frac1)
        for i in range(4):
            cart_ref[2, pl.ds(step * 4 + i, 1), :] = angles[:, i * LANES : (i + 1) * LANES]
        return carry

    lax.fori_loop(0, range_ref.shape[0] // 8, chunk, 0)
    real, imag, angles = cart_ref[0], cart_ref[1], cart_ref[2]
    cosine, sine = jnp.cos(angles), jnp.sin(angles)
    cart_ref[0] = cosine * real - sine * imag
    cart_ref[1] = sine * real + cosine * imag
    for row in range(cart_ref.shape[1]):
        for part in range(2):
            out_ref[row // 2, row % 2, part, :] = cart_ref[part, row, :]


def body(
    polar_beams,
    band_start,
    band_weight,
    phase_rate,
    layer_wave,
    beam_map,
    range_map,
    pixel_frac,
    *,
    interpret=False,
):
    sub_index = lax.axis_index("sub")
    sub_count = lax.axis_size("sub")
    beams = polar_beams.shape[2]
    range_count = polar_beams.shape[3]
    levels = band_start.shape[0]
    taps = band_weight.shape[-1]
    row_count, column_count = beam_map.shape
    matrices = levels * 4
    column_block = (sub_index >> 2) * 2 + (sub_index & 1)
    row_half = sub_index >> 1 & 1
    place = jnp.stack([sub_index, column_block, row_half]).astype(jnp.int32)
    params = jnp.concatenate(
        [
            phase_rate.reshape(matrices, beams),
            band_start.reshape(matrices, beams).astype(jnp.float32),
            band_weight.reshape(matrices, beams, taps)
            .transpose(0, 2, 1)
            .reshape(matrices * taps, beams)
            .astype(jnp.float32),
        ],
        axis=0,
    ).T

    slices = polar_beams.reshape(2, beams, sub_count, LANES).transpose(2, 0, 1, 3)
    slices = lax.all_to_all(slices, "sub", 0, 0, tiled=True)
    smem = pl.BlockSpec(memory_space=pltpu.SMEM)
    vmem = pl.BlockSpec(memory_space=pltpu.VMEM)
    windows = pl.pallas_call(
        functools.partial(
            merge_kernel,
            levels=levels,
            groups=sub_count // 2**levels,
            range_count=range_count,
        ),
        out_shape=jax.ShapeDtypeStruct((sub_count, 2, WINDOW, LANES), jnp.bfloat16),
        in_specs=[smem, smem, vmem, vmem],
        out_specs=vmem,
        scratch_shapes=[pltpu.VMEM((2, 144, LANES), jnp.float32)],
        interpret=interpret,
        name="merge",
    )(place, layer_wave, slices, params)
    table = lax.all_to_all(windows, "sub", 0, 0, tiled=True)
    rows = row_count // 2
    cart = pl.pallas_call(
        sample_kernel,
        out_shape=jax.ShapeDtypeStruct((rows // 2, 2, 2, LANES), jnp.float32),
        grid_spec=pltpu.PrefetchScalarGridSpec(
            num_scalar_prefetch=1,
            grid=(1,),
            in_specs=[
                smem,
                pl.BlockSpec(table.shape, lambda i, p: (0, 0, 0, 0)),
                pl.BlockSpec((row_count, LANES), lambda i, p: (0, p[1])),
                pl.BlockSpec((row_count, LANES), lambda i, p: (0, p[1])),
                pl.BlockSpec((3, row_count, LANES), lambda i, p: (0, 0, p[1])),
            ],
            out_specs=pl.BlockSpec((rows // 2, 2, 2, LANES), lambda i, p: (0, 0, 0, 0)),
            scratch_shapes=[
                pltpu.VMEM((range_count // BLOCK * 4 * WINDOW, BLOCK), jnp.bfloat16),
                pltpu.VMEM((3, row_count, LANES), jnp.float32),
                pltpu.VMEM((3, rows, LANES), jnp.float32),
            ],
        ),
        interpret=interpret,
        name="sample",
    )(place, layer_wave, table, beam_map, range_map, pixel_frac)
    halves = [[s for s in range(sub_count) if s >> 1 & 1 == half] for half in range(2)]
    tile = lax.all_to_all(cart, "sub", 0, 0, axis_index_groups=halves, tiled=True)
    layers = lax.axis_size("hgt")
    above = lax.ppermute(tile, "hgt", [(i, i - 1) for i in range(1, layers)])
    tile_rows = row_count // sub_count
    height_frac = lax.dynamic_slice_in_dim(
        pixel_frac[2], sub_index * tile_rows, tile_rows, 0
    ).astype(jnp.float32)
    height_frac = height_frac.reshape(tile_rows, column_count // LANES, LANES).transpose(1, 0, 2)
    height_frac = height_frac[:, :, None, :]
    blended = (1.0 - height_frac) * tile + height_frac * above
    return blended.transpose(1, 2, 0, 3).reshape(tile_rows, 1, 2, column_count)


def solution(mesh):
    in_specs = (P("hgt", None, "sub", None), P(), P(), P(), P("hgt"), P(), P(), P())
    out_specs = P("sub", "hgt", None, None)
    return jax.shard_map(body, mesh=mesh, in_specs=in_specs, out_specs=out_specs, check_vma=False)
```

```python
import functools

import jax
import jax.numpy as jnp
from jax import lax
from jax.experimental import pallas as pl
from jax.experimental.pallas import tpu as pltpu
from jax.sharding import PartitionSpec as P

range_phase = 0.003
LANES = 128
WINDOW = 16
HALO = 4
QUARTER = 8
ROWS = 64


def split_kernel(source_ref, out_ref):
    width = out_ref.shape[3]
    for i in range(out_ref.shape[0]):
        for part in range(out_ref.shape[1]):
            out_ref[i, part] = source_ref[0, part, :, i * width : (i + 1) * width]


def swap_quarters(values):
    lane = lax.broadcasted_iota(jnp.int32, values[0].shape, 1)
    values = list(values)
    for bit, width in ((1, 64), (0, 32)):
        keep = lane & width == 0
        for i in range(4):
            if i >> bit & 1:
                continue
            j = i | 1 << bit
            a, b = values[i], values[j]
            values[i] = jnp.where(keep, a, pltpu.roll(b, width, 1))
            values[j] = jnp.where(keep, pltpu.roll(a, LANES - width, 1), b)
    return values


def prepare_kernel(
    place_ref,
    wave_ref,
    params_ref,
    beam_ref,
    range_ref,
    frac_ref,
    trig_ref,
    first_ref,
    second_ref,
    third_ref,
    whole_ref,
    real_ref,
    pixel_ref,
    *,
    range_count,
):
    wave = wave_ref[0]
    params = params_ref[...]
    beams = params.shape[0]
    matrices = 12
    taps = (params.shape[1] - 2 * matrices) // matrices
    width = trig_ref.shape[3]
    lane = lax.broadcasted_iota(jnp.int32, (1, width), 1)
    position = ((place_ref[0] * width + lane).astype(jnp.float32) + 0.5) / range_count
    row_half = place_ref[1]
    upper = row_half == 1

    def column(offset, level, child, half):
        i = offset + (level * 2 + child) * 2 + half
        return params[:, i : i + 1]

    def mine(offset, level, half):
        return jnp.where(upper, column(offset, level, 1, half), column(offset, level, 0, half))

    def weight(tap, level, child, half):
        i = 2 * matrices + ((level * 2 + child) * 2 + half) * taps + tap
        return params[:, i : i + 1]

    rates = [column(0, 0, child, half) for half in range(2) for child in range(2)]
    rates += [mine(0, 1, half) for half in range(2)]
    rates += [column(0, 2, child, half) for half in range(2) for child in range(2)]
    for i, rate in enumerate(rates):
        angles = (wave * rate) * position
        trig_ref[i, 0] = jnp.cos(angles)
        trig_ref[i, 1] = jnp.sin(angles)

    def band(starts, weights):
        ids = lax.broadcasted_iota(jnp.int32, (beams, beams), 1).astype(jnp.float32) - starts
        block = jnp.zeros((beams, beams), jnp.float32)
        for tap in range(taps):
            block = jnp.where(ids == tap, weights[tap], block)
        return block

    def pair_bands(level, copies):
        rows = []
        for half in range(2):
            for child in range(2):
                block = band(
                    column(matrices, level, child, half),
                    [weight(tap, level, child, half) for tap in range(taps)],
                )
                empty = jnp.zeros_like(block)
                rows.append(
                    jnp.concatenate(
                        [block if c == child else empty for c in range(2) for _ in range(copies)],
                        axis=1,
                    )
                )
        return jnp.concatenate(rows, axis=0).astype(jnp.bfloat16)

    first_ref[...] = pair_bands(0, 1)
    third_ref[...] = pair_bands(2, 2)
    rows = []
    for half in range(2):
        block = band(
            mine(matrices, 1, half),
            [
                jnp.where(upper, weight(tap, 1, 1, half), weight(tap, 1, 0, half))
                for tap in range(taps)
            ],
        )
        rows.append(jnp.concatenate([block, block], axis=1))
    second_ref[...] = jnp.concatenate(rows, axis=0).astype(jnp.bfloat16)

    samples = range_ref[...]
    fracs = [frac_ref[i].astype(jnp.float32) for i in range(3)]
    angles = (wave * range_phase) * (samples.astype(jnp.float32) + fracs[1])
    pixel_ref[0] = jnp.cos(angles)
    pixel_ref[1] = jnp.sin(angles)
    pixel_ref[2] = fracs[2]
    first_beam = place_ref[2] * 8 - HALO
    for group in range(ROWS // 32):
        rows = [slice(group * 32 + 8 * j, group * 32 + 8 * j + 8) for j in range(4)]
        sample_parts = swap_quarters([samples[r] for r in rows])
        beam_parts = swap_quarters([beam_ref[r, :] - first_beam for r in rows])
        frac_parts = [swap_quarters([fracs[i][r] for r in rows]) for i in range(2)]
        for quarter in range(4):
            place = slice(quarter * 16 + group * 8, quarter * 16 + group * 8 + 8)
            whole_ref[0, place, :] = sample_parts[quarter] & (width - 1)
            whole_ref[1, place, :] = sample_parts[quarter] >> (width.bit_length() - 1)
            whole_ref[2, place, :] = beam_parts[quarter] - (2 * quarter + 2)
            for i in range(2):
                real_ref[i, place, :] = frac_parts[i][quarter]


def halves_of(value):
    high = value.astype(jnp.bfloat16)
    return high, (value - high.astype(jnp.float32)).astype(jnp.bfloat16)


def merge_kernel(
    data_ref, trig_ref, first_ref, second_ref, third_ref, out_ref, padded_ref, *, groups
):
    beams, width = data_ref.shape[2], data_ref.shape[3]

    def turn(i, product, row, col):
        real = product[row : row + beams, col : col + width]
        imag = product[row : row + beams, col + width : col + 2 * width]
        cosine, sine = trig_ref[i, 0], trig_ref[i, 1]
        return cosine * real - sine * imag, sine * real + cosine * imag

    def add(a, b):
        return a[0] + b[0], a[1] + b[1]

    sums = {}
    for low in range(2):
        for group in range(groups):
            source = (group * 2 + low) * 2
            stacked = jnp.concatenate(
                [
                    jnp.concatenate([data_ref[source + core, part] for part in range(2)], axis=1)
                    for core in range(2)
                ],
                axis=0,
            )
            product = jnp.dot(first_ref[...], stacked, preferred_element_type=jnp.float32)
            for half in range(2):
                terms = [
                    turn(half * 2 + child, product, (half * 2 + child) * beams, 0)
                    for child in range(2)
                ]
                level = tuple(
                    v.astype(jnp.bfloat16).astype(jnp.float32) for v in add(terms[0], terms[1])
                )
                sums[low, half] = level if group == 0 else add(sums[low, half], level)
    middle = {}
    for low in range(2):
        for half in range(2):
            parts = [halves_of(v) for v in sums[low, half]]
            stacked = jnp.concatenate(
                [jnp.concatenate([parts[0][i], parts[1][i]], axis=1) for i in range(2)], axis=0
            )
            product = jnp.dot(second_ref[...], stacked, preferred_element_type=jnp.float32)
            for next_half in range(2):
                middle[low, half, next_half] = turn(4 + next_half, product, next_half * beams, 0)
    merged = 8 * beams
    padding = padded_ref.shape[1] - HALO - merged
    for part in range(2):
        padded_ref[part, 0:HALO, :] = jnp.zeros((HALO, width), jnp.float32)
        padded_ref[part, HALO + merged :, :] = jnp.zeros((padding, width), jnp.float32)
    for half in range(2):
        for next_half in range(2):
            rows = []
            for low in range(2):
                parts = [halves_of(v) for v in middle[low, half, next_half]]
                rows += [jnp.concatenate([parts[0][i], parts[1][i]], axis=1) for i in range(2)]
            product = jnp.dot(
                third_ref[...], jnp.concatenate(rows, axis=0), preferred_element_type=jnp.float32
            )
            for last in range(2):
                terms = [
                    turn(6 + last * 2 + child, product, (last * 2 + child) * beams, 0)
                    for child in range(2)
                ]
                start = HALO + (half * 4 + next_half * 2 + last) * beams
                for part, value in enumerate(add(terms[0], terms[1])):
                    padded_ref[part, start : start + beams, :] = value
    for block in range(out_ref.shape[0]):
        for part in range(2):
            rows = padded_ref[part, 8 * block : 8 * block + WINDOW, :]
            out_ref[block, part] = rows.astype(jnp.bfloat16)


def sample_kernel(
    table_ref, whole_ref, real_ref, pixel_ref, out_ref, pair_ref, lhs_ref, cart_ref
):
    blocks, parts, _, width = table_ref.shape
    rows = 2 * parts * QUARTER
    lane = lax.broadcasted_iota(jnp.int32, (WINDOW, width), 1)
    for part in range(parts):
        values = [table_ref[i, part].astype(jnp.float32) for i in range(blocks)]
        rolled = [pltpu.roll(v, width - 1, 1) for v in values]
        for i in range(blocks):
            pair_ref[0, i, part] = values[i]
            pair_ref[1, i, part] = jnp.where(
                lane < width - 1, rolled[i], rolled[(i + 1) % blocks]
            )
    for quarter in range(4):
        low = 2 * quarter + 2
        for i in range(blocks):
            for tap in range(2):
                pair = [pair_ref[tap, i, part, low : low + QUARTER, :] for part in range(parts)]
                row = i * rows + tap * parts * QUARTER
                lhs_ref[quarter, row : row + parts * QUARTER, :] = jnp.concatenate(
                    pair, axis=0
                ).astype(jnp.bfloat16)
    pixels = 4 * LANES
    row_ids = lax.broadcasted_iota(jnp.int32, (width, pixels), 0)
    beam_ids = lax.broadcasted_iota(jnp.int32, (QUARTER, pixels), 0)

    def flat(value):
        return jnp.concatenate([value[i : i + 1, :] for i in range(4)], axis=1)

    def chunk(step, carry):
        place = pl.ds(step * 4, 4)
        inner, outer, beam = (flat(whole_ref[i, place, :]) for i in range(3))
        frac0, frac1 = (flat(real_ref[i, place, :]) for i in range(2))
        hot = jnp.where(row_ids == inner, 1.0, 0.0).astype(jnp.bfloat16)
        product = jnp.dot(lhs_ref[step >> 2], hot, preferred_element_type=jnp.float32)
        picked = product[0:rows]
        for k in range(1, blocks):
            picked = jnp.where(outer == k, product[k * rows : (k + 1) * rows], picked)
        weights = jnp.where(
            beam_ids == beam, 1.0 - frac0, jnp.where(beam_ids == beam + 1, frac0, 0.0)
        )
        low_weights = weights * (1.0 - frac1)
        high_weights = weights * frac1
        for part in range(parts):
            low = picked[part * QUARTER : (part + 1) * QUARTER]
            high = picked[(parts + part) * QUARTER : (parts + part + 1) * QUARTER]
            summed = jnp.sum(low_weights * low + high_weights * high, axis=0, keepdims=True)
            for i in range(4):
                cart_ref[part, pl.ds(step * 4 + i, 1), :] = summed[:, i * LANES : (i + 1) * LANES]
        return carry

    lax.fori_loop(0, whole_ref.shape[1] // 4, chunk, 0)
    for group in range(ROWS // 32):
        ordered = [
            swap_quarters(
                [
                    cart_ref[part, quarter * 16 + group * 8 : quarter * 16 + group * 8 + 8, :]
                    for quarter in range(4)
                ]
            )
            for part in range(parts)
        ]
        for j in range(4):
            start = group * 32 + 8 * j
            cosine = pixel_ref[0, start : start + 8, :]
            sine = pixel_ref[1, start : start + 8, :]
            real, imag = ordered[0][j], ordered[1][j]
            out_ref[pl.ds(2 * start, 8, stride=2), :] = cosine * real - sine * imag
            out_ref[pl.ds(2 * start + 1, 8, stride=2), :] = sine * real + cosine * imag


def body(
    polar_beams,
    band_start,
    band_weight,
    phase_rate,
    layer_wave,
    beam_map,
    range_map,
    pixel_frac,
    *,
    interpret=False,
):
    sub_index = lax.axis_index("sub")
    sub_count = lax.axis_size("sub")
    layers = lax.axis_size("hgt")
    beams = polar_beams.shape[2]
    range_count = polar_beams.shape[3]
    levels = band_start.shape[0]
    taps = band_weight.shape[-1]
    row_count, column_count = beam_map.shape
    matrices = levels * 4
    members = sub_count // 2
    width = range_count // members
    column_block = (sub_index >> 2) * 2 + (sub_index & 1)
    row_half = sub_index >> 1 & 1
    halves = [[s for s in range(sub_count) if s >> 1 & 1 == half] for half in range(2)]
    place = jnp.stack([column_block, row_half, column_block]).astype(jnp.int32)
    params = jnp.concatenate(
        [
            phase_rate.reshape(matrices, beams),
            band_start.reshape(matrices, beams).astype(jnp.float32),
            band_weight.reshape(matrices, beams, taps)
            .transpose(0, 2, 1)
            .reshape(matrices * taps, beams)
            .astype(jnp.float32),
        ],
        axis=0,
    ).T
    smem = pl.BlockSpec(memory_space=pltpu.SMEM)
    vmem = pl.BlockSpec(memory_space=pltpu.VMEM)
    shape = jax.ShapeDtypeStruct
    f32, bf16 = jnp.float32, jnp.bfloat16

    slices = pl.pallas_call(
        split_kernel,
        out_shape=shape((members, 2, beams, width), bf16),
        in_specs=[vmem],
        out_specs=vmem,
        interpret=interpret,
        name="split",
    )(polar_beams)
    slices = lax.all_to_all(slices, "sub", 0, 0, axis_index_groups=halves, tiled=True)
    trig, first, second, third, whole, real, pixel = pl.pallas_call(
        functools.partial(prepare_kernel, range_count=range_count),
        out_shape=[
            shape((10, 2, beams, width), f32),
            shape((4 * beams, 2 * beams), bf16),
            shape((2 * beams, 2 * beams), bf16),
            shape((4 * beams, 4 * beams), bf16),
            shape((3, row_count, LANES), jnp.int32),
            shape((2, row_count, LANES), f32),
            shape((3, row_count, LANES), f32),
        ],
        grid_spec=pltpu.PrefetchScalarGridSpec(
            num_scalar_prefetch=1,
            grid=(1,),
            in_specs=[
                smem,
                pl.BlockSpec((beams, params.shape[1]), lambda i, p: (0, 0)),
                pl.BlockSpec((row_count, LANES), lambda i, p: (0, p[0])),
                pl.BlockSpec((row_count, LANES), lambda i, p: (0, p[0])),
                pl.BlockSpec((3, row_count, LANES), lambda i, p: (0, 0, p[0])),
            ],
            out_specs=[
                pl.BlockSpec((10, 2, beams, width), lambda i, p: (0, 0, 0, 0)),
                pl.BlockSpec((4 * beams, 2 * beams), lambda i, p: (0, 0)),
                pl.BlockSpec((2 * beams, 2 * beams), lambda i, p: (0, 0)),
                pl.BlockSpec((4 * beams, 4 * beams), lambda i, p: (0, 0)),
                pl.BlockSpec((3, row_count, LANES), lambda i, p: (0, 0, 0)),
                pl.BlockSpec((2, row_count, LANES), lambda i, p: (0, 0, 0)),
                pl.BlockSpec((3, row_count, LANES), lambda i, p: (0, 0, 0)),
            ],
        ),
        interpret=interpret,
        name="prepare",
    )(place, layer_wave, params, beam_map, range_map, pixel_frac)
    windows = pl.pallas_call(
        functools.partial(merge_kernel, groups=sub_count // 2**levels),
        out_shape=shape((members, 2, WINDOW, width), bf16),
        in_specs=[vmem] * 5,
        out_specs=vmem,
        scratch_shapes=[pltpu.VMEM((2, 144, width), f32)],
        interpret=interpret,
        name="merge",
    )(slices, trig, first, second, third)
    table = lax.all_to_all(windows, "sub", 0, 0, axis_index_groups=halves, tiled=True)
    cart = pl.pallas_call(
        sample_kernel,
        out_shape=shape((2 * row_count, LANES), f32),
        in_specs=[vmem] * 4,
        out_specs=vmem,
        scratch_shapes=[
            pltpu.VMEM((2, members, 2, WINDOW, width), f32),
            pltpu.VMEM((4, members * 4 * QUARTER, width), bf16),
            pltpu.VMEM((2, row_count, LANES), f32),
        ],
        interpret=interpret,
        name="sample",
    )(table, whole, real, pixel)
    above = lax.ppermute(cart, "hgt", [(i, i - 1) for i in range(1, layers)])
    height_frac = pixel[2][:, None, :]
    blended = (1.0 - height_frac) * cart.reshape(row_count, 2, LANES) + (
        height_frac * above.reshape(row_count, 2, LANES)
    )
    tile_rows = row_count // sub_count
    blended = blended.reshape(sub_count, tile_rows * 2, LANES)
    tiles = lax.all_to_all(blended, "sub", 0, 0, tiled=True)
    tiles = tiles.reshape(sub_count // 4, 2, 2, tile_rows * 2, LANES)
    tiles = (tiles[:, 0] + tiles[:, 1]).reshape(members, tile_rows * 2, LANES)
    return tiles.transpose(1, 0, 2).reshape(tile_rows, 1, 2, column_count)


def solution(mesh):
    in_specs = (P("hgt", None, "sub", None), P(), P(), P(), P("hgt"), P(), P(), P())
    out_specs = P("sub", "hgt", None, None)
    return jax.shard_map(body, mesh=mesh, in_specs=in_specs, out_specs=out_specs, check_vma=False)
```

```python
import functools

import jax
import jax.numpy as jnp
from jax import lax
from jax.experimental import pallas as pl
from jax.experimental.pallas import tpu as pltpu
from jax.sharding import PartitionSpec as P

range_phase = 0.003
LANES = 128
WINDOW = 16
HALO = 4
QUARTER = 8
ROWS = 64


def split_kernel(source_ref, out_ref):
    width = out_ref.shape[3]
    for i in range(out_ref.shape[0]):
        for part in range(out_ref.shape[1]):
            out_ref[i, part] = source_ref[0, part, :, i * width : (i + 1) * width]


def swap_quarters(values):
    lane = lax.broadcasted_iota(jnp.int32, values[0].shape, 1)
    values = list(values)
    for bit, width in ((1, 64), (0, 32)):
        keep = lane & width == 0
        for i in range(4):
            if i >> bit & 1:
                continue
            j = i | 1 << bit
            a, b = values[i], values[j]
            values[i] = jnp.where(keep, a, pltpu.roll(b, width, 1))
            values[j] = jnp.where(keep, pltpu.roll(a, LANES - width, 1), b)
    return values


def prepare_kernel(
    place_ref,
    wave_ref,
    params_ref,
    beam_ref,
    range_ref,
    frac_ref,
    trig_ref,
    first_ref,
    second_ref,
    third_ref,
    whole_ref,
    real_ref,
    pixel_ref,
    height_ref,
    *,
    range_count,
):
    wave = wave_ref[0]
    params = params_ref[...]
    beams = params.shape[0]
    matrices = 12
    taps = (params.shape[1] - 2 * matrices) // matrices
    width = trig_ref.shape[3]
    lane = lax.broadcasted_iota(jnp.int32, (1, width), 1)
    position = ((place_ref[0] * width + lane).astype(jnp.float32) + 0.5) / range_count
    row_half = place_ref[1]
    upper = row_half == 1

    def column(offset, level, child, half):
        i = offset + (level * 2 + child) * 2 + half
        return params[:, i : i + 1]

    def mine(offset, level, half):
        return jnp.where(upper, column(offset, level, 1, half), column(offset, level, 0, half))

    def weight(tap, level, child, half):
        i = 2 * matrices + ((level * 2 + child) * 2 + half) * taps + tap
        return params[:, i : i + 1]

    rates = [column(0, 0, child, half) for half in range(2) for child in range(2)]
    rates += [mine(0, 1, half) for half in range(2)]
    rates += [column(0, 2, child, half) for half in range(2) for child in range(2)]
    for i, rate in enumerate(rates):
        angles = (wave * rate) * position
        trig_ref[i, 0] = jnp.cos(angles)
        trig_ref[i, 1] = jnp.sin(angles)

    def band(starts, weights):
        ids = lax.broadcasted_iota(jnp.int32, (beams, beams), 1).astype(jnp.float32) - starts
        block = jnp.zeros((beams, beams), jnp.float32)
        for tap in range(taps):
            block = jnp.where(ids == tap, weights[tap], block)
        return block

    def pair_bands(level, copies):
        rows = []
        for half in range(2):
            for child in range(2):
                block = band(
                    column(matrices, level, child, half),
                    [weight(tap, level, child, half) for tap in range(taps)],
                )
                empty = jnp.zeros_like(block)
                rows.append(
                    jnp.concatenate(
                        [block if c == child else empty for c in range(2) for _ in range(copies)],
                        axis=1,
                    )
                )
        return jnp.concatenate(rows, axis=0).astype(jnp.bfloat16)

    first_ref[...] = pair_bands(0, 1)
    third_ref[...] = pair_bands(2, 2)
    rows = []
    for half in range(2):
        block = band(
            mine(matrices, 1, half),
            [
                jnp.where(upper, weight(tap, 1, 1, half), weight(tap, 1, 0, half))
                for tap in range(taps)
            ],
        )
        rows.append(jnp.concatenate([block, block], axis=1))
    second_ref[...] = jnp.concatenate(rows, axis=0).astype(jnp.bfloat16)

    samples = range_ref[...]
    fracs = [frac_ref[i].astype(jnp.float32) for i in range(3)]
    angles = (wave * range_phase) * (samples.astype(jnp.float32) + fracs[1])
    pixel_ref[0] = jnp.cos(angles)
    pixel_ref[1] = jnp.sin(angles)
    for part in range(2):
        height_ref[pl.ds(part, ROWS, stride=2), :] = fracs[2]
    first_beam = place_ref[2] * 8 - HALO
    for group in range(ROWS // 32):
        rows = [slice(group * 32 + 8 * j, group * 32 + 8 * j + 8) for j in range(4)]
        sample_parts = swap_quarters([samples[r] for r in rows])
        beam_parts = swap_quarters([beam_ref[r, :] - first_beam for r in rows])
        frac_parts = [swap_quarters([fracs[i][r] for r in rows]) for i in range(2)]
        for quarter in range(4):
            place = slice(quarter * 16 + group * 8, quarter * 16 + group * 8 + 8)
            whole_ref[0, place, :] = sample_parts[quarter] & (width - 1)
            whole_ref[1, place, :] = sample_parts[quarter] >> (width.bit_length() - 1)
            whole_ref[2, place, :] = beam_parts[quarter] - (2 * quarter + 2)
            for i in range(2):
                real_ref[i, place, :] = frac_parts[i][quarter]


def halves_of(value):
    high = value.astype(jnp.bfloat16)
    return high, (value - high.astype(jnp.float32)).astype(jnp.bfloat16)


def merge_kernel(
    data_ref, trig_ref, first_ref, second_ref, third_ref, out_ref, padded_ref, *, groups
):
    beams, width = data_ref.shape[2], data_ref.shape[3]

    def turn(i, product, row, col):
        real = product[row : row + beams, col : col + width]
        imag = product[row : row + beams, col + width : col + 2 * width]
        cosine, sine = trig_ref[i, 0], trig_ref[i, 1]
        return cosine * real - sine * imag, sine * real + cosine * imag

    def add(a, b):
        return a[0] + b[0], a[1] + b[1]

    sums = {}
    for low in range(2):
        for group in range(groups):
            source = (group * 2 + low) * 2
            stacked = jnp.concatenate(
                [
                    jnp.concatenate([data_ref[source + core, part] for part in range(2)], axis=1)
                    for core in range(2)
                ],
                axis=0,
            )
            product = jnp.dot(first_ref[...], stacked, preferred_element_type=jnp.float32)
            for half in range(2):
                terms = [
                    turn(half * 2 + child, product, (half * 2 + child) * beams, 0)
                    for child in range(2)
                ]
                level = tuple(
                    v.astype(jnp.bfloat16).astype(jnp.float32) for v in add(terms[0], terms[1])
                )
                sums[low, half] = level if group == 0 else add(sums[low, half], level)
    middle = {}
    for low in range(2):
        for half in range(2):
            parts = [halves_of(v) for v in sums[low, half]]
            stacked = jnp.concatenate(
                [jnp.concatenate([parts[0][i], parts[1][i]], axis=1) for i in range(2)], axis=0
            )
            product = jnp.dot(second_ref[...], stacked, preferred_element_type=jnp.float32)
            for next_half in range(2):
                middle[low, half, next_half] = turn(4 + next_half, product, next_half * beams, 0)
    merged = 8 * beams
    padding = padded_ref.shape[1] - HALO - merged
    for part in range(2):
        padded_ref[part, 0:HALO, :] = jnp.zeros((HALO, width), jnp.float32)
        padded_ref[part, HALO + merged :, :] = jnp.zeros((padding, width), jnp.float32)
    for half in range(2):
        for next_half in range(2):
            rows = []
            for low in range(2):
                parts = [halves_of(v) for v in middle[low, half, next_half]]
                rows += [jnp.concatenate([parts[0][i], parts[1][i]], axis=1) for i in range(2)]
            product = jnp.dot(
                third_ref[...], jnp.concatenate(rows, axis=0), preferred_element_type=jnp.float32
            )
            for last in range(2):
                terms = [
                    turn(6 + last * 2 + child, product, (last * 2 + child) * beams, 0)
                    for child in range(2)
                ]
                start = HALO + (half * 4 + next_half * 2 + last) * beams
                for part, value in enumerate(add(terms[0], terms[1])):
                    padded_ref[part, start : start + beams, :] = value
    for block in range(out_ref.shape[0]):
        for part in range(2):
            rows = padded_ref[part, 8 * block : 8 * block + WINDOW, :]
            out_ref[block, part] = rows.astype(jnp.bfloat16)


def sample_kernel(
    table_ref, whole_ref, real_ref, pixel_ref, out_ref, pair_ref, lhs_ref, cart_ref
):
    blocks, parts, _, width = table_ref.shape
    rows = 2 * parts * QUARTER
    lane = lax.broadcasted_iota(jnp.int32, (WINDOW, width), 1)
    for part in range(parts):
        values = [table_ref[i, part].astype(jnp.float32) for i in range(blocks)]
        rolled = [pltpu.roll(v, width - 1, 1) for v in values]
        for i in range(blocks):
            pair_ref[0, i, part] = values[i]
            pair_ref[1, i, part] = jnp.where(
                lane < width - 1, rolled[i], rolled[(i + 1) % blocks]
            )
    for quarter in range(4):
        low = 2 * quarter + 2
        for i in range(blocks):
            for tap in range(2):
                pair = [pair_ref[tap, i, part, low : low + QUARTER, :] for part in range(parts)]
                row = i * rows + tap * parts * QUARTER
                lhs_ref[quarter, row : row + parts * QUARTER, :] = jnp.concatenate(
                    pair, axis=0
                ).astype(jnp.bfloat16)
    pixels = 4 * LANES
    row_ids = lax.broadcasted_iota(jnp.int32, (width, pixels), 0)
    beam_ids = lax.broadcasted_iota(jnp.int32, (QUARTER, pixels), 0)

    def flat(value):
        return jnp.concatenate([value[i : i + 1, :] for i in range(4)], axis=1)

    def chunk(quarter, step):
        place = pl.ds(step * 4, 4)
        inner, outer, beam = (flat(whole_ref[i, place, :]) for i in range(3))
        frac0, frac1 = (flat(real_ref[i, place, :]) for i in range(2))
        hot = jnp.where(row_ids == inner, 1.0, 0.0).astype(jnp.bfloat16)
        product = jnp.dot(lhs_ref[quarter], hot, preferred_element_type=jnp.float32)
        picked = product[0:rows]
        for k in range(1, blocks):
            picked = jnp.where(outer == k, product[k * rows : (k + 1) * rows], picked)
        weights = jnp.where(
            beam_ids == beam, 1.0 - frac0, jnp.where(beam_ids == beam + 1, frac0, 0.0)
        )
        low_weights = weights * (1.0 - frac1)
        high_weights = weights * frac1
        for part in range(parts):
            low = picked[part * QUARTER : (part + 1) * QUARTER]
            high = picked[(parts + part) * QUARTER : (parts + part + 1) * QUARTER]
            summed = jnp.sum(low_weights * low + high_weights * high, axis=0, keepdims=True)
            for i in range(4):
                cart_ref[part, pl.ds(step * 4 + i, 1), :] = summed[:, i * LANES : (i + 1) * LANES]

    def window(quarter, carry):
        for i in range(4):
            chunk(quarter, quarter * 4 + i)
        return carry

    lax.fori_loop(0, 4, window, 0)
    for group in range(ROWS // 32):
        ordered = [
            swap_quarters(
                [
                    cart_ref[part, quarter * 16 + group * 8 : quarter * 16 + group * 8 + 8, :]
                    for quarter in range(4)
                ]
            )
            for part in range(parts)
        ]
        for j in range(4):
            start = group * 32 + 8 * j
            cosine = pixel_ref[0, start : start + 8, :]
            sine = pixel_ref[1, start : start + 8, :]
            real, imag = ordered[0][j], ordered[1][j]
            out_ref[pl.ds(2 * start, 8, stride=2), :] = cosine * real - sine * imag
            out_ref[pl.ds(2 * start + 1, 8, stride=2), :] = sine * real + cosine * imag


def body(
    polar_beams,
    band_start,
    band_weight,
    phase_rate,
    layer_wave,
    beam_map,
    range_map,
    pixel_frac,
    *,
    interpret=False,
):
    sub_index = lax.axis_index("sub")
    sub_count = lax.axis_size("sub")
    layers = lax.axis_size("hgt")
    beams = polar_beams.shape[2]
    range_count = polar_beams.shape[3]
    levels = band_start.shape[0]
    taps = band_weight.shape[-1]
    row_count, column_count = beam_map.shape
    matrices = levels * 4
    members = sub_count // 2
    width = range_count // members
    column_block = (sub_index >> 2) * 2 + (sub_index & 1)
    row_half = sub_index >> 1 & 1
    halves = [[s for s in range(sub_count) if s >> 1 & 1 == half] for half in range(2)]
    place = jnp.stack([column_block, row_half, column_block]).astype(jnp.int32)
    params = jnp.concatenate(
        [
            phase_rate.reshape(matrices, beams),
            band_start.reshape(matrices, beams).astype(jnp.float32),
            band_weight.reshape(matrices, beams, taps)
            .transpose(0, 2, 1)
            .reshape(matrices * taps, beams)
            .astype(jnp.float32),
        ],
        axis=0,
    ).T
    smem = pl.BlockSpec(memory_space=pltpu.SMEM)
    vmem = pl.BlockSpec(memory_space=pltpu.VMEM)
    shape = jax.ShapeDtypeStruct
    f32, bf16 = jnp.float32, jnp.bfloat16

    kept = shape if interpret else pltpu.VMEM

    def local(value):
        return value if interpret else pltpu.with_memory_space_constraint(value, pltpu.VMEM)

    slices = pl.pallas_call(
        split_kernel,
        out_shape=shape((members, 2, beams, width), bf16),
        in_specs=[vmem],
        out_specs=vmem,
        interpret=interpret,
        name="split",
    )(polar_beams)
    slices = local(lax.all_to_all(slices, "sub", 0, 0, axis_index_groups=halves, tiled=True))
    trig, first, second, third, whole, real, pixel, height = pl.pallas_call(
        functools.partial(prepare_kernel, range_count=range_count),
        out_shape=[
            kept((10, 2, beams, width), f32),
            kept((4 * beams, 2 * beams), bf16),
            kept((2 * beams, 2 * beams), bf16),
            kept((4 * beams, 4 * beams), bf16),
            kept((3, row_count, LANES), jnp.int32),
            kept((2, row_count, LANES), f32),
            kept((2, row_count, LANES), f32),
            shape((2 * row_count, LANES), f32),
        ],
        grid_spec=pltpu.PrefetchScalarGridSpec(
            num_scalar_prefetch=1,
            grid=(1,),
            in_specs=[
                smem,
                pl.BlockSpec((beams, params.shape[1]), lambda i, p: (0, 0)),
                pl.BlockSpec((row_count, LANES), lambda i, p: (0, p[0])),
                pl.BlockSpec((row_count, LANES), lambda i, p: (0, p[0])),
                pl.BlockSpec((3, row_count, LANES), lambda i, p: (0, 0, p[0])),
            ],
            out_specs=[
                pl.BlockSpec((10, 2, beams, width), lambda i, p: (0, 0, 0, 0)),
                pl.BlockSpec((4 * beams, 2 * beams), lambda i, p: (0, 0)),
                pl.BlockSpec((2 * beams, 2 * beams), lambda i, p: (0, 0)),
                pl.BlockSpec((4 * beams, 4 * beams), lambda i, p: (0, 0)),
                pl.BlockSpec((3, row_count, LANES), lambda i, p: (0, 0, 0)),
                pl.BlockSpec((2, row_count, LANES), lambda i, p: (0, 0, 0)),
                pl.BlockSpec((2, row_count, LANES), lambda i, p: (0, 0, 0)),
                pl.BlockSpec((2 * row_count, LANES), lambda i, p: (0, 0)),
            ],
        ),
        interpret=interpret,
        name="prepare",
    )(place, layer_wave, params, beam_map, range_map, pixel_frac)
    windows = pl.pallas_call(
        functools.partial(merge_kernel, groups=sub_count // 2**levels),
        out_shape=shape((members, 2, WINDOW, width), bf16),
        in_specs=[vmem] * 5,
        out_specs=vmem,
        scratch_shapes=[pltpu.VMEM((2, 144, width), f32)],
        interpret=interpret,
        name="merge",
    )(slices, local(trig), local(first), local(second), local(third))
    table = local(lax.all_to_all(windows, "sub", 0, 0, axis_index_groups=halves, tiled=True))
    cart = pl.pallas_call(
        sample_kernel,
        out_shape=shape((2 * row_count, LANES), f32),
        in_specs=[vmem] * 4,
        out_specs=vmem,
        scratch_shapes=[
            pltpu.VMEM((2, members, 2, WINDOW, width), f32),
            pltpu.VMEM((4, members * 4 * QUARTER, width), bf16),
            pltpu.VMEM((2, row_count, LANES), f32),
        ],
        interpret=interpret,
        name="sample",
    )(table, local(whole), local(real), local(pixel))
    above = lax.ppermute(cart, "hgt", [(i, i - 1) for i in range(1, layers)])
    blended = (1.0 - height) * cart + height * above
    tile_rows = row_count // sub_count
    blended = blended.astype(bf16).reshape(sub_count, tile_rows * 2, LANES)
    tiles = lax.all_to_all(blended, "sub", 0, 0, tiled=True).astype(f32)
    tiles = tiles.reshape(sub_count // 4, 2, 2, tile_rows * 2, LANES)
    tiles = (tiles[:, 0] + tiles[:, 1]).reshape(members, tile_rows * 2, LANES)
    return tiles.transpose(1, 0, 2).reshape(tile_rows, 1, 2, column_count)


def solution(mesh):
    in_specs = (P("hgt", None, "sub", None), P(), P(), P(), P("hgt"), P(), P(), P())
    out_specs = P("sub", "hgt", None, None)
    return jax.shard_map(body, mesh=mesh, in_specs=in_specs, out_specs=out_specs, check_vma=False)
```

```python
import functools

import jax
import jax.numpy as jnp
from jax import lax
from jax.experimental import pallas as pl
from jax.experimental.pallas import tpu as pltpu
from jax.sharding import PartitionSpec as P

range_phase = 0.003
LANES = 128
WINDOW = 16
HALO = 4
QUARTER = 8
ROWS = 64


def split_kernel(source_ref, out_ref, semaphores):
    width = out_ref.shape[3]
    copies = [
        pltpu.make_async_copy(
            source_ref.at[0, :, :, pl.ds(i * width, width)], out_ref.at[i], semaphores.at[i]
        )
        for i in range(out_ref.shape[0])
    ]
    for copy in copies:
        copy.start()
    for copy in copies:
        copy.wait()


def swap_quarters(values):
    lane = lax.broadcasted_iota(jnp.int32, values[0].shape, 1)
    values = list(values)
    for bit, width in ((1, 64), (0, 32)):
        keep = lane & width == 0
        for i in range(4):
            if i >> bit & 1:
                continue
            j = i | 1 << bit
            a, b = values[i], values[j]
            values[i] = jnp.where(keep, a, pltpu.roll(b, width, 1))
            values[j] = jnp.where(keep, pltpu.roll(a, LANES - width, 1), b)
    return values


def prepare_kernel(
    place_ref,
    wave_ref,
    params_ref,
    beam_ref,
    range_ref,
    frac_ref,
    trig_ref,
    first_ref,
    second_ref,
    third_ref,
    whole_ref,
    real_ref,
    pixel_ref,
    *,
    range_count,
):
    wave = wave_ref[0]
    params = params_ref[...]
    beams = params.shape[0]
    matrices = 12
    taps = (params.shape[1] - 2 * matrices) // matrices
    width = trig_ref.shape[3]
    lane = lax.broadcasted_iota(jnp.int32, (1, width), 1)
    position = ((place_ref[0] * width + lane).astype(jnp.float32) + 0.5) / range_count
    row_half = place_ref[1]
    upper = row_half == 1

    def column(offset, level, child, half):
        i = offset + (level * 2 + child) * 2 + half
        return params[:, i : i + 1]

    def mine(offset, level, half):
        return jnp.where(upper, column(offset, level, 1, half), column(offset, level, 0, half))

    def weight(tap, level, child, half):
        i = 2 * matrices + ((level * 2 + child) * 2 + half) * taps + tap
        return params[:, i : i + 1]

    rates = [column(0, 0, child, half) for half in range(2) for child in range(2)]
    rates += [mine(0, 1, half) for half in range(2)]
    rates += [column(0, 2, child, half) for half in range(2) for child in range(2)]
    for i, rate in enumerate(rates):
        angles = (wave * rate) * position
        trig_ref[i, 0] = jnp.cos(angles)
        trig_ref[i, 1] = jnp.sin(angles)

    def band(starts, weights):
        ids = lax.broadcasted_iota(jnp.int32, (beams, beams), 1).astype(jnp.float32) - starts
        block = jnp.zeros((beams, beams), jnp.float32)
        for tap in range(taps):
            block = jnp.where(ids == tap, weights[tap], block)
        return block

    def pair_bands(level, copies):
        rows = []
        for half in range(2):
            for child in range(2):
                block = band(
                    column(matrices, level, child, half),
                    [weight(tap, level, child, half) for tap in range(taps)],
                )
                empty = jnp.zeros_like(block)
                rows.append(
                    jnp.concatenate(
                        [block if c == child else empty for c in range(2) for _ in range(copies)],
                        axis=1,
                    )
                )
        return jnp.concatenate(rows, axis=0).astype(jnp.bfloat16)

    first_ref[...] = pair_bands(0, 1)
    third_ref[...] = pair_bands(2, 2)
    rows = []
    for half in range(2):
        block = band(
            mine(matrices, 1, half),
            [
                jnp.where(upper, weight(tap, 1, 1, half), weight(tap, 1, 0, half))
                for tap in range(taps)
            ],
        )
        rows.append(jnp.concatenate([block, block], axis=1))
    second_ref[...] = jnp.concatenate(rows, axis=0).astype(jnp.bfloat16)

    samples = range_ref[...]
    fracs = [frac_ref[i].astype(jnp.float32) for i in range(2)]
    angles = (wave * range_phase) * (samples.astype(jnp.float32) + fracs[1])
    pixel_ref[0] = jnp.cos(angles)
    pixel_ref[1] = jnp.sin(angles)
    first_beam = place_ref[2] * 8 - HALO
    for group in range(ROWS // 32):
        rows = [slice(group * 32 + 8 * j, group * 32 + 8 * j + 8) for j in range(4)]
        sample_parts = swap_quarters([samples[r] for r in rows])
        beam_parts = swap_quarters([beam_ref[r, :] - first_beam for r in rows])
        frac_parts = [swap_quarters([fracs[i][r] for r in rows]) for i in range(2)]
        for quarter in range(4):
            place = slice(quarter * 16 + group * 8, quarter * 16 + group * 8 + 8)
            sample = sample_parts[quarter]
            block = (sample + 1 + (sample >> 8)) >> 8
            whole_ref[0, place, :] = sample - block * (width - 1)
            whole_ref[1, place, :] = block
            whole_ref[2, place, :] = beam_parts[quarter] - (2 * quarter + 2)
            for i in range(2):
                real_ref[i, place, :] = frac_parts[i][quarter]


def halves_of(value):
    high = value.astype(jnp.bfloat16)
    return high, (value - high.astype(jnp.float32)).astype(jnp.bfloat16)


def merge_kernel(
    data_ref, trig_ref, first_ref, second_ref, third_ref, out_ref, padded_ref, *, groups
):
    beams, width = data_ref.shape[2], data_ref.shape[3]

    def turn(i, product, row, col):
        real = product[row : row + beams, col : col + width]
        imag = product[row : row + beams, col + width : col + 2 * width]
        cosine, sine = trig_ref[i, 0], trig_ref[i, 1]
        return cosine * real - sine * imag, sine * real + cosine * imag

    def add(a, b):
        return a[0] + b[0], a[1] + b[1]

    sums = {}
    for low in range(2):
        for group in range(groups):
            source = (group * 2 + low) * 2
            stacked = jnp.concatenate(
                [
                    jnp.concatenate([data_ref[source + core, part] for part in range(2)], axis=1)
                    for core in range(2)
                ],
                axis=0,
            )
            product = jnp.dot(first_ref[...], stacked, preferred_element_type=jnp.float32)
            for half in range(2):
                terms = [
                    turn(half * 2 + child, product, (half * 2 + child) * beams, 0)
                    for child in range(2)
                ]
                level = tuple(
                    v.astype(jnp.bfloat16).astype(jnp.float32) for v in add(terms[0], terms[1])
                )
                sums[low, half] = level if group == 0 else add(sums[low, half], level)
    middle = {}
    for low in range(2):
        for half in range(2):
            parts = [halves_of(v) for v in sums[low, half]]
            stacked = jnp.concatenate(
                [jnp.concatenate([parts[0][i], parts[1][i]], axis=1) for i in range(2)], axis=0
            )
            product = jnp.dot(second_ref[...], stacked, preferred_element_type=jnp.float32)
            for next_half in range(2):
                middle[low, half, next_half] = turn(4 + next_half, product, next_half * beams, 0)
    merged = 8 * beams
    padding = padded_ref.shape[1] - HALO - merged
    for part in range(2):
        padded_ref[part, 0:HALO, :] = jnp.zeros((HALO, width), jnp.float32)
        padded_ref[part, HALO + merged :, :] = jnp.zeros((padding, width), jnp.float32)
    for half in range(2):
        for next_half in range(2):
            rows = []
            for low in range(2):
                parts = [halves_of(v) for v in middle[low, half, next_half]]
                rows += [jnp.concatenate([parts[0][i], parts[1][i]], axis=1) for i in range(2)]
            product = jnp.dot(
                third_ref[...], jnp.concatenate(rows, axis=0), preferred_element_type=jnp.float32
            )
            for last in range(2):
                terms = [
                    turn(6 + last * 2 + child, product, (last * 2 + child) * beams, 0)
                    for child in range(2)
                ]
                start = HALO + (half * 4 + next_half * 2 + last) * beams
                for part, value in enumerate(add(terms[0], terms[1])):
                    padded_ref[part, start : start + beams, :] = value
    for block in range(out_ref.shape[0]):
        for part in range(2):
            rows = padded_ref[part, 8 * block : 8 * block + WINDOW, :]
            out_ref[block, part] = rows.astype(jnp.bfloat16)


def flat(value):
    return jnp.concatenate([value[i : i + 1, :] for i in range(4)], axis=1)


def range_columns(whole_ref, real_ref, step, width):
    place = pl.ds(step * 4, 4)
    row_ids = lax.broadcasted_iota(jnp.int32, (width, 4 * LANES), 0)
    offset = row_ids - flat(whole_ref[0, place, :])
    frac = flat(real_ref[1, place, :])
    column = jnp.where(offset == 0, 1.0 - frac, jnp.where(offset == 1, frac, 0.0))
    return column.astype(jnp.bfloat16)


def weights_kernel(after_ref, whole_ref, real_ref, out_ref):
    del after_ref

    def chunk(step, carry):
        out_ref[step] = range_columns(whole_ref, real_ref, 2 * step, out_ref.shape[1])
        return carry

    lax.fori_loop(0, out_ref.shape[0], chunk, 0)


def sample_kernel(
    table_ref,
    column_ref,
    whole_ref,
    real_ref,
    pixel_ref,
    out_ref,
    block_ref,
    lhs_ref,
    cart_ref,
    order_ref,
):
    slices, parts, _, width = table_ref.shape
    blocks = slices + 1
    rows = parts * QUARTER
    lane = lax.broadcasted_iota(jnp.int32, (WINDOW, width), 1)
    for part in range(parts):
        values = [table_ref[i, part].astype(jnp.float32) for i in range(slices)]
        block_ref[0, part] = values[0]
        for k in range(1, blocks):
            before = pltpu.roll(values[k - 1], k, 1)
            after = pltpu.roll(values[k], k, 1) if k < slices else before
            block_ref[k, part] = jnp.where(lane < k, before, after)
    for quarter in range(4):
        low = 2 * quarter + 2
        for k in range(blocks):
            pair = [block_ref[k, part, low : low + QUARTER, :] for part in range(parts)]
            lhs_ref[quarter, k * rows : (k + 1) * rows, :] = jnp.concatenate(pair, axis=0).astype(
                jnp.bfloat16
            )
    beam_ids = lax.broadcasted_iota(jnp.int32, (QUARTER, column_ref.shape[2]), 0)

    def chunk(quarter, step, columns):
        place = pl.ds(step * 4, 4)
        outer, beam = flat(whole_ref[1, place, :]), flat(whole_ref[2, place, :])
        frac = flat(real_ref[0, place, :])
        product = jnp.dot(lhs_ref[quarter], columns, preferred_element_type=jnp.float32)
        picked = product[0:rows]
        for k in range(1, blocks):
            picked = jnp.where(outer == k, product[k * rows : (k + 1) * rows], picked)
        weights = jnp.where(
            beam_ids == beam, 1.0 - frac, jnp.where(beam_ids == beam + 1, frac, 0.0)
        )
        for part in range(parts):
            summed = jnp.sum(
                weights * picked[part * QUARTER : (part + 1) * QUARTER], axis=0, keepdims=True
            )
            for i in range(4):
                cart_ref[part, pl.ds(step * 4 + i, 1), :] = summed[:, i * LANES : (i + 1) * LANES]

    def window(quarter, carry):
        for i in range(2):
            step = quarter * 4 + 2 * i
            chunk(quarter, step, column_ref[quarter * 2 + i])
            chunk(quarter, step + 1, range_columns(whole_ref, real_ref, step + 1, width))
        return carry

    lax.fori_loop(0, 4, window, 0)
    for group in range(ROWS // 32):
        ordered = [
            swap_quarters(
                [
                    cart_ref[part, quarter * 16 + group * 8 : quarter * 16 + group * 8 + 8, :]
                    for quarter in range(4)
                ]
            )
            for part in range(parts)
        ]
        for j in range(4):
            start = group * 32 + 8 * j
            cosine = pixel_ref[0, start : start + 8, :]
            sine = pixel_ref[1, start : start + 8, :]
            real, imag = ordered[0][j], ordered[1][j]
            order_ref[pl.ds(2 * start, 8, stride=2), :] = cosine * real - sine * imag
            order_ref[pl.ds(2 * start + 1, 8, stride=2), :] = sine * real + cosine * imag
    out_ref[...] = order_ref[...].astype(jnp.bfloat16)


def body(
    polar_beams,
    band_start,
    band_weight,
    phase_rate,
    layer_wave,
    beam_map,
    range_map,
    pixel_frac,
    *,
    interpret=False,
):
    sub_index = lax.axis_index("sub")
    sub_count = lax.axis_size("sub")
    layers = lax.axis_size("hgt")
    beams = polar_beams.shape[2]
    range_count = polar_beams.shape[3]
    levels = band_start.shape[0]
    taps = band_weight.shape[-1]
    row_count, column_count = beam_map.shape
    matrices = levels * 4
    members = sub_count // 2
    width = range_count // members
    column_block = (sub_index >> 2) * 2 + (sub_index & 1)
    row_half = sub_index >> 1 & 1
    halves = [[s for s in range(sub_count) if s >> 1 & 1 == half] for half in range(2)]
    place = jnp.stack([column_block, row_half, column_block]).astype(jnp.int32)
    params = jnp.concatenate(
        [
            phase_rate.reshape(matrices, beams),
            band_start.reshape(matrices, beams).astype(jnp.float32),
            band_weight.reshape(matrices, beams, taps)
            .transpose(0, 2, 1)
            .reshape(matrices * taps, beams)
            .astype(jnp.float32),
        ],
        axis=0,
    ).T
    smem = pl.BlockSpec(memory_space=pltpu.SMEM)
    vmem = pl.BlockSpec(memory_space=pltpu.VMEM)
    far = pl.BlockSpec(memory_space=pl.ANY if interpret else pltpu.HBM)
    shape = jax.ShapeDtypeStruct
    limit = pltpu.CompilerParams(vmem_limit_bytes=24 * 2**20)
    f32, bf16 = jnp.float32, jnp.bfloat16

    kept = shape if interpret else pltpu.VMEM

    def local(value):
        return value if interpret else pltpu.with_memory_space_constraint(value, pltpu.VMEM)

    slices = pl.pallas_call(
        split_kernel,
        out_shape=shape((members, 2, beams, width), bf16),
        in_specs=[far],
        out_specs=far,
        scratch_shapes=[pltpu.SemaphoreType.DMA((members,))],
        interpret=interpret,
        name="split",
    )(polar_beams)
    slices = local(lax.all_to_all(slices, "sub", 0, 0, axis_index_groups=halves, tiled=True))
    trig, first, second, third, whole, real, pixel = pl.pallas_call(
        functools.partial(prepare_kernel, range_count=range_count),
        out_shape=[
            kept((10, 2, beams, width), f32),
            kept((4 * beams, 2 * beams), bf16),
            kept((2 * beams, 2 * beams), bf16),
            kept((4 * beams, 4 * beams), bf16),
            kept((3, row_count, LANES), jnp.int32),
            kept((2, row_count, LANES), f32),
            kept((2, row_count, LANES), f32),
        ],
        grid_spec=pltpu.PrefetchScalarGridSpec(
            num_scalar_prefetch=1,
            grid=(1,),
            in_specs=[
                smem,
                pl.BlockSpec((beams, params.shape[1]), lambda i, p: (0, 0)),
                pl.BlockSpec((row_count, LANES), lambda i, p: (0, p[0])),
                pl.BlockSpec((row_count, LANES), lambda i, p: (0, p[0])),
                pl.BlockSpec((2, row_count, LANES), lambda i, p: (0, 0, p[0])),
            ],
            out_specs=[
                pl.BlockSpec((10, 2, beams, width), lambda i, p: (0, 0, 0, 0)),
                pl.BlockSpec((4 * beams, 2 * beams), lambda i, p: (0, 0)),
                pl.BlockSpec((2 * beams, 2 * beams), lambda i, p: (0, 0)),
                pl.BlockSpec((4 * beams, 4 * beams), lambda i, p: (0, 0)),
                pl.BlockSpec((3, row_count, LANES), lambda i, p: (0, 0, 0)),
                pl.BlockSpec((2, row_count, LANES), lambda i, p: (0, 0, 0)),
                pl.BlockSpec((2, row_count, LANES), lambda i, p: (0, 0, 0)),
            ],
        ),
        interpret=interpret,
        name="prepare",
    )(place, layer_wave, params, beam_map, range_map, pixel_frac)
    windows = pl.pallas_call(
        functools.partial(merge_kernel, groups=sub_count // 2**levels),
        out_shape=kept((members, 2, WINDOW, width), bf16),
        in_specs=[vmem] * 5,
        out_specs=vmem,
        scratch_shapes=[pltpu.VMEM((2, 144, width), f32)],
        compiler_params=limit,
        interpret=interpret,
        name="merge",
    )(slices, local(trig), local(first), local(second), local(third))
    table = local(lax.all_to_all(windows, "sub", 0, 0, axis_index_groups=halves, tiled=True))
    columns = pl.pallas_call(
        weights_kernel,
        out_shape=kept((row_count // 8, width, 4 * LANES), bf16),
        in_specs=[pl.BlockSpec(memory_space=pl.ANY), vmem, vmem],
        out_specs=vmem,
        compiler_params=limit,
        interpret=interpret,
        name="weights",
    )(windows, local(whole), local(real))
    cart = pl.pallas_call(
        sample_kernel,
        out_shape=shape((2 * row_count, LANES), bf16),
        in_specs=[vmem] * 5,
        out_specs=vmem,
        scratch_shapes=[
            pltpu.VMEM((members + 1, 2, WINDOW, width), f32),
            pltpu.VMEM((4, (members + 1) * 2 * QUARTER, width), bf16),
            pltpu.VMEM((2, row_count, LANES), f32),
            pltpu.VMEM((2 * row_count, LANES), f32),
        ],
        compiler_params=limit,
        interpret=interpret,
        name="sample",
    )(table, local(columns), local(whole), local(real), local(pixel))
    tile_rows = row_count // sub_count
    tiles = cart.reshape(sub_count, tile_rows * 2, LANES)
    tiles = lax.all_to_all(tiles, "sub", 0, 0, tiled=True).astype(f32)
    tiles = tiles.reshape(sub_count // 4, 2, 2, tile_rows * 2, LANES)
    tile = (tiles[:, 0] + tiles[:, 1]).reshape(members, tile_rows, 2, LANES)
    above = lax.ppermute(tile, "hgt", [(i, i - 1) for i in range(1, layers)])
    height = lax.dynamic_slice_in_dim(pixel_frac[2], sub_index * tile_rows, tile_rows, 0)
    height = height.astype(f32).reshape(tile_rows, members, LANES).transpose(1, 0, 2)
    height = height[:, :, None, :]
    blended = (1.0 - height) * tile + height * above
    return blended.transpose(1, 2, 0, 3).reshape(tile_rows, 1, 2, column_count)


def solution(mesh):
    in_specs = (P("hgt", None, "sub", None), P(), P(), P(), P("hgt"), P(), P(), P())
    out_specs = P("sub", "hgt", None, None)
    return jax.shard_map(body, mesh=mesh, in_specs=in_specs, out_specs=out_specs, check_vma=False)
```

```python
import functools

import jax
import jax.numpy as jnp
from jax import lax
from jax.experimental import pallas as pl
from jax.experimental.pallas import tpu as pltpu
from jax.sharding import PartitionSpec as P

range_phase = 0.003
LANES = 128
WINDOW = 16
HALO = 4
QUARTER = 8
ROWS = 64


def swap_quarters(values):
    lane = lax.broadcasted_iota(jnp.int32, values[0].shape, 1)
    values = list(values)
    for bit, width in ((1, 64), (0, 32)):
        keep = lane & width == 0
        for i in range(4):
            if i >> bit & 1:
                continue
            j = i | 1 << bit
            a, b = values[i], values[j]
            values[i] = jnp.where(keep, a, pltpu.roll(b, width, 1))
            values[j] = jnp.where(keep, pltpu.roll(a, LANES - width, 1), b)
    return values


def prepare_kernel(
    place_ref,
    wave_ref,
    params_ref,
    beam_ref,
    range_ref,
    frac_ref,
    trig_ref,
    first_ref,
    second_ref,
    third_ref,
    whole_ref,
    real_ref,
    pixel_ref,
    *,
    range_count,
):
    wave = wave_ref[0]
    params = params_ref[...]
    beams = params.shape[0]
    matrices = 12
    taps = (params.shape[1] - 2 * matrices) // matrices
    width = trig_ref.shape[3]
    lane = lax.broadcasted_iota(jnp.int32, (1, width), 1)
    position = ((place_ref[0] * width + lane).astype(jnp.float32) + 0.5) / range_count
    row_half = place_ref[1]
    upper = row_half == 1

    def column(offset, level, child, half):
        i = offset + (level * 2 + child) * 2 + half
        return params[:, i : i + 1]

    def mine(offset, level, half):
        return jnp.where(upper, column(offset, level, 1, half), column(offset, level, 0, half))

    def weight(tap, level, child, half):
        i = 2 * matrices + ((level * 2 + child) * 2 + half) * taps + tap
        return params[:, i : i + 1]

    rates = [column(0, 0, child, half) for half in range(2) for child in range(2)]
    rates += [mine(0, 1, half) for half in range(2)]
    rates += [column(0, 2, child, half) for half in range(2) for child in range(2)]
    for i, rate in enumerate(rates):
        angles = (wave * rate) * position
        trig_ref[i, 0] = jnp.cos(angles)
        trig_ref[i, 1] = jnp.sin(angles)

    def band(starts, weights):
        ids = lax.broadcasted_iota(jnp.int32, (beams, beams), 1).astype(jnp.float32) - starts
        block = jnp.zeros((beams, beams), jnp.float32)
        for tap in range(taps):
            block = jnp.where(ids == tap, weights[tap], block)
        return block

    def pair_bands(level, copies):
        rows = []
        for half in range(2):
            for child in range(2):
                block = band(
                    column(matrices, level, child, half),
                    [weight(tap, level, child, half) for tap in range(taps)],
                )
                empty = jnp.zeros_like(block)
                rows.append(
                    jnp.concatenate(
                        [block if c == child else empty for c in range(2) for _ in range(copies)],
                        axis=1,
                    )
                )
        return jnp.concatenate(rows, axis=0).astype(jnp.bfloat16)

    first_ref[...] = pair_bands(0, 1)
    third_ref[...] = pair_bands(2, 2)
    rows = []
    for half in range(2):
        block = band(
            mine(matrices, 1, half),
            [
                jnp.where(upper, weight(tap, 1, 1, half), weight(tap, 1, 0, half))
                for tap in range(taps)
            ],
        )
        rows.append(jnp.concatenate([block, block], axis=1))
    second_ref[...] = jnp.concatenate(rows, axis=0).astype(jnp.bfloat16)

    samples = range_ref[...]
    fracs = [frac_ref[i].astype(jnp.float32) for i in range(2)]
    angles = (wave * range_phase) * (samples.astype(jnp.float32) + fracs[1])
    pixel_ref[0] = jnp.cos(angles)
    pixel_ref[1] = jnp.sin(angles)
    first_beam = place_ref[2] * 8 - HALO
    for group in range(ROWS // 32):
        rows = [slice(group * 32 + 8 * j, group * 32 + 8 * j + 8) for j in range(4)]
        sample_parts = swap_quarters([samples[r] for r in rows])
        beam_parts = swap_quarters([beam_ref[r, :] - first_beam for r in rows])
        frac_parts = [swap_quarters([fracs[i][r] for r in rows]) for i in range(2)]
        for quarter in range(4):
            place = slice(quarter * 16 + group * 8, quarter * 16 + group * 8 + 8)
            sample = sample_parts[quarter]
            block = (sample + 1 + (sample >> 8)) >> 8
            whole_ref[0, place, :] = sample - block * (width - 1)
            whole_ref[1, place, :] = block
            whole_ref[2, place, :] = beam_parts[quarter] - (2 * quarter + 2)
            for i in range(2):
                real_ref[i, place, :] = frac_parts[i][quarter]


def halves_of(value):
    high = value.astype(jnp.bfloat16)
    return high, (value - high.astype(jnp.float32)).astype(jnp.bfloat16)


def merge_kernel(
    data_ref, trig_ref, first_ref, second_ref, third_ref, out_ref, padded_ref, *, groups
):
    beams, width = data_ref.shape[2], data_ref.shape[3]

    def turn(i, product, row, col):
        real = product[row : row + beams, col : col + width]
        imag = product[row : row + beams, col + width : col + 2 * width]
        cosine, sine = trig_ref[i, 0], trig_ref[i, 1]
        return cosine * real - sine * imag, sine * real + cosine * imag

    def add(a, b):
        return a[0] + b[0], a[1] + b[1]

    sums = {}
    for low in range(2):
        for group in range(groups):
            source = (group * 2 + low) * 2
            stacked = jnp.concatenate(
                [
                    jnp.concatenate([data_ref[source + core, part] for part in range(2)], axis=1)
                    for core in range(2)
                ],
                axis=0,
            )
            product = jnp.dot(first_ref[...], stacked, preferred_element_type=jnp.float32)
            for half in range(2):
                terms = [
                    turn(half * 2 + child, product, (half * 2 + child) * beams, 0)
                    for child in range(2)
                ]
                level = tuple(
                    v.astype(jnp.bfloat16).astype(jnp.float32) for v in add(terms[0], terms[1])
                )
                sums[low, half] = level if group == 0 else add(sums[low, half], level)
    middle = {}
    for low in range(2):
        for half in range(2):
            parts = [halves_of(v) for v in sums[low, half]]
            stacked = jnp.concatenate(
                [jnp.concatenate([parts[0][i], parts[1][i]], axis=1) for i in range(2)], axis=0
            )
            product = jnp.dot(second_ref[...], stacked, preferred_element_type=jnp.float32)
            for next_half in range(2):
                middle[low, half, next_half] = turn(4 + next_half, product, next_half * beams, 0)
    merged = 8 * beams
    padding = padded_ref.shape[1] - HALO - merged
    for part in range(2):
        padded_ref[part, 0:HALO, :] = jnp.zeros((HALO, width), jnp.float32)
        padded_ref[part, HALO + merged :, :] = jnp.zeros((padding, width), jnp.float32)
    for half in range(2):
        for next_half in range(2):
            rows = []
            for low in range(2):
                parts = [halves_of(v) for v in middle[low, half, next_half]]
                rows += [jnp.concatenate([parts[0][i], parts[1][i]], axis=1) for i in range(2)]
            product = jnp.dot(
                third_ref[...], jnp.concatenate(rows, axis=0), preferred_element_type=jnp.float32
            )
            for last in range(2):
                terms = [
                    turn(6 + last * 2 + child, product, (last * 2 + child) * beams, 0)
                    for child in range(2)
                ]
                start = HALO + (half * 4 + next_half * 2 + last) * beams
                for part, value in enumerate(add(terms[0], terms[1])):
                    padded_ref[part, start : start + beams, :] = value
    for block in range(out_ref.shape[0]):
        for part in range(2):
            rows = padded_ref[part, 8 * block : 8 * block + WINDOW, :]
            out_ref[block, part] = rows.astype(jnp.bfloat16)


def flat(value):
    return jnp.concatenate([value[i : i + 1, :] for i in range(4)], axis=1)


def range_columns(whole_ref, real_ref, step, width):
    place = pl.ds(step * 4, 4)
    row_ids = lax.broadcasted_iota(jnp.int32, (width, 4 * LANES), 0)
    inner = flat(whole_ref[0, place, :])
    frac = flat(real_ref[1, place, :])
    column = jnp.where(row_ids == inner, 1.0 - frac, jnp.where(row_ids == inner + 1, frac, 0.0))
    return column.astype(jnp.bfloat16)


def weights_kernel(after_ref, whole_ref, real_ref, out_ref):
    del after_ref

    def chunk(step, carry):
        out_ref[step] = range_columns(whole_ref, real_ref, 2 * step, out_ref.shape[1])
        return carry

    lax.fori_loop(0, out_ref.shape[0], chunk, 0)


def sample_kernel(
    table_ref,
    column_ref,
    whole_ref,
    real_ref,
    pixel_ref,
    out_ref,
    block_ref,
    lhs_ref,
    cart_ref,
    order_ref,
):
    slices, parts, _, width = table_ref.shape
    blocks = slices + 1
    rows = parts * QUARTER
    lane = lax.broadcasted_iota(jnp.int32, (WINDOW, width), 1)
    for part in range(parts):
        values = [table_ref[i, part].astype(jnp.float32) for i in range(slices)]
        block_ref[0, part] = values[0]
        for k in range(1, blocks):
            before = pltpu.roll(values[k - 1], k, 1)
            after = pltpu.roll(values[k], k, 1) if k < slices else before
            block_ref[k, part] = jnp.where(lane < k, before, after)
    for quarter in range(4):
        low = 2 * quarter + 2
        for k in range(blocks):
            pair = [block_ref[k, part, low : low + QUARTER, :] for part in range(parts)]
            lhs_ref[quarter, k * rows : (k + 1) * rows, :] = jnp.concatenate(pair, axis=0).astype(
                jnp.bfloat16
            )
    beam_ids = lax.broadcasted_iota(jnp.int32, (QUARTER, column_ref.shape[2]), 0)

    def chunk(quarter, step, columns):
        place = pl.ds(step * 4, 4)
        outer, beam = flat(whole_ref[1, place, :]), flat(whole_ref[2, place, :])
        frac = flat(real_ref[0, place, :])
        product = jnp.dot(lhs_ref[quarter], columns, preferred_element_type=jnp.float32)
        outer = jnp.broadcast_to(outer, (QUARTER, outer.shape[1]))
        picked = [product[part * QUARTER : (part + 1) * QUARTER] for part in range(parts)]
        for k in range(1, blocks):
            here = outer == k
            for part in range(parts):
                row = k * rows + part * QUARTER
                picked[part] = jnp.where(here, product[row : row + QUARTER], picked[part])
        weights = jnp.where(
            beam_ids == beam, 1.0 - frac, jnp.where(beam_ids == beam + 1, frac, 0.0)
        )
        for part in range(parts):
            summed = jnp.sum(weights * picked[part], axis=0, keepdims=True)
            for i in range(4):
                cart_ref[part, pl.ds(step * 4 + i, 1), :] = summed[:, i * LANES : (i + 1) * LANES]

    def window(quarter, carry):
        for i in range(2):
            step = quarter * 4 + 2 * i
            chunk(quarter, step, column_ref[quarter * 2 + i])
            chunk(quarter, step + 1, range_columns(whole_ref, real_ref, step + 1, width))
        return carry

    lax.fori_loop(0, 4, window, 0)
    for group in range(ROWS // 32):
        ordered = [
            swap_quarters(
                [
                    cart_ref[part, quarter * 16 + group * 8 : quarter * 16 + group * 8 + 8, :]
                    for quarter in range(4)
                ]
            )
            for part in range(parts)
        ]
        for j in range(4):
            start = group * 32 + 8 * j
            cosine = pixel_ref[0, start : start + 8, :]
            sine = pixel_ref[1, start : start + 8, :]
            real, imag = ordered[0][j], ordered[1][j]
            order_ref[pl.ds(2 * start, 8, stride=2), :] = cosine * real - sine * imag
            order_ref[pl.ds(2 * start + 1, 8, stride=2), :] = sine * real + cosine * imag
    out_ref[...] = order_ref[...].astype(jnp.bfloat16)


def body(
    polar_beams,
    band_start,
    band_weight,
    phase_rate,
    layer_wave,
    beam_map,
    range_map,
    pixel_frac,
    *,
    interpret=False,
):
    sub_index = lax.axis_index("sub")
    sub_count = lax.axis_size("sub")
    layers = lax.axis_size("hgt")
    beams = polar_beams.shape[2]
    range_count = polar_beams.shape[3]
    levels = band_start.shape[0]
    taps = band_weight.shape[-1]
    row_count, column_count = beam_map.shape
    matrices = levels * 4
    members = sub_count // 2
    width = range_count // members
    column_block = (sub_index >> 2) * 2 + (sub_index & 1)
    row_half = sub_index >> 1 & 1
    halves = [[s for s in range(sub_count) if s >> 1 & 1 == half] for half in range(2)]
    place = jnp.stack([column_block, row_half, column_block]).astype(jnp.int32)
    params = jnp.concatenate(
        [
            phase_rate.reshape(matrices, beams),
            band_start.reshape(matrices, beams).astype(jnp.float32),
            band_weight.reshape(matrices, beams, taps)
            .transpose(0, 2, 1)
            .reshape(matrices * taps, beams)
            .astype(jnp.float32),
        ],
        axis=0,
    ).T
    smem = pl.BlockSpec(memory_space=pltpu.SMEM)
    vmem = pl.BlockSpec(memory_space=pltpu.VMEM)
    shape = jax.ShapeDtypeStruct
    limit = pltpu.CompilerParams(vmem_limit_bytes=24 * 2**20)
    f32, bf16 = jnp.float32, jnp.bfloat16

    kept = shape if interpret else pltpu.VMEM

    def local(value):
        return value if interpret else pltpu.with_memory_space_constraint(value, pltpu.VMEM)

    slices = polar_beams.reshape(2, beams // 8, 8, members, width // LANES, LANES)
    slices = slices.transpose(3, 0, 1, 4, 2, 5)
    slices = lax.all_to_all(slices, "sub", 0, 0, axis_index_groups=halves, tiled=True)
    slices = slices.transpose(0, 1, 2, 4, 3, 5).reshape(members, 2, beams, width)
    slices = local(slices)
    trig, first, second, third, whole, real, pixel = pl.pallas_call(
        functools.partial(prepare_kernel, range_count=range_count),
        out_shape=[
            kept((10, 2, beams, width), f32),
            kept((4 * beams, 2 * beams), bf16),
            kept((2 * beams, 2 * beams), bf16),
            kept((4 * beams, 4 * beams), bf16),
            kept((3, row_count, LANES), jnp.int32),
            kept((2, row_count, LANES), f32),
            kept((2, row_count, LANES), f32),
        ],
        grid_spec=pltpu.PrefetchScalarGridSpec(
            num_scalar_prefetch=1,
            grid=(1,),
            in_specs=[
                smem,
                pl.BlockSpec((beams, params.shape[1]), lambda i, p: (0, 0)),
                pl.BlockSpec((row_count, LANES), lambda i, p: (0, p[0])),
                pl.BlockSpec((row_count, LANES), lambda i, p: (0, p[0])),
                pl.BlockSpec((2, row_count, LANES), lambda i, p: (0, 0, p[0])),
            ],
            out_specs=[
                pl.BlockSpec((10, 2, beams, width), lambda i, p: (0, 0, 0, 0)),
                pl.BlockSpec((4 * beams, 2 * beams), lambda i, p: (0, 0)),
                pl.BlockSpec((2 * beams, 2 * beams), lambda i, p: (0, 0)),
                pl.BlockSpec((4 * beams, 4 * beams), lambda i, p: (0, 0)),
                pl.BlockSpec((3, row_count, LANES), lambda i, p: (0, 0, 0)),
                pl.BlockSpec((2, row_count, LANES), lambda i, p: (0, 0, 0)),
                pl.BlockSpec((2, row_count, LANES), lambda i, p: (0, 0, 0)),
            ],
        ),
        interpret=interpret,
        name="prepare",
    )(place, layer_wave, params, beam_map, range_map, pixel_frac)
    windows = pl.pallas_call(
        functools.partial(merge_kernel, groups=sub_count // 2**levels),
        out_shape=kept((members, 2, WINDOW, width), bf16),
        in_specs=[vmem] * 5,
        out_specs=vmem,
        scratch_shapes=[pltpu.VMEM((2, 144, width), f32)],
        compiler_params=limit,
        interpret=interpret,
        name="merge",
    )(slices, local(trig), local(first), local(second), local(third))
    table = local(lax.all_to_all(windows, "sub", 0, 0, axis_index_groups=halves, tiled=True))
    columns = pl.pallas_call(
        weights_kernel,
        out_shape=kept((row_count // 8, width, 4 * LANES), bf16),
        in_specs=[pl.BlockSpec(memory_space=pl.ANY), vmem, vmem],
        out_specs=vmem,
        compiler_params=limit,
        interpret=interpret,
        name="weights",
    )(windows, local(whole), local(real))
    cart = pl.pallas_call(
        sample_kernel,
        out_shape=shape((2 * row_count, LANES), bf16),
        in_specs=[vmem] * 5,
        out_specs=vmem,
        scratch_shapes=[
            pltpu.VMEM((members + 1, 2, WINDOW, width), f32),
            pltpu.VMEM((4, (members + 1) * 2 * QUARTER, width), bf16),
            pltpu.VMEM((2, row_count, LANES), f32),
            pltpu.VMEM((2 * row_count, LANES), f32),
        ],
        compiler_params=limit,
        interpret=interpret,
        name="sample",
    )(table, local(columns), local(whole), local(real), local(pixel))
    tile_rows = row_count // sub_count
    tiles = cart.reshape(sub_count, tile_rows * 2, LANES)
    tiles = lax.all_to_all(tiles, "sub", 0, 0, tiled=True).astype(f32)
    tiles = tiles.reshape(sub_count // 4, 2, 2, tile_rows * 2, LANES)
    tile = (tiles[:, 0] + tiles[:, 1]).reshape(members, tile_rows, 2, LANES)
    above = lax.ppermute(tile, "hgt", [(i, i - 1) for i in range(1, layers)])
    height = lax.dynamic_slice_in_dim(pixel_frac[2], sub_index * tile_rows, tile_rows, 0)
    height = height.astype(f32).reshape(tile_rows, members, LANES).transpose(1, 0, 2)
    height = height[:, :, None, :]
    blended = (1.0 - height) * tile + height * above
    return blended.transpose(1, 2, 0, 3).reshape(tile_rows, 1, 2, column_count)


def solution(mesh):
    in_specs = (P("hgt", None, "sub", None), P(), P(), P(), P("hgt"), P(), P(), P())
    out_specs = P("sub", "hgt", None, None)
    return jax.shard_map(body, mesh=mesh, in_specs=in_specs, out_specs=out_specs, check_vma=False)
```

```python
import functools

import jax
import jax.numpy as jnp
from jax import lax
from jax.experimental import pallas as pl
from jax.experimental.pallas import tpu as pltpu
from jax.sharding import PartitionSpec as P

range_phase = 0.003
LANES = 128
WINDOW = 16
HALO = 4
QUARTER = 8
ROWS = 64


def swap_quarters(values):
    lane = lax.broadcasted_iota(jnp.int32, values[0].shape, 1)
    values = list(values)
    for bit, width in ((1, 64), (0, 32)):
        keep = lane & width == 0
        for i in range(4):
            if i >> bit & 1:
                continue
            j = i | 1 << bit
            a, b = values[i], values[j]
            values[i] = jnp.where(keep, a, pltpu.roll(b, width, 1))
            values[j] = jnp.where(keep, pltpu.roll(a, LANES - width, 1), b)
    return values


def block_of(sub_index):
    return (sub_index >> 2) * 2 + (sub_index & 1)


def prepare_kernel(
    place_ref,
    wave_ref,
    start_ref,
    weight_ref,
    rate_ref,
    beam_ref,
    range_ref,
    frac_ref,
    tall_ref,
    trig_ref,
    first_ref,
    second_ref,
    third_ref,
    whole_ref,
    real_ref,
    pixel_ref,
    height_ref,
    params_ref,
    tall_scratch,
    *,
    range_count,
):
    wave = wave_ref[0]
    levels, children, halves, taps, beams = weight_ref.shape
    matrices = levels * children * halves
    params_ref[...] = jnp.zeros_like(params_ref)
    for level in range(levels):
        for child in range(children):
            i = (level * children + child) * halves
            params_ref[i : i + halves, 0:beams] = rate_ref[level, child]
            row = matrices + i
            params_ref[row : row + halves, 0:beams] = start_ref[level, child].astype(jnp.float32)
            for half in range(halves):
                row = 2 * matrices + (i + half) * taps
                params_ref[row : row + taps, 0:beams] = weight_ref[level, child, half].astype(
                    jnp.float32
                )
    params = params_ref[...].T[0:beams]
    width = trig_ref.shape[3]
    lane = lax.broadcasted_iota(jnp.int32, (1, width), 1)
    sub_index = place_ref[0]
    column_block = block_of(sub_index)
    position = ((column_block * width + lane).astype(jnp.float32) + 0.5) / range_count
    upper = sub_index >> 1 & 1 == 1

    def column(offset, level, child, half):
        i = offset + (level * 2 + child) * 2 + half
        return params[:, i : i + 1]

    def mine(offset, level, half):
        return jnp.where(upper, column(offset, level, 1, half), column(offset, level, 0, half))

    def weight(tap, level, child, half):
        i = 2 * matrices + ((level * 2 + child) * 2 + half) * taps + tap
        return params[:, i : i + 1]

    rates = [column(0, 0, child, half) for half in range(2) for child in range(2)]
    rates += [mine(0, 1, half) for half in range(2)]
    rates += [column(0, 2, child, half) for half in range(2) for child in range(2)]
    for i, rate in enumerate(rates):
        angles = (wave * rate) * position
        trig_ref[i, 0] = jnp.cos(angles)
        trig_ref[i, 1] = jnp.sin(angles)

    def band(starts, weights):
        ids = lax.broadcasted_iota(jnp.int32, (beams, beams), 1).astype(jnp.float32) - starts
        block = jnp.zeros((beams, beams), jnp.float32)
        for tap in range(taps):
            block = jnp.where(ids == tap, weights[tap], block)
        return block

    def pair_bands(level, copies):
        rows = []
        for half in range(2):
            for child in range(2):
                block = band(
                    column(matrices, level, child, half),
                    [weight(tap, level, child, half) for tap in range(taps)],
                )
                empty = jnp.zeros_like(block)
                rows.append(
                    jnp.concatenate(
                        [block if c == child else empty for c in range(2) for _ in range(copies)],
                        axis=1,
                    )
                )
        return jnp.concatenate(rows, axis=0).astype(jnp.bfloat16)

    first_ref[...] = pair_bands(0, 1)
    third_ref[...] = pair_bands(2, 2)
    rows = []
    for half in range(2):
        block = band(
            mine(matrices, 1, half),
            [
                jnp.where(upper, weight(tap, 1, 1, half), weight(tap, 1, 0, half))
                for tap in range(taps)
            ],
        )
        rows.append(jnp.concatenate([block, block], axis=1))
    second_ref[...] = jnp.concatenate(rows, axis=0).astype(jnp.bfloat16)

    for block in range(height_ref.shape[0] // 4):
        tall_scratch[block] = tall_ref[0, :, block * LANES : (block + 1) * LANES].astype(
            jnp.float32
        )
        tall = tall_scratch[block, pl.ds((sub_index & 7) * 2, 2), :]
        for row in range(4):
            height_ref[pl.ds(block * 4 + row, 1), :] = tall[row // 2 : row // 2 + 1]
    samples = range_ref[...]
    fracs = [frac_ref[i].astype(jnp.float32) for i in range(2)]
    angles = (wave * range_phase) * (samples.astype(jnp.float32) + fracs[1])
    pixel_ref[0] = jnp.cos(angles)
    pixel_ref[1] = jnp.sin(angles)
    first_beam = column_block * 8 - HALO
    for group in range(ROWS // 32):
        rows = [slice(group * 32 + 8 * j, group * 32 + 8 * j + 8) for j in range(4)]
        sample_parts = swap_quarters([samples[r] for r in rows])
        beam_parts = swap_quarters([beam_ref[r, :] - first_beam for r in rows])
        frac_parts = [swap_quarters([fracs[i][r] for r in rows]) for i in range(2)]
        for quarter in range(4):
            place = slice(quarter * 16 + group * 8, quarter * 16 + group * 8 + 8)
            sample = sample_parts[quarter]
            block = (sample + 1 + (sample >> 8)) >> 8
            whole_ref[0, place, :] = sample - block * (width - 1)
            whole_ref[1, place, :] = block
            whole_ref[2, place, :] = beam_parts[quarter] - (2 * quarter + 2)
            for i in range(2):
                real_ref[i, place, :] = frac_parts[i][quarter]


def halves_of(value):
    high = value.astype(jnp.bfloat16)
    return high, (value - high.astype(jnp.float32)).astype(jnp.bfloat16)


def merge_kernel(
    data_ref, trig_ref, first_ref, second_ref, third_ref, before_ref, out_ref, padded_ref, *, groups
):
    del before_ref
    beams, width = data_ref.shape[2], data_ref.shape[3]

    def turn(i, product, row, col):
        real = product[row : row + beams, col : col + width]
        imag = product[row : row + beams, col + width : col + 2 * width]
        cosine, sine = trig_ref[i, 0], trig_ref[i, 1]
        return cosine * real - sine * imag, sine * real + cosine * imag

    def add(a, b):
        return a[0] + b[0], a[1] + b[1]

    sums = {}
    for low in range(2):
        for group in range(groups):
            source = (group * 2 + low) * 2
            stacked = jnp.concatenate(
                [
                    jnp.concatenate([data_ref[source + core, part] for part in range(2)], axis=1)
                    for core in range(2)
                ],
                axis=0,
            )
            product = jnp.dot(first_ref[...], stacked, preferred_element_type=jnp.float32)
            for half in range(2):
                terms = [
                    turn(half * 2 + child, product, (half * 2 + child) * beams, 0)
                    for child in range(2)
                ]
                level = tuple(
                    v.astype(jnp.bfloat16).astype(jnp.float32) for v in add(terms[0], terms[1])
                )
                sums[low, half] = level if group == 0 else add(sums[low, half], level)
    middle = {}
    for low in range(2):
        for half in range(2):
            parts = [halves_of(v) for v in sums[low, half]]
            stacked = jnp.concatenate(
                [jnp.concatenate([parts[0][i], parts[1][i]], axis=1) for i in range(2)], axis=0
            )
            product = jnp.dot(second_ref[...], stacked, preferred_element_type=jnp.float32)
            for next_half in range(2):
                middle[low, half, next_half] = turn(4 + next_half, product, next_half * beams, 0)
    merged = 8 * beams
    padding = padded_ref.shape[1] - HALO - merged
    for part in range(2):
        padded_ref[part, 0:HALO, :] = jnp.zeros((HALO, width), jnp.float32)
        padded_ref[part, HALO + merged :, :] = jnp.zeros((padding, width), jnp.float32)
    for half in range(2):
        for next_half in range(2):
            rows = []
            for low in range(2):
                parts = [halves_of(v) for v in middle[low, half, next_half]]
                rows += [jnp.concatenate([parts[0][i], parts[1][i]], axis=1) for i in range(2)]
            product = jnp.dot(
                third_ref[...], jnp.concatenate(rows, axis=0), preferred_element_type=jnp.float32
            )
            for last in range(2):
                terms = [
                    turn(6 + last * 2 + child, product, (last * 2 + child) * beams, 0)
                    for child in range(2)
                ]
                start = HALO + (half * 4 + next_half * 2 + last) * beams
                for part, value in enumerate(add(terms[0], terms[1])):
                    padded_ref[part, start : start + beams, :] = value
    for block in range(out_ref.shape[0]):
        for part in range(2):
            rows = padded_ref[part, 8 * block : 8 * block + WINDOW, :]
            out_ref[block, part] = rows.astype(jnp.bfloat16)


def flat(value):
    return jnp.concatenate([value[i : i + 1, :] for i in range(4)], axis=1)


def range_columns(whole_ref, real_ref, step, width):
    place = pl.ds(step * 4, 4)
    row_ids = lax.broadcasted_iota(jnp.int32, (width, 4 * LANES), 0)
    inner = flat(whole_ref[0, place, :])
    frac = flat(real_ref[1, place, :])
    column = jnp.where(row_ids == inner, 1.0 - frac, jnp.where(row_ids == inner + 1, frac, 0.0))
    return column.astype(jnp.bfloat16)


def weights_kernel(whole_ref, real_ref, out_ref):
    def chunk(step, carry):
        out_ref[step] = range_columns(whole_ref, real_ref, 2 * step, out_ref.shape[1])
        return carry

    lax.fori_loop(0, out_ref.shape[0], chunk, 0)


def sample_kernel(
    table_ref,
    column_ref,
    whole_ref,
    real_ref,
    pixel_ref,
    out_ref,
    block_ref,
    lhs_ref,
    cart_ref,
    order_ref,
):
    slices, parts, _, width = table_ref.shape
    blocks = slices + 1
    rows = parts * QUARTER
    lane = lax.broadcasted_iota(jnp.int32, (WINDOW, width), 1)
    for part in range(parts):
        values = [table_ref[i, part].astype(jnp.float32) for i in range(slices)]
        block_ref[0, part] = values[0]
        for k in range(1, blocks):
            before = pltpu.roll(values[k - 1], k, 1)
            after = pltpu.roll(values[k], k, 1) if k < slices else before
            block_ref[k, part] = jnp.where(lane < k, before, after)
    for quarter in range(4):
        low = 2 * quarter + 2
        for k in range(blocks):
            pair = [block_ref[k, part, low : low + QUARTER, :] for part in range(parts)]
            lhs_ref[quarter, k * rows : (k + 1) * rows, :] = jnp.concatenate(pair, axis=0).astype(
                jnp.bfloat16
            )
    beam_ids = lax.broadcasted_iota(jnp.int32, (QUARTER, column_ref.shape[2]), 0)

    def chunk(quarter, step, columns):
        place = pl.ds(step * 4, 4)
        outer, beam = flat(whole_ref[1, place, :]), flat(whole_ref[2, place, :])
        frac = flat(real_ref[0, place, :])
        product = jnp.dot(lhs_ref[quarter], columns, preferred_element_type=jnp.float32)
        outer = jnp.broadcast_to(outer, (QUARTER, outer.shape[1]))
        picked = [product[part * QUARTER : (part + 1) * QUARTER] for part in range(parts)]
        for k in range(1, blocks):
            here = outer == k
            for part in range(parts):
                row = k * rows + part * QUARTER
                picked[part] = jnp.where(here, product[row : row + QUARTER], picked[part])
        weights = jnp.where(
            beam_ids == beam, 1.0 - frac, jnp.where(beam_ids == beam + 1, frac, 0.0)
        )
        for part in range(parts):
            summed = jnp.sum(weights * picked[part], axis=0, keepdims=True)
            for i in range(4):
                cart_ref[part, pl.ds(step * 4 + i, 1), :] = summed[:, i * LANES : (i + 1) * LANES]

    def window(quarter, carry):
        for i in range(2):
            step = quarter * 4 + 2 * i
            chunk(quarter, step, column_ref[quarter * 2 + i])
            chunk(quarter, step + 1, range_columns(whole_ref, real_ref, step + 1, width))
        return carry

    lax.fori_loop(0, 4, window, 0)
    for group in range(ROWS // 32):
        ordered = [
            swap_quarters(
                [
                    cart_ref[part, quarter * 16 + group * 8 : quarter * 16 + group * 8 + 8, :]
                    for quarter in range(4)
                ]
            )
            for part in range(parts)
        ]
        for j in range(4):
            start = group * 32 + 8 * j
            cosine = pixel_ref[0, start : start + 8, :]
            sine = pixel_ref[1, start : start + 8, :]
            real, imag = ordered[0][j], ordered[1][j]
            order_ref[pl.ds(2 * start, 8, stride=2), :] = cosine * real - sine * imag
            order_ref[pl.ds(2 * start + 1, 8, stride=2), :] = sine * real + cosine * imag
    out_ref[...] = order_ref[...].astype(jnp.bfloat16)


def body(
    polar_beams,
    band_start,
    band_weight,
    phase_rate,
    layer_wave,
    beam_map,
    range_map,
    pixel_frac,
    *,
    interpret=False,
):
    sub_index = lax.axis_index("sub")
    sub_count = lax.axis_size("sub")
    layers = lax.axis_size("hgt")
    beams = polar_beams.shape[2]
    range_count = polar_beams.shape[3]
    levels = band_start.shape[0]
    taps = band_weight.shape[-1]
    row_count, column_count = beam_map.shape
    members = sub_count // 2
    width = range_count // members
    halves = [[s for s in range(sub_count) if s >> 1 & 1 == half] for half in range(2)]
    place = sub_index.astype(jnp.int32).reshape(1)
    smem = pl.BlockSpec(memory_space=pltpu.SMEM)
    vmem = pl.BlockSpec(memory_space=pltpu.VMEM)
    shape = jax.ShapeDtypeStruct
    limit = pltpu.CompilerParams(vmem_limit_bytes=24 * 2**20)
    f32, bf16 = jnp.float32, jnp.bfloat16

    kept = shape if interpret else pltpu.VMEM

    def local(value):
        return value if interpret else pltpu.with_memory_space_constraint(value, pltpu.VMEM)

    slices = polar_beams.reshape(2, beams // 8, 8, members, width // LANES, LANES)
    slices = slices.transpose(3, 0, 1, 4, 2, 5)
    slices = lax.all_to_all(slices, "sub", 0, 0, axis_index_groups=halves, tiled=True)
    slices = slices.transpose(0, 1, 2, 4, 3, 5).reshape(members, 2, beams, width)
    slices = local(slices)
    trig, first, second, third, whole, real, pixel, height = pl.pallas_call(
        functools.partial(prepare_kernel, range_count=range_count),
        out_shape=[
            kept((10, 2, beams, width), f32),
            kept((4 * beams, 2 * beams), bf16),
            kept((2 * beams, 2 * beams), bf16),
            kept((4 * beams, 4 * beams), bf16),
            kept((3, row_count, LANES), jnp.int32),
            kept((2, row_count, LANES), f32),
            kept((2, row_count, LANES), f32),
            shape((4 * members, LANES), f32),
        ],
        grid_spec=pltpu.PrefetchScalarGridSpec(
            num_scalar_prefetch=1,
            grid=(1,),
            in_specs=[
                smem,
                pl.BlockSpec(band_start.shape, lambda i, p: (0, 0, 0, 0)),
                pl.BlockSpec((levels, 2, 2, taps, beams), lambda i, p: (0, 0, 0, 0, 0)),
                pl.BlockSpec(phase_rate.shape, lambda i, p: (0, 0, 0, 0)),
                pl.BlockSpec((row_count, LANES), lambda i, p: (0, block_of(p[0]))),
                pl.BlockSpec((row_count, LANES), lambda i, p: (0, block_of(p[0]))),
                pl.BlockSpec((2, row_count, LANES), lambda i, p: (0, 0, block_of(p[0]))),
                pl.BlockSpec((1, 16, column_count), lambda i, p: (2, p[0] >> 3, 0)),
            ],
            out_specs=[
                pl.BlockSpec((10, 2, beams, width), lambda i, p: (0, 0, 0, 0)),
                pl.BlockSpec((4 * beams, 2 * beams), lambda i, p: (0, 0)),
                pl.BlockSpec((2 * beams, 2 * beams), lambda i, p: (0, 0)),
                pl.BlockSpec((4 * beams, 4 * beams), lambda i, p: (0, 0)),
                pl.BlockSpec((3, row_count, LANES), lambda i, p: (0, 0, 0)),
                pl.BlockSpec((2, row_count, LANES), lambda i, p: (0, 0, 0)),
                pl.BlockSpec((2, row_count, LANES), lambda i, p: (0, 0, 0)),
                pl.BlockSpec((4 * members, LANES), lambda i, p: (0, 0)),
            ],
            scratch_shapes=[
                pltpu.VMEM((LANES, LANES), f32),
                pltpu.VMEM((members, 16, LANES), f32),
            ],
        ),
        interpret=interpret,
        name="prepare",
    )(
        place,
        layer_wave,
        band_start,
        band_weight.transpose(0, 1, 2, 4, 3),
        phase_rate,
        beam_map,
        range_map,
        pixel_frac,
        pixel_frac,
    )
    columns = pl.pallas_call(
        weights_kernel,
        out_shape=kept((row_count // 8, width, 4 * LANES), bf16),
        in_specs=[vmem, vmem],
        out_specs=vmem,
        compiler_params=limit,
        interpret=interpret,
        name="weights",
    )(local(whole), local(real))
    windows = pl.pallas_call(
        functools.partial(merge_kernel, groups=sub_count // 2**levels),
        out_shape=kept((members, 2, WINDOW, width), bf16),
        in_specs=[vmem] * 5 + [pl.BlockSpec(memory_space=pl.ANY)],
        out_specs=vmem,
        scratch_shapes=[pltpu.VMEM((2, 144, width), f32)],
        compiler_params=limit,
        interpret=interpret,
        name="merge",
    )(slices, local(trig), local(first), local(second), local(third), local(columns))
    table = local(lax.all_to_all(windows, "sub", 0, 0, axis_index_groups=halves, tiled=True))
    cart = pl.pallas_call(
        sample_kernel,
        out_shape=kept((2 * row_count, LANES), bf16),
        in_specs=[vmem] * 5,
        out_specs=vmem,
        scratch_shapes=[
            pltpu.VMEM((members + 1, 2, WINDOW, width), f32),
            pltpu.VMEM((4, (members + 1) * 2 * QUARTER, width), bf16),
            pltpu.VMEM((2, row_count, LANES), f32),
            pltpu.VMEM((2 * row_count, LANES), f32),
        ],
        compiler_params=limit,
        interpret=interpret,
        name="sample",
    )(table, local(columns), local(whole), local(real), local(pixel))
    tile_rows = row_count // sub_count
    tiles = cart.reshape(sub_count, tile_rows * 2, LANES)
    tiles = lax.all_to_all(tiles, "sub", 0, 0, tiled=True).astype(f32)
    tiles = tiles.reshape(sub_count // 4, 2, 2, tile_rows * 2, LANES)
    tile = (tiles[:, 0] + tiles[:, 1]).reshape(members, tile_rows, 2, LANES)
    above = lax.ppermute(tile, "hgt", [(i, i - 1) for i in range(1, layers)])
    height = height.reshape(members, tile_rows, 2, LANES)
    blended = (1.0 - height) * tile + height * above
    return blended.transpose(1, 2, 0, 3).reshape(tile_rows, 1, 2, column_count)


def solution(mesh):
    in_specs = (P("hgt", None, "sub", None), P(), P(), P(), P("hgt"), P(), P(), P())
    out_specs = P("sub", "hgt", None, None)
    return jax.shard_map(body, mesh=mesh, in_specs=in_specs, out_specs=out_specs, check_vma=False)
```

```python
import functools

import jax
import jax.numpy as jnp
from jax import lax
from jax.experimental import pallas as pl
from jax.experimental.pallas import tpu as pltpu
from jax.sharding import PartitionSpec as P

range_phase = 0.003
LANES = 128
WINDOW = 16
HALO = 4
QUARTER = 8
ROWS = 64


def swap_quarters(values):
    lane = lax.broadcasted_iota(jnp.int32, values[0].shape, 1)
    values = list(values)
    for bit, width in ((1, 64), (0, 32)):
        keep = lane & width == 0
        for i in range(4):
            if i >> bit & 1:
                continue
            j = i | 1 << bit
            a, b = values[i], values[j]
            values[i] = jnp.where(keep, a, pltpu.roll(b, width, 1))
            values[j] = jnp.where(keep, pltpu.roll(a, LANES - width, 1), b)
    return values


def block_of(sub_index):
    return (sub_index >> 2) * 2 + (sub_index & 1)


def prepare_kernel(
    place_ref,
    wave_ref,
    start_ref,
    weight_ref,
    rate_ref,
    beam_ref,
    range_ref,
    frac_ref,
    tall_ref,
    trig_ref,
    first_ref,
    second_ref,
    third_ref,
    whole_ref,
    real_ref,
    pixel_ref,
    height_ref,
    params_ref,
    tall_scratch,
    *,
    range_count,
):
    wave = wave_ref[0]
    levels, children, halves, taps, beams = weight_ref.shape
    matrices = levels * children * halves
    params_ref[...] = jnp.zeros_like(params_ref)
    for level in range(levels):
        for child in range(children):
            i = (level * children + child) * halves
            params_ref[i : i + halves, 0:beams] = rate_ref[level, child]
            row = matrices + i
            params_ref[row : row + halves, 0:beams] = start_ref[level, child].astype(jnp.float32)
            for half in range(halves):
                row = 2 * matrices + (i + half) * taps
                params_ref[row : row + taps, 0:beams] = weight_ref[level, child, half].astype(
                    jnp.float32
                )
    params = params_ref[...].T[0:beams]
    width = trig_ref.shape[3]
    lane = lax.broadcasted_iota(jnp.int32, (1, width), 1)
    sub_index = place_ref[0]
    column_block = block_of(sub_index)
    position = ((column_block * width + lane).astype(jnp.float32) + 0.5) / range_count
    upper = sub_index >> 1 & 1 == 1

    def column(offset, level, child, half):
        i = offset + (level * 2 + child) * 2 + half
        return params[:, i : i + 1]

    def mine(offset, level, half):
        return jnp.where(upper, column(offset, level, 1, half), column(offset, level, 0, half))

    def weight(tap, level, child, half):
        i = 2 * matrices + ((level * 2 + child) * 2 + half) * taps + tap
        return params[:, i : i + 1]

    rates = [column(0, 0, child, half) for half in range(2) for child in range(2)]
    rates += [mine(0, 1, half) for half in range(2)]
    rates += [column(0, 2, child, half) for half in range(2) for child in range(2)]
    for i, rate in enumerate(rates):
        angles = (wave * rate) * position
        trig_ref[i, 0] = jnp.cos(angles)
        trig_ref[i, 1] = jnp.sin(angles)

    def band(starts, weights):
        ids = lax.broadcasted_iota(jnp.int32, (beams, beams), 1).astype(jnp.float32) - starts
        block = jnp.zeros((beams, beams), jnp.float32)
        for tap in range(taps):
            block = jnp.where(ids == tap, weights[tap], block)
        return block

    def pair_bands(level, copies):
        rows = []
        for half in range(2):
            for child in range(2):
                block = band(
                    column(matrices, level, child, half),
                    [weight(tap, level, child, half) for tap in range(taps)],
                )
                empty = jnp.zeros_like(block)
                rows.append(
                    jnp.concatenate(
                        [block if c == child else empty for c in range(2) for _ in range(copies)],
                        axis=1,
                    )
                )
        return jnp.concatenate(rows, axis=0).astype(jnp.bfloat16)

    first_ref[...] = pair_bands(0, 1)
    third_ref[...] = pair_bands(2, 2)
    rows = []
    for half in range(2):
        block = band(
            mine(matrices, 1, half),
            [
                jnp.where(upper, weight(tap, 1, 1, half), weight(tap, 1, 0, half))
                for tap in range(taps)
            ],
        )
        rows.append(jnp.concatenate([block, block], axis=1))
    second_ref[...] = jnp.concatenate(rows, axis=0).astype(jnp.bfloat16)

    for block in range(height_ref.shape[0] // 4):
        tall_scratch[block] = tall_ref[0, :, block * LANES : (block + 1) * LANES].astype(
            jnp.float32
        )
        tall = tall_scratch[block, pl.ds((sub_index & 7) * 2, 2), :]
        for row in range(4):
            height_ref[pl.ds(block * 4 + row, 1), :] = tall[row // 2 : row // 2 + 1]
    samples = range_ref[...]
    fracs = [frac_ref[i].astype(jnp.float32) for i in range(2)]
    angles = (wave * range_phase) * (samples.astype(jnp.float32) + fracs[1])
    pixel_ref[0] = jnp.cos(angles)
    pixel_ref[1] = jnp.sin(angles)
    first_beam = column_block * 8 - HALO
    for group in range(ROWS // 32):
        rows = [slice(group * 32 + 8 * j, group * 32 + 8 * j + 8) for j in range(4)]
        sample_parts = swap_quarters([samples[r] for r in rows])
        beam_parts = swap_quarters([beam_ref[r, :] - first_beam for r in rows])
        frac_parts = [swap_quarters([fracs[i][r] for r in rows]) for i in range(2)]
        for quarter in range(4):
            place = slice(quarter * 16 + group * 8, quarter * 16 + group * 8 + 8)
            sample = sample_parts[quarter]
            block = (sample + 1 + (sample >> 8)) >> 8
            whole_ref[0, place, :] = sample - block * (width - 1)
            whole_ref[1, place, :] = block
            whole_ref[2, place, :] = beam_parts[quarter] - (2 * quarter + 2)
            for i in range(2):
                real_ref[i, place, :] = frac_parts[i][quarter]


def halves_of(value):
    high = value.astype(jnp.bfloat16)
    return high, (value - high.astype(jnp.float32)).astype(jnp.bfloat16)


def merge_kernel(
    data_ref, trig_ref, first_ref, second_ref, third_ref, before_ref, out_ref, padded_ref, *, groups
):
    del before_ref
    beams, width = data_ref.shape[2], data_ref.shape[3]

    def turn(i, product, row, col):
        real = product[row : row + beams, col : col + width]
        imag = product[row : row + beams, col + width : col + 2 * width]
        cosine, sine = trig_ref[i, 0], trig_ref[i, 1]
        return cosine * real - sine * imag, sine * real + cosine * imag

    def add(a, b):
        return a[0] + b[0], a[1] + b[1]

    sums = {}
    for low in range(2):
        for group in range(groups):
            source = (group * 2 + low) * 2
            stacked = jnp.concatenate(
                [
                    jnp.concatenate([data_ref[source + core, part] for part in range(2)], axis=1)
                    for core in range(2)
                ],
                axis=0,
            )
            product = jnp.dot(first_ref[...], stacked, preferred_element_type=jnp.float32)
            for half in range(2):
                terms = [
                    turn(half * 2 + child, product, (half * 2 + child) * beams, 0)
                    for child in range(2)
                ]
                level = tuple(
                    v.astype(jnp.bfloat16).astype(jnp.float32) for v in add(terms[0], terms[1])
                )
                sums[low, half] = level if group == 0 else add(sums[low, half], level)
    middle = {}
    for low in range(2):
        for half in range(2):
            parts = [halves_of(v) for v in sums[low, half]]
            stacked = jnp.concatenate(
                [jnp.concatenate([parts[0][i], parts[1][i]], axis=1) for i in range(2)], axis=0
            )
            product = jnp.dot(second_ref[...], stacked, preferred_element_type=jnp.float32)
            for next_half in range(2):
                middle[low, half, next_half] = turn(4 + next_half, product, next_half * beams, 0)
    merged = 8 * beams
    padding = padded_ref.shape[1] - HALO - merged
    for part in range(2):
        padded_ref[part, 0:HALO, :] = jnp.zeros((HALO, width), jnp.float32)
        padded_ref[part, HALO + merged :, :] = jnp.zeros((padding, width), jnp.float32)
    for half in range(2):
        for next_half in range(2):
            rows = []
            for low in range(2):
                parts = [halves_of(v) for v in middle[low, half, next_half]]
                rows += [jnp.concatenate([parts[0][i], parts[1][i]], axis=1) for i in range(2)]
            product = jnp.dot(
                third_ref[...], jnp.concatenate(rows, axis=0), preferred_element_type=jnp.float32
            )
            for last in range(2):
                terms = [
                    turn(6 + last * 2 + child, product, (last * 2 + child) * beams, 0)
                    for child in range(2)
                ]
                start = HALO + (half * 4 + next_half * 2 + last) * beams
                for part, value in enumerate(add(terms[0], terms[1])):
                    padded_ref[part, start : start + beams, :] = value
    for block in range(out_ref.shape[0]):
        for part in range(2):
            rows = padded_ref[part, 8 * block : 8 * block + WINDOW, :]
            out_ref[block, part] = rows.astype(jnp.bfloat16)


def flat(value):
    return jnp.concatenate([value[i : i + 1, :] for i in range(4)], axis=1)


def range_columns(whole_ref, real_ref, step, width):
    place = pl.ds(step * 4, 4)
    row_ids = lax.broadcasted_iota(jnp.int16, (width, 4 * LANES), 0)
    inner = flat(whole_ref[0, place, :])
    frac = flat(real_ref[1, place, :])
    low, high = (1.0 - frac).astype(jnp.bfloat16), frac.astype(jnp.bfloat16)
    first, second = inner.astype(jnp.int16), (inner + 1).astype(jnp.int16)
    return jnp.where(row_ids == first, low, jnp.where(row_ids == second, high, jnp.bfloat16(0)))


def weights_kernel(whole_ref, real_ref, out_ref):
    def chunk(step, carry):
        out_ref[step] = range_columns(whole_ref, real_ref, 2 * step, out_ref.shape[1])
        return carry

    lax.fori_loop(0, out_ref.shape[0], chunk, 0)


def sample_kernel(
    table_ref,
    column_ref,
    whole_ref,
    real_ref,
    pixel_ref,
    out_ref,
    block_ref,
    lhs_ref,
    cart_ref,
    order_ref,
):
    slices, parts, _, width = table_ref.shape
    blocks = slices + 1
    rows = parts * QUARTER
    lane = lax.broadcasted_iota(jnp.int32, (WINDOW, width), 1)
    for part in range(parts):
        values = [table_ref[i, part].astype(jnp.float32) for i in range(slices)]
        block_ref[0, part] = values[0]
        for k in range(1, blocks):
            before = pltpu.roll(values[k - 1], k, 1)
            after = pltpu.roll(values[k], k, 1) if k < slices else before
            block_ref[k, part] = jnp.where(lane < k, before, after)
    for quarter in range(4):
        low = 2 * quarter + 2
        for k in range(blocks):
            pair = [block_ref[k, part, low : low + QUARTER, :] for part in range(parts)]
            lhs_ref[quarter, k * rows : (k + 1) * rows, :] = jnp.concatenate(pair, axis=0).astype(
                jnp.bfloat16
            )
    beam_ids = lax.broadcasted_iota(jnp.int32, (QUARTER, column_ref.shape[2]), 0)

    def chunk(quarter, step, columns):
        place = pl.ds(step * 4, 4)
        outer, beam = flat(whole_ref[1, place, :]), flat(whole_ref[2, place, :])
        frac = flat(real_ref[0, place, :])
        product = jnp.dot(lhs_ref[quarter], columns, preferred_element_type=jnp.float32)
        outer = jnp.broadcast_to(outer, (QUARTER, outer.shape[1]))
        picked = [product[part * QUARTER : (part + 1) * QUARTER] for part in range(parts)]
        for k in range(1, blocks):
            here = outer == k
            for part in range(parts):
                row = k * rows + part * QUARTER
                picked[part] = jnp.where(here, product[row : row + QUARTER], picked[part])
        weights = jnp.where(
            beam_ids == beam, 1.0 - frac, jnp.where(beam_ids == beam + 1, frac, 0.0)
        )
        for part in range(parts):
            summed = jnp.sum(weights * picked[part], axis=0, keepdims=True)
            for i in range(4):
                cart_ref[part, pl.ds(step * 4 + i, 1), :] = summed[:, i * LANES : (i + 1) * LANES]

    def window(quarter, carry):
        for i in range(2):
            step = quarter * 4 + 2 * i
            chunk(quarter, step, column_ref[quarter * 2 + i])
            chunk(quarter, step + 1, range_columns(whole_ref, real_ref, step + 1, width))
        return carry

    lax.fori_loop(0, 4, window, 0)
    for group in range(ROWS // 32):
        ordered = [
            swap_quarters(
                [
                    cart_ref[part, quarter * 16 + group * 8 : quarter * 16 + group * 8 + 8, :]
                    for quarter in range(4)
                ]
            )
            for part in range(parts)
        ]
        for j in range(4):
            start = group * 32 + 8 * j
            cosine = pixel_ref[0, start : start + 8, :]
            sine = pixel_ref[1, start : start + 8, :]
            real, imag = ordered[0][j], ordered[1][j]
            order_ref[pl.ds(2 * start, 8, stride=2), :] = cosine * real - sine * imag
            order_ref[pl.ds(2 * start + 1, 8, stride=2), :] = sine * real + cosine * imag
    out_ref[...] = order_ref[...].astype(jnp.bfloat16)


def blend_kernel(tile_ref, above_ref, height_ref, out_ref):
    for block in range(tile_ref.shape[0]):
        height = height_ref[block * 4 : block * 4 + 4, :]
        value = (1.0 - height) * tile_ref[block] + height * above_ref[block]
        for row in range(out_ref.shape[0]):
            out_ref[row, 0, :, block * LANES : (block + 1) * LANES] = value[2 * row : 2 * row + 2]


def body(
    polar_beams,
    band_start,
    band_weight,
    phase_rate,
    layer_wave,
    beam_map,
    range_map,
    pixel_frac,
    *,
    interpret=False,
):
    sub_index = lax.axis_index("sub")
    sub_count = lax.axis_size("sub")
    layers = lax.axis_size("hgt")
    beams = polar_beams.shape[2]
    range_count = polar_beams.shape[3]
    levels = band_start.shape[0]
    taps = band_weight.shape[-1]
    row_count, column_count = beam_map.shape
    members = sub_count // 2
    width = range_count // members
    halves = [[s for s in range(sub_count) if s >> 1 & 1 == half] for half in range(2)]
    place = sub_index.astype(jnp.int32).reshape(1)
    smem = pl.BlockSpec(memory_space=pltpu.SMEM)
    vmem = pl.BlockSpec(memory_space=pltpu.VMEM)
    shape = jax.ShapeDtypeStruct
    limit = pltpu.CompilerParams(vmem_limit_bytes=24 * 2**20)
    f32, bf16 = jnp.float32, jnp.bfloat16

    kept = shape if interpret else pltpu.VMEM

    def local(value):
        return value if interpret else pltpu.with_memory_space_constraint(value, pltpu.VMEM)

    slices = polar_beams.reshape(2, beams // 8, 8, members, width // LANES, LANES)
    slices = slices.transpose(3, 0, 1, 4, 2, 5)
    slices = lax.all_to_all(slices, "sub", 0, 0, axis_index_groups=halves, tiled=True)
    slices = slices.transpose(0, 1, 2, 4, 3, 5).reshape(members, 2, beams, width)
    slices = local(slices)
    trig, first, second, third, whole, real, pixel, height = pl.pallas_call(
        functools.partial(prepare_kernel, range_count=range_count),
        out_shape=[
            kept((10, 2, beams, width), f32),
            kept((4 * beams, 2 * beams), bf16),
            kept((2 * beams, 2 * beams), bf16),
            kept((4 * beams, 4 * beams), bf16),
            kept((3, row_count, LANES), jnp.int32),
            kept((2, row_count, LANES), f32),
            kept((2, row_count, LANES), f32),
            kept((4 * members, LANES), f32),
        ],
        grid_spec=pltpu.PrefetchScalarGridSpec(
            num_scalar_prefetch=1,
            grid=(1,),
            in_specs=[
                smem,
                pl.BlockSpec(band_start.shape, lambda i, p: (0, 0, 0, 0)),
                pl.BlockSpec((levels, 2, 2, taps, beams), lambda i, p: (0, 0, 0, 0, 0)),
                pl.BlockSpec(phase_rate.shape, lambda i, p: (0, 0, 0, 0)),
                pl.BlockSpec((row_count, LANES), lambda i, p: (0, block_of(p[0]))),
                pl.BlockSpec((row_count, LANES), lambda i, p: (0, block_of(p[0]))),
                pl.BlockSpec((2, row_count, LANES), lambda i, p: (0, 0, block_of(p[0]))),
                pl.BlockSpec((1, 16, column_count), lambda i, p: (2, p[0] >> 3, 0)),
            ],
            out_specs=[
                pl.BlockSpec((10, 2, beams, width), lambda i, p: (0, 0, 0, 0)),
                pl.BlockSpec((4 * beams, 2 * beams), lambda i, p: (0, 0)),
                pl.BlockSpec((2 * beams, 2 * beams), lambda i, p: (0, 0)),
                pl.BlockSpec((4 * beams, 4 * beams), lambda i, p: (0, 0)),
                pl.BlockSpec((3, row_count, LANES), lambda i, p: (0, 0, 0)),
                pl.BlockSpec((2, row_count, LANES), lambda i, p: (0, 0, 0)),
                pl.BlockSpec((2, row_count, LANES), lambda i, p: (0, 0, 0)),
                pl.BlockSpec((4 * members, LANES), lambda i, p: (0, 0)),
            ],
            scratch_shapes=[
                pltpu.VMEM((LANES, LANES), f32),
                pltpu.VMEM((members, 16, LANES), f32),
            ],
        ),
        interpret=interpret,
        name="prepare",
    )(
        place,
        layer_wave,
        band_start,
        band_weight.transpose(0, 1, 2, 4, 3),
        phase_rate,
        beam_map,
        range_map,
        pixel_frac,
        pixel_frac,
    )
    columns = pl.pallas_call(
        weights_kernel,
        out_shape=kept((row_count // 8, width, 4 * LANES), bf16),
        in_specs=[vmem, vmem],
        out_specs=vmem,
        compiler_params=limit,
        interpret=interpret,
        name="weights",
    )(local(whole), local(real))
    windows = pl.pallas_call(
        functools.partial(merge_kernel, groups=sub_count // 2**levels),
        out_shape=kept((members, 2, WINDOW, width), bf16),
        in_specs=[vmem] * 5 + [pl.BlockSpec(memory_space=pl.ANY)],
        out_specs=vmem,
        scratch_shapes=[pltpu.VMEM((2, 144, width), f32)],
        compiler_params=limit,
        interpret=interpret,
        name="merge",
    )(slices, local(trig), local(first), local(second), local(third), local(columns))
    table = local(lax.all_to_all(windows, "sub", 0, 0, axis_index_groups=halves, tiled=True))
    cart = pl.pallas_call(
        sample_kernel,
        out_shape=kept((2 * row_count, LANES), bf16),
        in_specs=[vmem] * 5,
        out_specs=vmem,
        scratch_shapes=[
            pltpu.VMEM((members + 1, 2, WINDOW, width), f32),
            pltpu.VMEM((4, (members + 1) * 2 * QUARTER, width), bf16),
            pltpu.VMEM((2, row_count, LANES), f32),
            pltpu.VMEM((2 * row_count, LANES), f32),
        ],
        compiler_params=limit,
        interpret=interpret,
        name="sample",
    )(table, local(columns), local(whole), local(real), local(pixel))
    tile_rows = row_count // sub_count
    tiles = cart.reshape(sub_count, tile_rows * 2, LANES)
    tiles = lax.all_to_all(tiles, "sub", 0, 0, tiled=True).astype(f32)
    tiles = tiles.reshape(sub_count // 4, 2, 2 * tile_rows * 2, LANES)
    tile = (tiles[:, 0] + tiles[:, 1]).reshape(members, tile_rows * 2, LANES)
    above = lax.ppermute(tile, "hgt", [(i, i - 1) for i in range(1, layers)])
    return pl.pallas_call(
        blend_kernel,
        out_shape=shape((tile_rows, 1, 2, column_count), f32),
        in_specs=[vmem] * 3,
        out_specs=vmem,
        interpret=interpret,
        name="blend",
    )(local(tile), local(above), local(height))


def solution(mesh):
    in_specs = (P("hgt", None, "sub", None), P(), P(), P(), P("hgt"), P(), P(), P())
    out_specs = P("sub", "hgt", None, None)
    return jax.shard_map(body, mesh=mesh, in_specs=in_specs, out_specs=out_specs, check_vma=False)
```

```python
import functools

import jax
import jax.numpy as jnp
from jax import lax
from jax.experimental import pallas as pl
from jax.experimental.pallas import tpu as pltpu
from jax.sharding import PartitionSpec as P

range_phase = 0.003
LANES = 128
WINDOW = 16
HALO = 4
QUARTER = 8
ROWS = 64


def swap_quarters(values):
    lane = lax.broadcasted_iota(jnp.int32, values[0].shape, 1)
    values = list(values)
    for bit, width in ((1, 64), (0, 32)):
        keep = lane & width == 0
        for i in range(4):
            if i >> bit & 1:
                continue
            j = i | 1 << bit
            a, b = values[i], values[j]
            values[i] = jnp.where(keep, a, pltpu.roll(b, width, 1))
            values[j] = jnp.where(keep, pltpu.roll(a, LANES - width, 1), b)
    return values


def block_of(sub_index):
    return (sub_index >> 2) * 2 + (sub_index & 1)


def prepare_kernel(
    place_ref,
    wave_ref,
    start_ref,
    weight_ref,
    rate_ref,
    beam_ref,
    range_ref,
    frac_ref,
    tall_ref,
    trig_ref,
    first_ref,
    second_ref,
    third_ref,
    whole_ref,
    real_ref,
    pixel_ref,
    height_ref,
    params_ref,
    tall_scratch,
    *,
    range_count,
):
    wave = wave_ref[0]
    levels, children, halves, taps, beams = weight_ref.shape
    matrices = levels * children * halves
    params_ref[...] = jnp.zeros_like(params_ref)
    for level in range(levels):
        for child in range(children):
            i = (level * children + child) * halves
            params_ref[i : i + halves, 0:beams] = rate_ref[level, child]
            row = matrices + i
            params_ref[row : row + halves, 0:beams] = start_ref[level, child].astype(jnp.float32)
            for half in range(halves):
                row = 2 * matrices + (i + half) * taps
                params_ref[row : row + taps, 0:beams] = weight_ref[level, child, half].astype(
                    jnp.float32
                )
    params = params_ref[...].T[0:beams]
    width = trig_ref.shape[3]
    lane = lax.broadcasted_iota(jnp.int32, (1, width), 1)
    sub_index = place_ref[0]
    column_block = block_of(sub_index)
    position = ((column_block * width + lane).astype(jnp.float32) + 0.5) / range_count
    upper = sub_index >> 1 & 1 == 1

    def column(offset, level, child, half):
        i = offset + (level * 2 + child) * 2 + half
        return params[:, i : i + 1]

    def mine(offset, level, half):
        return jnp.where(upper, column(offset, level, 1, half), column(offset, level, 0, half))

    def weight(tap, level, child, half):
        i = 2 * matrices + ((level * 2 + child) * 2 + half) * taps + tap
        return params[:, i : i + 1]

    rates = [column(0, 0, child, half) for half in range(2) for child in range(2)]
    rates += [mine(0, 1, half) for half in range(2)]
    rates += [column(0, 2, child, half) for half in range(2) for child in range(2)]
    for i, rate in enumerate(rates):
        angles = (wave * rate) * position
        trig_ref[i, 0] = jnp.cos(angles)
        trig_ref[i, 1] = jnp.sin(angles)

    def band(starts, weights):
        ids = lax.broadcasted_iota(jnp.int32, (beams, beams), 1).astype(jnp.float32) - starts
        block = jnp.zeros((beams, beams), jnp.float32)
        for tap in range(taps):
            block = jnp.where(ids == tap, weights[tap], block)
        return block

    def pair_bands(level, copies):
        rows = []
        for half in range(2):
            for child in range(2):
                block = band(
                    column(matrices, level, child, half),
                    [weight(tap, level, child, half) for tap in range(taps)],
                )
                empty = jnp.zeros_like(block)
                rows.append(
                    jnp.concatenate(
                        [block if c == child else empty for c in range(2) for _ in range(copies)],
                        axis=1,
                    )
                )
        return jnp.concatenate(rows, axis=0).astype(jnp.bfloat16)

    first_ref[...] = pair_bands(0, 1)
    third_ref[...] = pair_bands(2, 2)
    rows = []
    for half in range(2):
        block = band(
            mine(matrices, 1, half),
            [
                jnp.where(upper, weight(tap, 1, 1, half), weight(tap, 1, 0, half))
                for tap in range(taps)
            ],
        )
        rows.append(jnp.concatenate([block, block], axis=1))
    second_ref[...] = jnp.concatenate(rows, axis=0).astype(jnp.bfloat16)

    for block in range(height_ref.shape[0] // 4):
        tall_scratch[block] = tall_ref[0, :, block * LANES : (block + 1) * LANES].astype(
            jnp.float32
        )
        tall = tall_scratch[block, pl.ds((sub_index & 7) * 2, 2), :]
        for row in range(4):
            height_ref[pl.ds(block * 4 + row, 1), :] = tall[row // 2 : row // 2 + 1]
    samples = range_ref[...]
    fracs = [frac_ref[i].astype(jnp.float32) for i in range(2)]
    angles = (wave * range_phase) * (samples.astype(jnp.float32) + fracs[1])
    pixel_ref[0] = jnp.cos(angles)
    pixel_ref[1] = jnp.sin(angles)
    first_beam = column_block * 8 - HALO
    for group in range(ROWS // 32):
        rows = [slice(group * 32 + 8 * j, group * 32 + 8 * j + 8) for j in range(4)]
        sample_parts = swap_quarters([samples[r] for r in rows])
        beam_parts = swap_quarters([beam_ref[r, :] - first_beam for r in rows])
        frac_parts = [swap_quarters([fracs[i][r] for r in rows]) for i in range(2)]
        for quarter in range(4):
            place = slice(quarter * 16 + group * 8, quarter * 16 + group * 8 + 8)
            sample = sample_parts[quarter]
            block = (sample + 1 + (sample >> 8)) >> 8
            whole_ref[0, place, :] = sample - block * (width - 1)
            whole_ref[1, place, :] = block
            whole_ref[2, place, :] = beam_parts[quarter] - (2 * quarter + 2)
            for i in range(2):
                real_ref[i, place, :] = frac_parts[i][quarter]


def halves_of(value):
    high = value.astype(jnp.bfloat16)
    return high, (value - high.astype(jnp.float32)).astype(jnp.bfloat16)


def merge_kernel(
    data_ref, trig_ref, first_ref, second_ref, third_ref, before_ref, out_ref, padded_ref, *, groups
):
    del before_ref
    beams, width = data_ref.shape[2], data_ref.shape[3]

    def turn(i, product, row, col):
        real = product[row : row + beams, col : col + width]
        imag = product[row : row + beams, col + width : col + 2 * width]
        cosine, sine = trig_ref[i, 0], trig_ref[i, 1]
        return cosine * real - sine * imag, sine * real + cosine * imag

    def add(a, b):
        return a[0] + b[0], a[1] + b[1]

    sums = {}
    for low in range(2):
        for group in range(groups):
            source = (group * 2 + low) * 2
            stacked = jnp.concatenate(
                [
                    jnp.concatenate([data_ref[source + core, part] for part in range(2)], axis=1)
                    for core in range(2)
                ],
                axis=0,
            )
            product = jnp.dot(first_ref[...], stacked, preferred_element_type=jnp.float32)
            for half in range(2):
                terms = [
                    turn(half * 2 + child, product, (half * 2 + child) * beams, 0)
                    for child in range(2)
                ]
                level = tuple(
                    v.astype(jnp.bfloat16).astype(jnp.float32) for v in add(terms[0], terms[1])
                )
                sums[low, half] = level if group == 0 else add(sums[low, half], level)
    middle = {}
    for low in range(2):
        for half in range(2):
            parts = [halves_of(v) for v in sums[low, half]]
            stacked = jnp.concatenate(
                [jnp.concatenate([parts[0][i], parts[1][i]], axis=1) for i in range(2)], axis=0
            )
            product = jnp.dot(second_ref[...], stacked, preferred_element_type=jnp.float32)
            for next_half in range(2):
                middle[low, half, next_half] = turn(4 + next_half, product, next_half * beams, 0)
    merged = 8 * beams
    padding = padded_ref.shape[1] - HALO - merged
    for part in range(2):
        padded_ref[part, 0:HALO, :] = jnp.zeros((HALO, width), jnp.float32)
        padded_ref[part, HALO + merged :, :] = jnp.zeros((padding, width), jnp.float32)
    for half in range(2):
        for next_half in range(2):
            rows = []
            for low in range(2):
                parts = [halves_of(v) for v in middle[low, half, next_half]]
                rows += [jnp.concatenate([parts[0][i], parts[1][i]], axis=1) for i in range(2)]
            product = jnp.dot(
                third_ref[...], jnp.concatenate(rows, axis=0), preferred_element_type=jnp.float32
            )
            for last in range(2):
                terms = [
                    turn(6 + last * 2 + child, product, (last * 2 + child) * beams, 0)
                    for child in range(2)
                ]
                start = HALO + (half * 4 + next_half * 2 + last) * beams
                for part, value in enumerate(add(terms[0], terms[1])):
                    padded_ref[part, start : start + beams, :] = value
    for block in range(out_ref.shape[0]):
        for part in range(2):
            rows = padded_ref[part, 8 * block : 8 * block + WINDOW, :]
            out_ref[block, part] = rows.astype(jnp.bfloat16)


def flat(value):
    return jnp.concatenate([value[i : i + 1, :] for i in range(4)], axis=1)


def range_columns(whole_ref, real_ref, step, width):
    place = pl.ds(step * 4, 4)
    row_ids = lax.broadcasted_iota(jnp.int16, (width, 4 * LANES), 0)
    inner = flat(whole_ref[0, place, :])
    frac = flat(real_ref[1, place, :])
    low, high = (1.0 - frac).astype(jnp.bfloat16), frac.astype(jnp.bfloat16)
    first, second = inner.astype(jnp.int16), (inner + 1).astype(jnp.int16)
    return jnp.where(row_ids == first, low, jnp.where(row_ids == second, high, jnp.bfloat16(0)))


def weights_kernel(whole_ref, real_ref, out_ref):
    def chunk(step, carry):
        out_ref[step] = range_columns(whole_ref, real_ref, 2 * step, out_ref.shape[1])
        return carry

    lax.fori_loop(0, out_ref.shape[0], chunk, 0)


def sample_kernel(
    table_ref,
    column_ref,
    whole_ref,
    real_ref,
    pixel_ref,
    out_ref,
    block_ref,
    lhs_ref,
    cart_ref,
    order_ref,
):
    slices, parts, _, width = table_ref.shape
    blocks = slices + 1
    rows = parts * QUARTER
    lane = lax.broadcasted_iota(jnp.int32, (WINDOW, width), 1)
    for part in range(parts):
        values = [table_ref[i, part].astype(jnp.float32) for i in range(slices)]
        block_ref[0, part] = values[0]
        for k in range(1, blocks):
            before = pltpu.roll(values[k - 1], k, 1)
            after = pltpu.roll(values[k], k, 1) if k < slices else before
            block_ref[k, part] = jnp.where(lane < k, before, after)
    beam_ids = lax.broadcasted_iota(jnp.int32, (QUARTER, column_ref.shape[2]), 0)

    def chunk(quarter, step, columns):
        place = pl.ds(step * 4, 4)
        outer, beam = flat(whole_ref[1, place, :]), flat(whole_ref[2, place, :])
        frac = flat(real_ref[0, place, :])
        product = jnp.dot(lhs_ref[quarter], columns, preferred_element_type=jnp.float32)
        outer = jnp.broadcast_to(outer, (QUARTER, outer.shape[1]))
        picked = [product[part * QUARTER : (part + 1) * QUARTER] for part in range(parts)]
        for k in range(1, blocks):
            here = outer == k
            for part in range(parts):
                row = k * rows + part * QUARTER
                picked[part] = jnp.where(here, product[row : row + QUARTER], picked[part])
        weights = jnp.where(
            beam_ids == beam, 1.0 - frac, jnp.where(beam_ids == beam + 1, frac, 0.0)
        )
        for part in range(parts):
            summed = jnp.sum(weights * picked[part], axis=0, keepdims=True)
            for i in range(4):
                cart_ref[part, pl.ds(step * 4 + i, 1), :] = summed[:, i * LANES : (i + 1) * LANES]

    for quarter in range(4):
        low = 2 * quarter + 2
        for k in range(blocks):
            pair = [block_ref[k, part, low : low + QUARTER, :] for part in range(parts)]
            lhs_ref[quarter, k * rows : (k + 1) * rows, :] = jnp.concatenate(pair, axis=0).astype(
                jnp.bfloat16
            )
        for i in range(2):
            step = quarter * 4 + 2 * i
            chunk(quarter, step, column_ref[quarter * 2 + i])
            chunk(quarter, step + 1, range_columns(whole_ref, real_ref, step + 1, width))
    for group in range(ROWS // 32):
        ordered = [
            swap_quarters(
                [
                    cart_ref[part, quarter * 16 + group * 8 : quarter * 16 + group * 8 + 8, :]
                    for quarter in range(4)
                ]
            )
            for part in range(parts)
        ]
        for j in range(4):
            start = group * 32 + 8 * j
            cosine = pixel_ref[0, start : start + 8, :]
            sine = pixel_ref[1, start : start + 8, :]
            real, imag = ordered[0][j], ordered[1][j]
            order_ref[pl.ds(2 * start, 8, stride=2), :] = cosine * real - sine * imag
            order_ref[pl.ds(2 * start + 1, 8, stride=2), :] = sine * real + cosine * imag
    out_ref[...] = order_ref[...].astype(jnp.bfloat16)


def blend_kernel(tile_ref, above_ref, height_ref, out_ref):
    for block in range(tile_ref.shape[0]):
        height = height_ref[block * 4 : block * 4 + 4, :]
        value = (1.0 - height) * tile_ref[block] + height * above_ref[block]
        for row in range(out_ref.shape[0]):
            out_ref[row, 0, :, block * LANES : (block + 1) * LANES] = value[2 * row : 2 * row + 2]


def body(
    polar_beams,
    band_start,
    band_weight,
    phase_rate,
    layer_wave,
    beam_map,
    range_map,
    pixel_frac,
    *,
    interpret=False,
):
    sub_index = lax.axis_index("sub")
    sub_count = lax.axis_size("sub")
    layers = lax.axis_size("hgt")
    beams = polar_beams.shape[2]
    range_count = polar_beams.shape[3]
    levels = band_start.shape[0]
    taps = band_weight.shape[-1]
    row_count, column_count = beam_map.shape
    members = sub_count // 2
    width = range_count // members
    halves = [[s for s in range(sub_count) if s >> 1 & 1 == half] for half in range(2)]
    place = sub_index.astype(jnp.int32).reshape(1)
    smem = pl.BlockSpec(memory_space=pltpu.SMEM)
    vmem = pl.BlockSpec(memory_space=pltpu.VMEM)
    shape = jax.ShapeDtypeStruct
    limit = pltpu.CompilerParams(vmem_limit_bytes=24 * 2**20)
    f32, bf16 = jnp.float32, jnp.bfloat16

    kept = shape if interpret else pltpu.VMEM

    def local(value):
        return value if interpret else pltpu.with_memory_space_constraint(value, pltpu.VMEM)

    slices = polar_beams.reshape(2, beams // 8, 8, members, width // LANES, LANES)
    slices = slices.transpose(3, 0, 1, 4, 2, 5)
    slices = lax.all_to_all(slices, "sub", 0, 0, axis_index_groups=halves, tiled=True)
    slices = slices.transpose(0, 1, 2, 4, 3, 5).reshape(members, 2, beams, width)
    slices = local(slices)
    trig, first, second, third, whole, real, pixel, height = pl.pallas_call(
        functools.partial(prepare_kernel, range_count=range_count),
        out_shape=[
            kept((10, 2, beams, width), f32),
            kept((4 * beams, 2 * beams), bf16),
            kept((2 * beams, 2 * beams), bf16),
            kept((4 * beams, 4 * beams), bf16),
            kept((3, row_count, LANES), jnp.int32),
            kept((2, row_count, LANES), f32),
            kept((2, row_count, LANES), f32),
            kept((4 * members, LANES), f32),
        ],
        grid_spec=pltpu.PrefetchScalarGridSpec(
            num_scalar_prefetch=1,
            grid=(1,),
            in_specs=[
                smem,
                pl.BlockSpec(band_start.shape, lambda i, p: (0, 0, 0, 0)),
                pl.BlockSpec((levels, 2, 2, taps, beams), lambda i, p: (0, 0, 0, 0, 0)),
                pl.BlockSpec(phase_rate.shape, lambda i, p: (0, 0, 0, 0)),
                pl.BlockSpec((row_count, LANES), lambda i, p: (0, block_of(p[0]))),
                pl.BlockSpec((row_count, LANES), lambda i, p: (0, block_of(p[0]))),
                pl.BlockSpec((2, row_count, LANES), lambda i, p: (0, 0, block_of(p[0]))),
                pl.BlockSpec((1, 16, column_count), lambda i, p: (2, p[0] >> 3, 0)),
            ],
            out_specs=[
                pl.BlockSpec((10, 2, beams, width), lambda i, p: (0, 0, 0, 0)),
                pl.BlockSpec((4 * beams, 2 * beams), lambda i, p: (0, 0)),
                pl.BlockSpec((2 * beams, 2 * beams), lambda i, p: (0, 0)),
                pl.BlockSpec((4 * beams, 4 * beams), lambda i, p: (0, 0)),
                pl.BlockSpec((3, row_count, LANES), lambda i, p: (0, 0, 0)),
                pl.BlockSpec((2, row_count, LANES), lambda i, p: (0, 0, 0)),
                pl.BlockSpec((2, row_count, LANES), lambda i, p: (0, 0, 0)),
                pl.BlockSpec((4 * members, LANES), lambda i, p: (0, 0)),
            ],
            scratch_shapes=[
                pltpu.VMEM((LANES, LANES), f32),
                pltpu.VMEM((members, 16, LANES), f32),
            ],
        ),
        interpret=interpret,
        name="prepare",
    )(
        place,
        layer_wave,
        band_start,
        band_weight.transpose(0, 1, 2, 4, 3),
        phase_rate,
        beam_map,
        range_map,
        pixel_frac,
        pixel_frac,
    )
    columns = pl.pallas_call(
        weights_kernel,
        out_shape=kept((row_count // 8, width, 4 * LANES), bf16),
        in_specs=[vmem, vmem],
        out_specs=vmem,
        compiler_params=limit,
        interpret=interpret,
        name="weights",
    )(local(whole), local(real))
    windows = pl.pallas_call(
        functools.partial(merge_kernel, groups=sub_count // 2**levels),
        out_shape=kept((members, 2, WINDOW, width), bf16),
        in_specs=[vmem] * 5 + [pl.BlockSpec(memory_space=pl.ANY)],
        out_specs=vmem,
        scratch_shapes=[pltpu.VMEM((2, 144, width), f32)],
        compiler_params=limit,
        interpret=interpret,
        name="merge",
    )(slices, local(trig), local(first), local(second), local(third), local(columns))
    table = local(lax.all_to_all(windows, "sub", 0, 0, axis_index_groups=halves, tiled=True))
    cart = pl.pallas_call(
        sample_kernel,
        out_shape=kept((2 * row_count, LANES), bf16),
        in_specs=[vmem] * 5,
        out_specs=vmem,
        scratch_shapes=[
            pltpu.VMEM((members + 1, 2, WINDOW, width), f32),
            pltpu.VMEM((4, (members + 1) * 2 * QUARTER, width), bf16),
            pltpu.VMEM((2, row_count, LANES), f32),
            pltpu.VMEM((2 * row_count, LANES), f32),
        ],
        compiler_params=limit,
        interpret=interpret,
        name="sample",
    )(table, local(columns), local(whole), local(real), local(pixel))
    tile_rows = row_count // sub_count
    tiles = cart.reshape(sub_count, tile_rows * 2, LANES)
    tiles = lax.all_to_all(tiles, "sub", 0, 0, tiled=True).astype(f32)
    tiles = tiles.reshape(sub_count // 4, 2, 2 * tile_rows * 2, LANES)
    tile = (tiles[:, 0] + tiles[:, 1]).reshape(members, tile_rows * 2, LANES)
    above = lax.ppermute(tile, "hgt", [(i, i - 1) for i in range(1, layers)])
    return pl.pallas_call(
        blend_kernel,
        out_shape=shape((tile_rows, 1, 2, column_count), f32),
        in_specs=[vmem] * 3,
        out_specs=vmem,
        interpret=interpret,
        name="blend",
    )(local(tile), local(above), local(height))


def solution(mesh):
    in_specs = (P("hgt", None, "sub", None), P(), P(), P(), P("hgt"), P(), P(), P())
    out_specs = P("sub", "hgt", None, None)
    return jax.shard_map(body, mesh=mesh, in_specs=in_specs, out_specs=out_specs, check_vma=False)
```

```python
import functools

import jax
import jax.numpy as jnp
from jax import lax
from jax.experimental import pallas as pl
from jax.experimental.pallas import tpu as pltpu
from jax.sharding import PartitionSpec as P

range_phase = 0.003
LANES = 128
WINDOW = 16
SENT = 13
PACKED = 56
HALO = 2
QUARTER = 8
ROWS = 64


def swap_quarters(values):
    lane = lax.broadcasted_iota(jnp.int32, values[0].shape, 1)
    values = list(values)
    for bit, width in ((1, 64), (0, 32)):
        keep = lane & width == 0
        for i in range(4):
            if i >> bit & 1:
                continue
            j = i | 1 << bit
            a, b = values[i], values[j]
            values[i] = jnp.where(keep, a, pltpu.roll(b, width, 1))
            values[j] = jnp.where(keep, pltpu.roll(a, LANES - width, 1), b)
    return values


def block_of(sub_index):
    return (sub_index >> 2) * 2 + (sub_index & 1)


def prepare_kernel(
    place_ref,
    wave_ref,
    start_ref,
    weight_ref,
    rate_ref,
    beam_ref,
    range_ref,
    frac_ref,
    tall_ref,
    trig_ref,
    first_ref,
    second_ref,
    third_ref,
    whole_ref,
    real_ref,
    pixel_ref,
    height_ref,
    params_ref,
    tall_scratch,
    *,
    range_count,
):
    wave = wave_ref[0]
    levels, children, halves, taps, beams = weight_ref.shape
    matrices = levels * children * halves
    params_ref[...] = jnp.zeros_like(params_ref)
    for level in range(levels):
        for child in range(children):
            i = (level * children + child) * halves
            params_ref[i : i + halves, 0:beams] = rate_ref[level, child]
            row = matrices + i
            params_ref[row : row + halves, 0:beams] = start_ref[level, child].astype(jnp.float32)
            for half in range(halves):
                row = 2 * matrices + (i + half) * taps
                params_ref[row : row + taps, 0:beams] = weight_ref[level, child, half].astype(
                    jnp.float32
                )
    params = params_ref[...].T[0:beams]
    width = trig_ref.shape[3]
    lane = lax.broadcasted_iota(jnp.int32, (1, width), 1)
    sub_index = place_ref[0]
    column_block = block_of(sub_index)
    position = ((column_block * width + lane).astype(jnp.float32) + 0.5) / range_count
    upper = sub_index >> 1 & 1 == 1

    def column(offset, level, child, half):
        i = offset + (level * 2 + child) * 2 + half
        return params[:, i : i + 1]

    def mine(offset, level, half):
        return jnp.where(upper, column(offset, level, 1, half), column(offset, level, 0, half))

    def weight(tap, level, child, half):
        i = 2 * matrices + ((level * 2 + child) * 2 + half) * taps + tap
        return params[:, i : i + 1]

    rates = [column(0, 0, child, half) for half in range(2) for child in range(2)]
    rates += [mine(0, 1, half) for half in range(2)]
    rates += [column(0, 2, child, half) for half in range(2) for child in range(2)]
    for i, rate in enumerate(rates):
        angles = (wave * rate) * position
        trig_ref[i, 0] = jnp.cos(angles)
        trig_ref[i, 1] = jnp.sin(angles)

    def band(starts, weights):
        ids = lax.broadcasted_iota(jnp.int32, (beams, beams), 1).astype(jnp.float32) - starts
        block = jnp.zeros((beams, beams), jnp.float32)
        for tap in range(taps):
            block = jnp.where(ids == tap, weights[tap], block)
        return block

    def pair_bands(level, copies):
        rows = []
        for half in range(2):
            for child in range(2):
                block = band(
                    column(matrices, level, child, half),
                    [weight(tap, level, child, half) for tap in range(taps)],
                )
                empty = jnp.zeros_like(block)
                rows.append(
                    jnp.concatenate(
                        [block if c == child else empty for c in range(2) for _ in range(copies)],
                        axis=1,
                    )
                )
        return jnp.concatenate(rows, axis=0).astype(jnp.bfloat16)

    first_ref[...] = pair_bands(0, 1)
    third_ref[...] = pair_bands(2, 2)
    rows = []
    for half in range(2):
        block = band(
            mine(matrices, 1, half),
            [
                jnp.where(upper, weight(tap, 1, 1, half), weight(tap, 1, 0, half))
                for tap in range(taps)
            ],
        )
        rows.append(jnp.concatenate([block, block], axis=1))
    second_ref[...] = jnp.concatenate(rows, axis=0).astype(jnp.bfloat16)

    for block in range(height_ref.shape[0] // 4):
        tall_scratch[block] = tall_ref[0, :, block * LANES : (block + 1) * LANES].astype(
            jnp.float32
        )
        tall = tall_scratch[block, pl.ds((sub_index & 7) * 2, 2), :]
        for row in range(4):
            height_ref[pl.ds(block * 4 + row, 1), :] = tall[row // 2 : row // 2 + 1]
    samples = range_ref[...]
    fracs = [frac_ref[i].astype(jnp.float32) for i in range(2)]
    angles = (wave * range_phase) * (samples.astype(jnp.float32) + fracs[1])
    pixel_ref[0] = jnp.cos(angles)
    pixel_ref[1] = jnp.sin(angles)
    first_beam = column_block * 8 - HALO
    for group in range(ROWS // 32):
        rows = [slice(group * 32 + 8 * j, group * 32 + 8 * j + 8) for j in range(4)]
        sample_parts = swap_quarters([samples[r] for r in rows])
        beam_parts = swap_quarters([beam_ref[r, :] - first_beam for r in rows])
        frac_parts = [swap_quarters([fracs[i][r] for r in rows]) for i in range(2)]
        for quarter in range(4):
            place = slice(quarter * 16 + group * 8, quarter * 16 + group * 8 + 8)
            sample = sample_parts[quarter]
            block = (sample + 1 + (sample >> 8)) >> 8
            whole_ref[0, place, :] = sample - block * (width - 1)
            whole_ref[1, place, :] = block
            whole_ref[2, place, :] = beam_parts[quarter] - 2 * quarter
            for i in range(2):
                real_ref[i, place, :] = frac_parts[i][quarter]


def halves_of(value):
    high = value.astype(jnp.bfloat16)
    return high, (value - high.astype(jnp.float32)).astype(jnp.bfloat16)


def merge_kernel(
    data_ref, trig_ref, first_ref, second_ref, third_ref, before_ref, out_ref, padded_ref, stage_ref, *, groups
):
    del before_ref
    beams, width = data_ref.shape[2], data_ref.shape[3]

    def turn(i, product, row, col):
        real = product[row : row + beams, col : col + width]
        imag = product[row : row + beams, col + width : col + 2 * width]
        cosine, sine = trig_ref[i, 0], trig_ref[i, 1]
        return cosine * real - sine * imag, sine * real + cosine * imag

    def add(a, b):
        return a[0] + b[0], a[1] + b[1]

    sums = {}
    for low in range(2):
        for group in range(groups):
            source = (group * 2 + low) * 2
            stacked = jnp.concatenate(
                [
                    jnp.concatenate([data_ref[source + core, part] for part in range(2)], axis=1)
                    for core in range(2)
                ],
                axis=0,
            )
            product = jnp.dot(first_ref[...], stacked, preferred_element_type=jnp.float32)
            for half in range(2):
                terms = [
                    turn(half * 2 + child, product, (half * 2 + child) * beams, 0)
                    for child in range(2)
                ]
                level = tuple(
                    v.astype(jnp.bfloat16).astype(jnp.float32) for v in add(terms[0], terms[1])
                )
                sums[low, half] = level if group == 0 else add(sums[low, half], level)
    middle = {}
    for low in range(2):
        for half in range(2):
            parts = [halves_of(v) for v in sums[low, half]]
            stacked = jnp.concatenate(
                [jnp.concatenate([parts[0][i], parts[1][i]], axis=1) for i in range(2)], axis=0
            )
            product = jnp.dot(second_ref[...], stacked, preferred_element_type=jnp.float32)
            for next_half in range(2):
                middle[low, half, next_half] = turn(4 + next_half, product, next_half * beams, 0)
    merged = 8 * beams
    padding = padded_ref.shape[1] - HALO - merged
    for part in range(2):
        padded_ref[part, 0:HALO, :] = jnp.zeros((HALO, width), jnp.float32)
        padded_ref[part, HALO + merged :, :] = jnp.zeros((padding, width), jnp.float32)
    for half in range(2):
        for next_half in range(2):
            rows = []
            for low in range(2):
                parts = [halves_of(v) for v in middle[low, half, next_half]]
                rows += [jnp.concatenate([parts[0][i], parts[1][i]], axis=1) for i in range(2)]
            product = jnp.dot(
                third_ref[...], jnp.concatenate(rows, axis=0), preferred_element_type=jnp.float32
            )
            for last in range(2):
                terms = [
                    turn(6 + last * 2 + child, product, (last * 2 + child) * beams, 0)
                    for child in range(2)
                ]
                start = HALO + (half * 4 + next_half * 2 + last) * beams
                for part, value in enumerate(add(terms[0], terms[1])):
                    padded_ref[part, start : start + beams, :] = value
    for block in range(out_ref.shape[0]):
        for piece in range(width // LANES):
            for part in range(2):
                row = (piece * 2 + part) * SENT
                stage_ref[block, row : row + SENT, :] = padded_ref[
                    part, 8 * block : 8 * block + SENT, piece * LANES : (piece + 1) * LANES
                ]
        row = 2 * (width // LANES) * SENT
        stage_ref[block, row:, :] = jnp.zeros((PACKED - row, LANES), jnp.float32)
        out_ref[block] = stage_ref[block].astype(jnp.bfloat16)


def flat(value):
    return jnp.concatenate([value[i : i + 1, :] for i in range(4)], axis=1)


def range_columns(whole_ref, real_ref, step, width):
    place = pl.ds(step * 4, 4)
    row_ids = lax.broadcasted_iota(jnp.int16, (width, 4 * LANES), 0)
    inner = flat(whole_ref[0, place, :])
    frac = flat(real_ref[1, place, :])
    low, high = (1.0 - frac).astype(jnp.bfloat16), frac.astype(jnp.bfloat16)
    first, second = inner.astype(jnp.int16), (inner + 1).astype(jnp.int16)
    return jnp.where(row_ids == first, low, jnp.where(row_ids == second, high, jnp.bfloat16(0)))


def weights_kernel(whole_ref, real_ref, out_ref):
    def chunk(step, carry):
        out_ref[step] = range_columns(whole_ref, real_ref, 2 * step, out_ref.shape[1])
        return carry

    lax.fori_loop(0, out_ref.shape[0], chunk, 0)


def sample_kernel(
    table_ref,
    column_ref,
    whole_ref,
    real_ref,
    pixel_ref,
    out_ref,
    table_scratch,
    block_ref,
    lhs_ref,
    cart_ref,
    order_ref,
):
    slices = table_ref.shape[0]
    parts, width = block_ref.shape[1], block_ref.shape[3]
    blocks = slices + 1
    for i in range(slices):
        table_scratch[i] = table_ref[i].astype(jnp.float32)
    rows = parts * QUARTER
    lane = lax.broadcasted_iota(jnp.int32, (WINDOW, width), 1)
    for part in range(parts):
        starts = [(piece * parts + part) * SENT for piece in range(width // LANES)]
        values = [
            jnp.concatenate(
                [table_scratch[i, start : start + WINDOW, :] for start in starts], axis=1
            )
            for i in range(slices)
        ]
        block_ref[0, part] = values[0]
        for k in range(1, blocks):
            before = pltpu.roll(values[k - 1], k, 1)
            after = pltpu.roll(values[k], k, 1) if k < slices else before
            block_ref[k, part] = jnp.where(lane < k, before, after)
    beam_ids = lax.broadcasted_iota(jnp.int32, (QUARTER, column_ref.shape[2]), 0)

    def chunk(quarter, step, columns):
        place = pl.ds(step * 4, 4)
        outer, beam = flat(whole_ref[1, place, :]), flat(whole_ref[2, place, :])
        frac = flat(real_ref[0, place, :])
        product = jnp.dot(lhs_ref[quarter], columns, preferred_element_type=jnp.float32)
        outer = jnp.broadcast_to(outer, (QUARTER, outer.shape[1]))
        picked = [product[part * QUARTER : (part + 1) * QUARTER] for part in range(parts)]
        for k in range(1, blocks):
            here = outer == k
            for part in range(parts):
                row = k * rows + part * QUARTER
                picked[part] = jnp.where(here, product[row : row + QUARTER], picked[part])
        weights = jnp.where(
            beam_ids == beam, 1.0 - frac, jnp.where(beam_ids == beam + 1, frac, 0.0)
        )
        for part in range(parts):
            summed = jnp.sum(weights * picked[part], axis=0, keepdims=True)
            for i in range(4):
                cart_ref[part, pl.ds(step * 4 + i, 1), :] = summed[:, i * LANES : (i + 1) * LANES]

    for quarter in range(4):
        low = 2 * quarter
        for k in range(blocks):
            pair = [block_ref[k, part, low : low + QUARTER, :] for part in range(parts)]
            lhs_ref[quarter, k * rows : (k + 1) * rows, :] = jnp.concatenate(pair, axis=0).astype(
                jnp.bfloat16
            )
        for i in range(2):
            step = quarter * 4 + 2 * i
            chunk(quarter, step, column_ref[quarter * 2 + i])
            chunk(quarter, step + 1, range_columns(whole_ref, real_ref, step + 1, width))
    for group in range(ROWS // 32):
        ordered = [
            swap_quarters(
                [
                    cart_ref[part, quarter * 16 + group * 8 : quarter * 16 + group * 8 + 8, :]
                    for quarter in range(4)
                ]
            )
            for part in range(parts)
        ]
        for j in range(4):
            start = group * 32 + 8 * j
            cosine = pixel_ref[0, start : start + 8, :]
            sine = pixel_ref[1, start : start + 8, :]
            real, imag = ordered[0][j], ordered[1][j]
            order_ref[pl.ds(2 * start, 8, stride=2), :] = cosine * real - sine * imag
            order_ref[pl.ds(2 * start + 1, 8, stride=2), :] = sine * real + cosine * imag
    out_ref[...] = order_ref[...].astype(jnp.bfloat16)


def blend_kernel(tile_ref, above_ref, height_ref, out_ref):
    for block in range(tile_ref.shape[0]):
        height = height_ref[block * 4 : block * 4 + 4, :]
        value = (1.0 - height) * tile_ref[block] + height * above_ref[block]
        for row in range(out_ref.shape[0]):
            out_ref[row, 0, :, block * LANES : (block + 1) * LANES] = value[2 * row : 2 * row + 2]


def body(
    polar_beams,
    band_start,
    band_weight,
    phase_rate,
    layer_wave,
    beam_map,
    range_map,
    pixel_frac,
    *,
    interpret=False,
):
    sub_index = lax.axis_index("sub")
    sub_count = lax.axis_size("sub")
    layers = lax.axis_size("hgt")
    beams = polar_beams.shape[2]
    range_count = polar_beams.shape[3]
    levels = band_start.shape[0]
    taps = band_weight.shape[-1]
    row_count, column_count = beam_map.shape
    members = sub_count // 2
    width = range_count // members
    halves = [[s for s in range(sub_count) if s >> 1 & 1 == half] for half in range(2)]
    place = sub_index.astype(jnp.int32).reshape(1)
    smem = pl.BlockSpec(memory_space=pltpu.SMEM)
    vmem = pl.BlockSpec(memory_space=pltpu.VMEM)
    shape = jax.ShapeDtypeStruct
    limit = pltpu.CompilerParams(vmem_limit_bytes=24 * 2**20)
    f32, bf16 = jnp.float32, jnp.bfloat16

    kept = shape if interpret else pltpu.VMEM

    def local(value):
        return value if interpret else pltpu.with_memory_space_constraint(value, pltpu.VMEM)

    slices = polar_beams.reshape(2, beams // 8, 8, members, width // LANES, LANES)
    slices = slices.transpose(3, 0, 1, 4, 2, 5)
    slices = lax.all_to_all(slices, "sub", 0, 0, axis_index_groups=halves, tiled=True)
    slices = slices.transpose(0, 1, 2, 4, 3, 5).reshape(members, 2, beams, width)
    slices = local(slices)
    trig, first, second, third, whole, real, pixel, height = pl.pallas_call(
        functools.partial(prepare_kernel, range_count=range_count),
        out_shape=[
            kept((10, 2, beams, width), f32),
            kept((4 * beams, 2 * beams), bf16),
            kept((2 * beams, 2 * beams), bf16),
            kept((4 * beams, 4 * beams), bf16),
            kept((3, row_count, LANES), jnp.int32),
            kept((2, row_count, LANES), f32),
            kept((2, row_count, LANES), f32),
            kept((4 * members, LANES), f32),
        ],
        grid_spec=pltpu.PrefetchScalarGridSpec(
            num_scalar_prefetch=1,
            grid=(1,),
            in_specs=[
                smem,
                pl.BlockSpec(band_start.shape, lambda i, p: (0, 0, 0, 0)),
                pl.BlockSpec((levels, 2, 2, taps, beams), lambda i, p: (0, 0, 0, 0, 0)),
                pl.BlockSpec(phase_rate.shape, lambda i, p: (0, 0, 0, 0)),
                pl.BlockSpec((row_count, LANES), lambda i, p: (0, block_of(p[0]))),
                pl.BlockSpec((row_count, LANES), lambda i, p: (0, block_of(p[0]))),
                pl.BlockSpec((2, row_count, LANES), lambda i, p: (0, 0, block_of(p[0]))),
                pl.BlockSpec((1, 16, column_count), lambda i, p: (2, p[0] >> 3, 0)),
            ],
            out_specs=[
                pl.BlockSpec((10, 2, beams, width), lambda i, p: (0, 0, 0, 0)),
                pl.BlockSpec((4 * beams, 2 * beams), lambda i, p: (0, 0)),
                pl.BlockSpec((2 * beams, 2 * beams), lambda i, p: (0, 0)),
                pl.BlockSpec((4 * beams, 4 * beams), lambda i, p: (0, 0)),
                pl.BlockSpec((3, row_count, LANES), lambda i, p: (0, 0, 0)),
                pl.BlockSpec((2, row_count, LANES), lambda i, p: (0, 0, 0)),
                pl.BlockSpec((2, row_count, LANES), lambda i, p: (0, 0, 0)),
                pl.BlockSpec((4 * members, LANES), lambda i, p: (0, 0)),
            ],
            scratch_shapes=[
                pltpu.VMEM((LANES, LANES), f32),
                pltpu.VMEM((members, 16, LANES), f32),
            ],
        ),
        interpret=interpret,
        name="prepare",
    )(
        place,
        layer_wave,
        band_start,
        band_weight.transpose(0, 1, 2, 4, 3),
        phase_rate,
        beam_map,
        range_map,
        pixel_frac,
        pixel_frac,
    )
    columns = pl.pallas_call(
        weights_kernel,
        out_shape=kept((row_count // 8, width, 4 * LANES), bf16),
        in_specs=[vmem, vmem],
        out_specs=vmem,
        compiler_params=limit,
        interpret=interpret,
        name="weights",
    )(local(whole), local(real))
    windows = pl.pallas_call(
        functools.partial(merge_kernel, groups=sub_count // 2**levels),
        out_shape=kept((members, PACKED, LANES), bf16),
        in_specs=[vmem] * 5 + [pl.BlockSpec(memory_space=pl.ANY)],
        out_specs=vmem,
        scratch_shapes=[
            pltpu.VMEM((2, 144, width), f32),
            pltpu.VMEM((members, PACKED, LANES), f32),
        ],
        compiler_params=limit,
        interpret=interpret,
        name="merge",
    )(slices, local(trig), local(first), local(second), local(third), local(columns))
    table = local(lax.all_to_all(windows, "sub", 0, 0, axis_index_groups=halves, tiled=True))
    cart = pl.pallas_call(
        sample_kernel,
        out_shape=kept((2 * row_count, LANES), bf16),
        in_specs=[vmem] * 5,
        out_specs=vmem,
        scratch_shapes=[
            pltpu.VMEM((members, PACKED, LANES), f32),
            pltpu.VMEM((members + 1, 2, WINDOW, width), f32),
            pltpu.VMEM((4, (members + 1) * 2 * QUARTER, width), bf16),
            pltpu.VMEM((2, row_count, LANES), f32),
            pltpu.VMEM((2 * row_count, LANES), f32),
        ],
        compiler_params=limit,
        interpret=interpret,
        name="sample",
    )(table, local(columns), local(whole), local(real), local(pixel))
    tile_rows = row_count // sub_count
    tiles = cart.reshape(sub_count, tile_rows * 2, LANES)
    tiles = lax.all_to_all(tiles, "sub", 0, 0, tiled=True).astype(f32)
    tiles = tiles.reshape(sub_count // 4, 2, 2 * tile_rows * 2, LANES)
    tile = (tiles[:, 0] + tiles[:, 1]).reshape(members, tile_rows * 2, LANES)
    above = lax.ppermute(tile, "hgt", [(i, i - 1) for i in range(1, layers)])
    return pl.pallas_call(
        blend_kernel,
        out_shape=shape((tile_rows, 1, 2, column_count), f32),
        in_specs=[vmem] * 3,
        out_specs=vmem,
        interpret=interpret,
        name="blend",
    )(local(tile), local(above), local(height))


def solution(mesh):
    in_specs = (P("hgt", None, "sub", None), P(), P(), P(), P("hgt"), P(), P(), P())
    out_specs = P("sub", "hgt", None, None)
    return jax.shard_map(body, mesh=mesh, in_specs=in_specs, out_specs=out_specs, check_vma=False)
```

```python
import functools

import jax
import jax.numpy as jnp
from jax import lax
from jax.experimental import pallas as pl
from jax.experimental.pallas import tpu as pltpu
from jax.sharding import PartitionSpec as P

range_phase = 0.003
LANES = 128
WINDOW = 16
SENT = 13
PACKED = 56
HALO = 2
QUARTER = 8
ROWS = 64


def swap_quarters(values):
    lane = lax.broadcasted_iota(jnp.int32, values[0].shape, 1)
    values = list(values)
    for bit, width in ((1, 64), (0, 32)):
        keep = lane & width == 0
        for i in range(4):
            if i >> bit & 1:
                continue
            j = i | 1 << bit
            a, b = values[i], values[j]
            values[i] = jnp.where(keep, a, pltpu.roll(b, width, 1))
            values[j] = jnp.where(keep, pltpu.roll(a, LANES - width, 1), b)
    return values


def block_of(sub_index):
    return (sub_index >> 2) * 2 + (sub_index & 1)


def prepare_kernel(
    place_ref,
    wave_ref,
    start_ref,
    weight_ref,
    rate_ref,
    beam_ref,
    range_ref,
    frac_ref,
    tall_ref,
    trig_ref,
    first_ref,
    second_ref,
    third_ref,
    whole_ref,
    real_ref,
    pixel_ref,
    height_ref,
    params_ref,
    tall_scratch,
    *,
    range_count,
):
    wave = wave_ref[0]
    levels, children, halves, taps, beams = weight_ref.shape
    matrices = levels * children * halves
    params_ref[...] = jnp.zeros_like(params_ref)
    for level in range(levels):
        for child in range(children):
            i = (level * children + child) * halves
            params_ref[i : i + halves, 0:beams] = rate_ref[level, child]
            row = matrices + i
            params_ref[row : row + halves, 0:beams] = start_ref[level, child].astype(jnp.float32)
            for half in range(halves):
                row = 2 * matrices + (i + half) * taps
                params_ref[row : row + taps, 0:beams] = weight_ref[level, child, half].astype(
                    jnp.float32
                )
    params = params_ref[...].T[0:beams]
    width = trig_ref.shape[3]
    lane = lax.broadcasted_iota(jnp.int32, (1, width), 1)
    sub_index = place_ref[0]
    column_block = block_of(sub_index)
    position = ((column_block * width + lane).astype(jnp.float32) + 0.5) / range_count
    upper = sub_index >> 1 & 1 == 1

    def column(offset, level, child, half):
        i = offset + (level * 2 + child) * 2 + half
        return params[:, i : i + 1]

    def mine(offset, level, half):
        return jnp.where(upper, column(offset, level, 1, half), column(offset, level, 0, half))

    def weight(tap, level, child, half):
        i = 2 * matrices + ((level * 2 + child) * 2 + half) * taps + tap
        return params[:, i : i + 1]

    rates = [column(0, 0, child, half) for half in range(2) for child in range(2)]
    rates += [mine(0, 1, half) for half in range(2)]
    rates += [column(0, 2, child, half) for half in range(2) for child in range(2)]
    for i, rate in enumerate(rates):
        angles = (wave * rate) * position
        trig_ref[i, 0] = jnp.cos(angles)
        trig_ref[i, 1] = jnp.sin(angles)

    def band(starts, weights):
        ids = lax.broadcasted_iota(jnp.int32, (beams, beams), 1).astype(jnp.float32) - starts
        block = jnp.zeros((beams, beams), jnp.float32)
        for tap in range(taps):
            block = jnp.where(ids == tap, weights[tap], block)
        return block

    def pair_bands(level, copies):
        rows = []
        for half in range(2):
            for child in range(2):
                block = band(
                    column(matrices, level, child, half),
                    [weight(tap, level, child, half) for tap in range(taps)],
                )
                empty = jnp.zeros_like(block)
                rows.append(
                    jnp.concatenate(
                        [block if c == child else empty for c in range(2) for _ in range(copies)],
                        axis=1,
                    )
                )
        return jnp.concatenate(rows, axis=0).astype(jnp.bfloat16)

    first_ref[...] = pair_bands(0, 1)
    third_ref[...] = pair_bands(2, 2)
    rows = []
    for half in range(2):
        block = band(
            mine(matrices, 1, half),
            [
                jnp.where(upper, weight(tap, 1, 1, half), weight(tap, 1, 0, half))
                for tap in range(taps)
            ],
        )
        rows.append(jnp.concatenate([block, block], axis=1))
    second_ref[...] = jnp.concatenate(rows, axis=0).astype(jnp.bfloat16)

    for block in range(height_ref.shape[0] // 4):
        tall_scratch[block] = tall_ref[0, :, block * LANES : (block + 1) * LANES].astype(
            jnp.float32
        )
        tall = tall_scratch[block, pl.ds((sub_index & 7) * 2, 2), :]
        for row in range(4):
            height_ref[pl.ds(block * 4 + row, 1), :] = tall[row // 2 : row // 2 + 1]
    samples = range_ref[...]
    fracs = [frac_ref[i].astype(jnp.float32) for i in range(2)]
    angles = (wave * range_phase) * (samples.astype(jnp.float32) + fracs[1])
    pixel_ref[0] = jnp.cos(angles)
    pixel_ref[1] = jnp.sin(angles)
    first_beam = column_block * 8 - HALO
    for group in range(ROWS // 32):
        rows = [slice(group * 32 + 8 * j, group * 32 + 8 * j + 8) for j in range(4)]
        sample_parts = swap_quarters([samples[r] for r in rows])
        beam_parts = swap_quarters([beam_ref[r, :] - first_beam for r in rows])
        frac_parts = [swap_quarters([fracs[i][r] for r in rows]) for i in range(2)]
        for quarter in range(4):
            place = slice(quarter * 16 + group * 8, quarter * 16 + group * 8 + 8)
            sample = sample_parts[quarter]
            block = (sample + 1 + (sample >> 8)) >> 8
            whole_ref[0, place, :] = sample - block * (width - 1)
            whole_ref[1, place, :] = block
            whole_ref[2, place, :] = beam_parts[quarter] - 2 * quarter
            for i in range(2):
                real_ref[i, place, :] = frac_parts[i][quarter]


def halves_of(value):
    high = value.astype(jnp.bfloat16)
    return high, (value - high.astype(jnp.float32)).astype(jnp.bfloat16)


def merge_kernel(
    data_ref, trig_ref, first_ref, second_ref, third_ref, before_ref, out_ref, padded_ref, stage_ref, *, groups
):
    del before_ref
    beams, width = data_ref.shape[2], data_ref.shape[3]

    def turn(i, product, row, col):
        real = product[row : row + beams, col : col + width]
        imag = product[row : row + beams, col + width : col + 2 * width]
        cosine, sine = trig_ref[i, 0], trig_ref[i, 1]
        return cosine * real - sine * imag, sine * real + cosine * imag

    def add(a, b):
        return a[0] + b[0], a[1] + b[1]

    sums = {}
    for low in range(2):
        for group in range(groups):
            source = (group * 2 + low) * 2
            stacked = jnp.concatenate(
                [
                    jnp.concatenate([data_ref[source + core, part] for part in range(2)], axis=1)
                    for core in range(2)
                ],
                axis=0,
            )
            product = jnp.dot(first_ref[...], stacked, preferred_element_type=jnp.float32)
            for half in range(2):
                terms = [
                    turn(half * 2 + child, product, (half * 2 + child) * beams, 0)
                    for child in range(2)
                ]
                level = tuple(
                    v.astype(jnp.bfloat16).astype(jnp.float32) for v in add(terms[0], terms[1])
                )
                sums[low, half] = level if group == 0 else add(sums[low, half], level)
    middle = {}
    for low in range(2):
        for half in range(2):
            parts = [halves_of(v) for v in sums[low, half]]
            stacked = jnp.concatenate(
                [jnp.concatenate([parts[0][i], parts[1][i]], axis=1) for i in range(2)], axis=0
            )
            product = jnp.dot(second_ref[...], stacked, preferred_element_type=jnp.float32)
            for next_half in range(2):
                middle[low, half, next_half] = turn(4 + next_half, product, next_half * beams, 0)
    merged = 8 * beams
    padding = padded_ref.shape[1] - HALO - merged
    for part in range(2):
        padded_ref[part, 0:HALO, :] = jnp.zeros((HALO, width), jnp.float32)
        padded_ref[part, HALO + merged :, :] = jnp.zeros((padding, width), jnp.float32)
    for half in range(2):
        for next_half in range(2):
            rows = []
            for low in range(2):
                parts = [halves_of(v) for v in middle[low, half, next_half]]
                rows += [jnp.concatenate([parts[0][i], parts[1][i]], axis=1) for i in range(2)]
            product = jnp.dot(
                third_ref[...], jnp.concatenate(rows, axis=0), preferred_element_type=jnp.float32
            )
            for last in range(2):
                terms = [
                    turn(6 + last * 2 + child, product, (last * 2 + child) * beams, 0)
                    for child in range(2)
                ]
                start = HALO + (half * 4 + next_half * 2 + last) * beams
                for part, value in enumerate(add(terms[0], terms[1])):
                    padded_ref[part, start : start + beams, :] = value
    for block in range(out_ref.shape[0]):
        for piece in range(width // LANES):
            for part in range(2):
                row = (piece * 2 + part) * SENT
                stage_ref[block, row : row + SENT, :] = padded_ref[
                    part, 8 * block : 8 * block + SENT, piece * LANES : (piece + 1) * LANES
                ]
        row = 2 * (width // LANES) * SENT
        stage_ref[block, row:, :] = jnp.zeros((PACKED - row, LANES), jnp.float32)
        out_ref[block] = stage_ref[block].astype(jnp.bfloat16)


def flat(value):
    return jnp.concatenate([value[i : i + 1, :] for i in range(4)], axis=1)


def range_columns(whole_ref, real_ref, step, width):
    place = pl.ds(step * 4, 4)
    row_ids = lax.broadcasted_iota(jnp.int16, (width, 4 * LANES), 0)
    inner = flat(whole_ref[0, place, :])
    frac = flat(real_ref[1, place, :])
    low, high = (1.0 - frac).astype(jnp.bfloat16), frac.astype(jnp.bfloat16)
    first, second = inner.astype(jnp.int16), (inner + 1).astype(jnp.int16)
    return jnp.where(row_ids == first, low, jnp.where(row_ids == second, high, jnp.bfloat16(0)))


def weights_kernel(whole_ref, real_ref, out_ref):
    def chunk(step, carry):
        out_ref[step] = range_columns(whole_ref, real_ref, 2 * step, out_ref.shape[1])
        return carry

    lax.fori_loop(0, out_ref.shape[0], chunk, 0)


def sample_kernel(
    table_ref,
    column_ref,
    whole_ref,
    real_ref,
    pixel_ref,
    out_ref,
    table_scratch,
    block_ref,
    lhs_ref,
    cart_ref,
    order_ref,
):
    slices = table_ref.shape[0]
    parts, width = block_ref.shape[1], block_ref.shape[3]
    blocks = slices + 1
    for i in range(slices):
        table_scratch[i] = table_ref[i].astype(jnp.float32)
    rows = parts * QUARTER
    lane = lax.broadcasted_iota(jnp.int32, (WINDOW, width), 1)
    for part in range(parts):
        starts = [(piece * parts + part) * SENT for piece in range(width // LANES)]
        values = [
            jnp.concatenate(
                [table_scratch[i, start : start + WINDOW, :] for start in starts], axis=1
            )
            for i in range(slices)
        ]
        block_ref[0, part] = values[0]
        for k in range(1, blocks):
            before = pltpu.roll(values[k - 1], k, 1)
            after = pltpu.roll(values[k], k, 1) if k < slices else before
            block_ref[k, part] = jnp.where(lane < k, before, after)
    beam_ids = lax.broadcasted_iota(jnp.int32, (QUARTER, column_ref.shape[2]), 0)

    def chunk(quarter, step, columns):
        place = pl.ds(step * 4, 4)
        outer, beam = flat(whole_ref[1, place, :]), flat(whole_ref[2, place, :])
        frac = flat(real_ref[0, place, :])
        product = jnp.dot(lhs_ref[quarter], columns, preferred_element_type=jnp.float32)
        outer = jnp.broadcast_to(outer, (QUARTER, outer.shape[1]))
        picked = [product[part * QUARTER : (part + 1) * QUARTER] for part in range(parts)]
        for k in range(1, blocks):
            here = outer == k
            for part in range(parts):
                row = k * rows + part * QUARTER
                picked[part] = jnp.where(here, product[row : row + QUARTER], picked[part])
        weights = jnp.where(
            beam_ids == beam, 1.0 - frac, jnp.where(beam_ids == beam + 1, frac, 0.0)
        )
        for part in range(parts):
            summed = jnp.sum(weights * picked[part], axis=0, keepdims=True)
            for i in range(4):
                cart_ref[part, pl.ds(step * 4 + i, 1), :] = summed[:, i * LANES : (i + 1) * LANES]

    for quarter in range(4):
        low = 2 * quarter
        for k in range(blocks):
            pair = [block_ref[k, part, low : low + QUARTER, :] for part in range(parts)]
            lhs_ref[quarter, k * rows : (k + 1) * rows, :] = jnp.concatenate(pair, axis=0).astype(
                jnp.bfloat16
            )
        for i in range(2):
            step = quarter * 4 + 2 * i
            chunk(quarter, step, column_ref[quarter * 2 + i])
            chunk(quarter, step + 1, range_columns(whole_ref, real_ref, step + 1, width))
    for group in range(ROWS // 32):
        ordered = [
            swap_quarters(
                [
                    cart_ref[part, quarter * 16 + group * 8 : quarter * 16 + group * 8 + 8, :]
                    for quarter in range(4)
                ]
            )
            for part in range(parts)
        ]
        for j in range(4):
            start = group * 32 + 8 * j
            cosine = pixel_ref[0, start : start + 8, :]
            sine = pixel_ref[1, start : start + 8, :]
            real, imag = ordered[0][j], ordered[1][j]
            order_ref[pl.ds(2 * start, 8, stride=2), :] = cosine * real - sine * imag
            order_ref[pl.ds(2 * start + 1, 8, stride=2), :] = sine * real + cosine * imag
    out_ref[...] = order_ref[...].astype(jnp.bfloat16)


def blend_kernel(tile_ref, above_ref, height_ref, out_ref):
    def pair(ref, group):
        rows = ref[group * 16 : group * 16 + 16, :].astype(jnp.float32)
        return rows[0:8] + rows[8:16]

    for group in range(tile_ref.shape[0] // 16):
        height = height_ref[group * 8 : group * 8 + 8, :]
        value = (1.0 - height) * pair(tile_ref, group) + height * pair(above_ref, group)
        for core in range(2):
            lanes = slice((group * 2 + core) * LANES, (group * 2 + core + 1) * LANES)
            for row in range(out_ref.shape[0]):
                start = core * 4 + 2 * row
                out_ref[row, 0, :, lanes] = value[start : start + 2]


def body(
    polar_beams,
    band_start,
    band_weight,
    phase_rate,
    layer_wave,
    beam_map,
    range_map,
    pixel_frac,
    *,
    interpret=False,
):
    sub_index = lax.axis_index("sub")
    sub_count = lax.axis_size("sub")
    layers = lax.axis_size("hgt")
    beams = polar_beams.shape[2]
    range_count = polar_beams.shape[3]
    levels = band_start.shape[0]
    taps = band_weight.shape[-1]
    row_count, column_count = beam_map.shape
    members = sub_count // 2
    width = range_count // members
    halves = [[s for s in range(sub_count) if s >> 1 & 1 == half] for half in range(2)]
    place = sub_index.astype(jnp.int32).reshape(1)
    smem = pl.BlockSpec(memory_space=pltpu.SMEM)
    vmem = pl.BlockSpec(memory_space=pltpu.VMEM)
    shape = jax.ShapeDtypeStruct
    limit = pltpu.CompilerParams(vmem_limit_bytes=24 * 2**20)
    f32, bf16 = jnp.float32, jnp.bfloat16

    kept = shape if interpret else pltpu.VMEM

    def local(value):
        return value if interpret else pltpu.with_memory_space_constraint(value, pltpu.VMEM)

    slices = polar_beams.reshape(2, beams // 8, 8, members, width // LANES, LANES)
    slices = slices.transpose(3, 0, 1, 4, 2, 5)
    slices = lax.all_to_all(slices, "sub", 0, 0, axis_index_groups=halves, tiled=True)
    slices = slices.transpose(0, 1, 2, 4, 3, 5).reshape(members, 2, beams, width)
    slices = local(slices)
    trig, first, second, third, whole, real, pixel, height = pl.pallas_call(
        functools.partial(prepare_kernel, range_count=range_count),
        out_shape=[
            kept((10, 2, beams, width), f32),
            kept((4 * beams, 2 * beams), bf16),
            kept((2 * beams, 2 * beams), bf16),
            kept((4 * beams, 4 * beams), bf16),
            kept((3, row_count, LANES), jnp.int32),
            kept((2, row_count, LANES), f32),
            kept((2, row_count, LANES), f32),
            kept((4 * members, LANES), f32),
        ],
        grid_spec=pltpu.PrefetchScalarGridSpec(
            num_scalar_prefetch=1,
            grid=(1,),
            in_specs=[
                smem,
                pl.BlockSpec(band_start.shape, lambda i, p: (0, 0, 0, 0)),
                pl.BlockSpec((levels, 2, 2, taps, beams), lambda i, p: (0, 0, 0, 0, 0)),
                pl.BlockSpec(phase_rate.shape, lambda i, p: (0, 0, 0, 0)),
                pl.BlockSpec((row_count, LANES), lambda i, p: (0, block_of(p[0]))),
                pl.BlockSpec((row_count, LANES), lambda i, p: (0, block_of(p[0]))),
                pl.BlockSpec((2, row_count, LANES), lambda i, p: (0, 0, block_of(p[0]))),
                pl.BlockSpec((1, 16, column_count), lambda i, p: (2, p[0] >> 3, 0)),
            ],
            out_specs=[
                pl.BlockSpec((10, 2, beams, width), lambda i, p: (0, 0, 0, 0)),
                pl.BlockSpec((4 * beams, 2 * beams), lambda i, p: (0, 0)),
                pl.BlockSpec((2 * beams, 2 * beams), lambda i, p: (0, 0)),
                pl.BlockSpec((4 * beams, 4 * beams), lambda i, p: (0, 0)),
                pl.BlockSpec((3, row_count, LANES), lambda i, p: (0, 0, 0)),
                pl.BlockSpec((2, row_count, LANES), lambda i, p: (0, 0, 0)),
                pl.BlockSpec((2, row_count, LANES), lambda i, p: (0, 0, 0)),
                pl.BlockSpec((4 * members, LANES), lambda i, p: (0, 0)),
            ],
            scratch_shapes=[
                pltpu.VMEM((LANES, LANES), f32),
                pltpu.VMEM((members, 16, LANES), f32),
            ],
        ),
        interpret=interpret,
        name="prepare",
    )(
        place,
        layer_wave,
        band_start,
        band_weight.transpose(0, 1, 2, 4, 3),
        phase_rate,
        beam_map,
        range_map,
        pixel_frac,
        pixel_frac,
    )
    columns = pl.pallas_call(
        weights_kernel,
        out_shape=kept((row_count // 8, width, 4 * LANES), bf16),
        in_specs=[vmem, vmem],
        out_specs=vmem,
        compiler_params=limit,
        interpret=interpret,
        name="weights",
    )(local(whole), local(real))
    windows = pl.pallas_call(
        functools.partial(merge_kernel, groups=sub_count // 2**levels),
        out_shape=kept((members, PACKED, LANES), bf16),
        in_specs=[vmem] * 5 + [pl.BlockSpec(memory_space=pl.ANY)],
        out_specs=vmem,
        scratch_shapes=[
            pltpu.VMEM((2, 144, width), f32),
            pltpu.VMEM((members, PACKED, LANES), f32),
        ],
        compiler_params=limit,
        interpret=interpret,
        name="merge",
    )(slices, local(trig), local(first), local(second), local(third), local(columns))
    table = local(lax.all_to_all(windows, "sub", 0, 0, axis_index_groups=halves, tiled=True))
    cart = pl.pallas_call(
        sample_kernel,
        out_shape=kept((2 * row_count, LANES), bf16),
        in_specs=[vmem] * 5,
        out_specs=vmem,
        scratch_shapes=[
            pltpu.VMEM((members, PACKED, LANES), f32),
            pltpu.VMEM((members + 1, 2, WINDOW, width), f32),
            pltpu.VMEM((4, (members + 1) * 2 * QUARTER, width), bf16),
            pltpu.VMEM((2, row_count, LANES), f32),
            pltpu.VMEM((2 * row_count, LANES), f32),
        ],
        compiler_params=limit,
        interpret=interpret,
        name="sample",
    )(table, local(columns), local(whole), local(real), local(pixel))
    tile_rows = row_count // sub_count
    tiles = cart.reshape(sub_count, tile_rows * 2, LANES)
    tiles = lax.all_to_all(tiles, "sub", 0, 0, tiled=True)
    tiles = tiles.reshape(2 * row_count, LANES)
    above = lax.ppermute(tiles, "hgt", [(i, i - 1) for i in range(1, layers)])
    return pl.pallas_call(
        blend_kernel,
        out_shape=shape((tile_rows, 1, 2, column_count), f32),
        in_specs=[vmem] * 3,
        out_specs=vmem,
        interpret=interpret,
        name="blend",
    )(local(tiles), local(above), local(height))


def solution(mesh):
    in_specs = (P("hgt", None, "sub", None), P(), P(), P(), P("hgt"), P(), P(), P())
    out_specs = P("sub", "hgt", None, None)
    return jax.shard_map(body, mesh=mesh, in_specs=in_specs, out_specs=out_specs, check_vma=False)
```

```python
import functools

import jax
import jax.numpy as jnp
from jax import lax
from jax.experimental import pallas as pl
from jax.experimental.pallas import tpu as pltpu
from jax.sharding import PartitionSpec as P

range_phase = 0.003
LANES = 128
WINDOW = 16
SENT = 13
PACKED = 56
HALO = 2
QUARTER = 8
ROWS = 64


def swap_quarters(values):
    lane = lax.broadcasted_iota(jnp.int32, values[0].shape, 1)
    values = list(values)
    for bit, width in ((1, 64), (0, 32)):
        keep = lane & width == 0
        for i in range(4):
            if i >> bit & 1:
                continue
            j = i | 1 << bit
            a, b = values[i], values[j]
            values[i] = jnp.where(keep, a, pltpu.roll(b, width, 1))
            values[j] = jnp.where(keep, pltpu.roll(a, LANES - width, 1), b)
    return values


def block_of(sub_index):
    return (sub_index >> 2) * 2 + (sub_index & 1)


def prepare_kernel(
    place_ref,
    wave_ref,
    start_ref,
    weight_ref,
    rate_ref,
    beam_ref,
    range_ref,
    frac_ref,
    tall_ref,
    trig_ref,
    first_ref,
    second_ref,
    third_ref,
    whole_ref,
    real_ref,
    pixel_ref,
    height_ref,
    params_ref,
    tall_scratch,
    *,
    range_count,
):
    wave = wave_ref[0]
    levels, children, halves, taps, beams = weight_ref.shape
    matrices = levels * children * halves
    params_ref[...] = jnp.zeros_like(params_ref)
    for level in range(levels):
        for child in range(children):
            i = (level * children + child) * halves
            params_ref[i : i + halves, 0:beams] = rate_ref[level, child]
            row = matrices + i
            params_ref[row : row + halves, 0:beams] = start_ref[level, child].astype(jnp.float32)
            for half in range(halves):
                row = 2 * matrices + (i + half) * taps
                params_ref[row : row + taps, 0:beams] = weight_ref[level, child, half].astype(
                    jnp.float32
                )
    params = params_ref[...].T[0:beams]
    width = trig_ref.shape[3]
    lane = lax.broadcasted_iota(jnp.int32, (1, width), 1)
    sub_index = place_ref[0]
    column_block = block_of(sub_index)
    position = ((column_block * width + lane).astype(jnp.float32) + 0.5) / range_count
    upper = sub_index >> 1 & 1 == 1

    def column(offset, level, child, half):
        i = offset + (level * 2 + child) * 2 + half
        return params[:, i : i + 1]

    def mine(offset, level, half):
        return jnp.where(upper, column(offset, level, 1, half), column(offset, level, 0, half))

    def weight(tap, level, child, half):
        i = 2 * matrices + ((level * 2 + child) * 2 + half) * taps + tap
        return params[:, i : i + 1]

    rates = [column(0, 0, child, half) for half in range(2) for child in range(2)]
    rates += [mine(0, 1, half) for half in range(2)]
    rates += [column(0, 2, child, half) for half in range(2) for child in range(2)]
    for i, rate in enumerate(rates):
        angles = (wave * rate) * position
        trig_ref[i, 0] = jnp.cos(angles)
        trig_ref[i, 1] = jnp.sin(angles)

    def band(starts, weights):
        ids = lax.broadcasted_iota(jnp.int32, (beams, beams), 1).astype(jnp.float32) - starts
        block = jnp.zeros((beams, beams), jnp.float32)
        for tap in range(taps):
            block = jnp.where(ids == tap, weights[tap], block)
        return block

    def pair_bands(level, copies):
        rows = []
        for half in range(2):
            for child in range(2):
                block = band(
                    column(matrices, level, child, half),
                    [weight(tap, level, child, half) for tap in range(taps)],
                )
                empty = jnp.zeros_like(block)
                rows.append(
                    jnp.concatenate(
                        [block if c == child else empty for c in range(2) for _ in range(copies)],
                        axis=1,
                    )
                )
        return jnp.concatenate(rows, axis=0).astype(jnp.bfloat16)

    first_ref[...] = pair_bands(0, 1)
    third_ref[...] = pair_bands(2, 2)
    rows = []
    for half in range(2):
        block = band(
            mine(matrices, 1, half),
            [
                jnp.where(upper, weight(tap, 1, 1, half), weight(tap, 1, 0, half))
                for tap in range(taps)
            ],
        )
        rows.append(jnp.concatenate([block, block], axis=1))
    second_ref[...] = jnp.concatenate(rows, axis=0).astype(jnp.bfloat16)

    for block in range(height_ref.shape[0] // 4):
        tall_scratch[block] = tall_ref[0, :, block * LANES : (block + 1) * LANES].astype(
            jnp.float32
        )
        tall = tall_scratch[block, pl.ds((sub_index & 7) * 2, 2), :]
        for row in range(4):
            height_ref[pl.ds(block * 4 + row, 1), :] = tall[row // 2 : row // 2 + 1]
    samples = range_ref[...]
    fracs = [frac_ref[i].astype(jnp.float32) for i in range(2)]
    angles = (wave * range_phase) * (samples.astype(jnp.float32) + fracs[1])
    pixel_ref[0] = jnp.cos(angles)
    pixel_ref[1] = jnp.sin(angles)
    first_beam = column_block * 8 - HALO
    for group in range(ROWS // 32):
        rows = [slice(group * 32 + 8 * j, group * 32 + 8 * j + 8) for j in range(4)]
        sample_parts = swap_quarters([samples[r] for r in rows])
        beam_parts = swap_quarters([beam_ref[r, :] - first_beam for r in rows])
        frac_parts = [swap_quarters([fracs[i][r] for r in rows]) for i in range(2)]
        for quarter in range(4):
            place = slice(quarter * 16 + group * 8, quarter * 16 + group * 8 + 8)
            sample = sample_parts[quarter]
            block = (sample + 1 + (sample >> 8)) >> 8
            whole_ref[0, place, :] = sample - block * (width - 1)
            whole_ref[1, place, :] = block
            whole_ref[2, place, :] = beam_parts[quarter] - 2 * quarter
            for i in range(2):
                real_ref[i, place, :] = frac_parts[i][quarter]


def halves_of(value):
    high = value.astype(jnp.bfloat16)
    return high, (value - high.astype(jnp.float32)).astype(jnp.bfloat16)


def merge_kernel(
    data_ref, trig_ref, first_ref, second_ref, third_ref, before_ref, out_ref, padded_ref, stage_ref, *, groups
):
    del before_ref
    beams, width = data_ref.shape[2], data_ref.shape[3]

    def turn(i, product, row, col):
        real = product[row : row + beams, col : col + width]
        imag = product[row : row + beams, col + width : col + 2 * width]
        cosine, sine = trig_ref[i, 0], trig_ref[i, 1]
        return cosine * real - sine * imag, sine * real + cosine * imag

    def add(a, b):
        return a[0] + b[0], a[1] + b[1]

    sums = {}
    for low in range(2):
        for group in range(groups):
            source = (group * 2 + low) * 2
            stacked = jnp.concatenate(
                [
                    jnp.concatenate([data_ref[source + core, part] for part in range(2)], axis=1)
                    for core in range(2)
                ],
                axis=0,
            )
            product = jnp.dot(first_ref[...], stacked, preferred_element_type=jnp.float32)
            for half in range(2):
                terms = [
                    turn(half * 2 + child, product, (half * 2 + child) * beams, 0)
                    for child in range(2)
                ]
                level = tuple(
                    v.astype(jnp.bfloat16).astype(jnp.float32) for v in add(terms[0], terms[1])
                )
                sums[low, half] = level if group == 0 else add(sums[low, half], level)
    middle = {}
    for low in range(2):
        for half in range(2):
            parts = [halves_of(v) for v in sums[low, half]]
            stacked = jnp.concatenate(
                [jnp.concatenate([parts[0][i], parts[1][i]], axis=1) for i in range(2)], axis=0
            )
            product = jnp.dot(second_ref[...], stacked, preferred_element_type=jnp.float32)
            for next_half in range(2):
                middle[low, half, next_half] = turn(4 + next_half, product, next_half * beams, 0)
    merged = 8 * beams
    padding = padded_ref.shape[1] - HALO - merged
    for part in range(2):
        padded_ref[part, 0:HALO, :] = jnp.zeros((HALO, width), jnp.float32)
        padded_ref[part, HALO + merged :, :] = jnp.zeros((padding, width), jnp.float32)
    for half in range(2):
        for next_half in range(2):
            rows = []
            for low in range(2):
                parts = [halves_of(v) for v in middle[low, half, next_half]]
                rows += [jnp.concatenate([parts[0][i], parts[1][i]], axis=1) for i in range(2)]
            product = jnp.dot(
                third_ref[...], jnp.concatenate(rows, axis=0), preferred_element_type=jnp.float32
            )
            for last in range(2):
                terms = [
                    turn(6 + last * 2 + child, product, (last * 2 + child) * beams, 0)
                    for child in range(2)
                ]
                start = HALO + (half * 4 + next_half * 2 + last) * beams
                for part, value in enumerate(add(terms[0], terms[1])):
                    padded_ref[part, start : start + beams, :] = value
    for block in range(out_ref.shape[0]):
        for piece in range(width // LANES):
            for part in range(2):
                row = (piece * 2 + part) * SENT
                stage_ref[block, row : row + SENT, :] = padded_ref[
                    part, 8 * block : 8 * block + SENT, piece * LANES : (piece + 1) * LANES
                ]
        row = 2 * (width // LANES) * SENT
        stage_ref[block, row:, :] = jnp.zeros((PACKED - row, LANES), jnp.float32)
        out_ref[block] = stage_ref[block].astype(jnp.bfloat16)


def flat(value):
    return jnp.concatenate([value[i : i + 1, :] for i in range(4)], axis=1)


def range_columns(whole_ref, real_ref, step, width):
    place = pl.ds(step * 4, 4)
    row_ids = lax.broadcasted_iota(jnp.int16, (width, 4 * LANES), 0)
    inner = flat(whole_ref[0, place, :])
    frac = flat(real_ref[1, place, :])
    low, high = (1.0 - frac).astype(jnp.bfloat16), frac.astype(jnp.bfloat16)
    first, second = inner.astype(jnp.int16), (inner + 1).astype(jnp.int16)
    return jnp.where(row_ids == first, low, jnp.where(row_ids == second, high, jnp.bfloat16(0)))


def weights_kernel(whole_ref, real_ref, out_ref):
    def chunk(step, carry):
        ahead = jnp.where(step < 8, 2 * step, 2 * step - 15)
        out_ref[step] = range_columns(whole_ref, real_ref, ahead, out_ref.shape[1])
        return carry

    lax.fori_loop(0, out_ref.shape[0], chunk, 0)


def sample_kernel(
    table_ref,
    column_ref,
    whole_ref,
    real_ref,
    pixel_ref,
    out_ref,
    table_scratch,
    block_ref,
    lhs_ref,
    cart_ref,
    order_ref,
):
    slices = table_ref.shape[0]
    parts, width = block_ref.shape[1], block_ref.shape[3]
    blocks = slices + 1
    for i in range(slices):
        table_scratch[i] = table_ref[i].astype(jnp.float32)
    rows = parts * QUARTER
    lane = lax.broadcasted_iota(jnp.int32, (WINDOW, width), 1)
    for part in range(parts):
        starts = [(piece * parts + part) * SENT for piece in range(width // LANES)]
        values = [
            jnp.concatenate(
                [table_scratch[i, start : start + WINDOW, :] for start in starts], axis=1
            )
            for i in range(slices)
        ]
        block_ref[0, part] = values[0]
        for k in range(1, blocks):
            before = pltpu.roll(values[k - 1], k, 1)
            after = pltpu.roll(values[k], k, 1) if k < slices else before
            block_ref[k, part] = jnp.where(lane < k, before, after)
    beam_ids = lax.broadcasted_iota(jnp.int32, (QUARTER, column_ref.shape[2]), 0)

    def chunk(quarter, step, columns):
        place = pl.ds(step * 4, 4)
        outer, beam = flat(whole_ref[1, place, :]), flat(whole_ref[2, place, :])
        frac = flat(real_ref[0, place, :])
        product = jnp.dot(lhs_ref[quarter], columns, preferred_element_type=jnp.float32)
        outer = jnp.broadcast_to(outer, (QUARTER, outer.shape[1]))
        picked = [product[part * QUARTER : (part + 1) * QUARTER] for part in range(parts)]
        for k in range(1, blocks):
            here = outer == k
            for part in range(parts):
                row = k * rows + part * QUARTER
                picked[part] = jnp.where(here, product[row : row + QUARTER], picked[part])
        weights = jnp.where(
            beam_ids == beam, 1.0 - frac, jnp.where(beam_ids == beam + 1, frac, 0.0)
        )
        for part in range(parts):
            summed = jnp.sum(weights * picked[part], axis=0, keepdims=True)
            for i in range(4):
                cart_ref[part, pl.ds(step * 4 + i, 1), :] = summed[:, i * LANES : (i + 1) * LANES]

    for quarter in range(4):
        low = 2 * quarter
        for k in range(blocks):
            pair = [block_ref[k, part, low : low + QUARTER, :] for part in range(parts)]
            lhs_ref[quarter, k * rows : (k + 1) * rows, :] = jnp.concatenate(pair, axis=0).astype(
                jnp.bfloat16
            )
        for i in range(2):
            step = quarter * 4 + 2 * i
            chunk(quarter, step, column_ref[quarter * 2 + i])
            columns = (
                column_ref[8 + i]
                if quarter == 0
                else range_columns(whole_ref, real_ref, step + 1, width)
            )
            chunk(quarter, step + 1, columns)
    for group in range(ROWS // 32):
        ordered = [
            swap_quarters(
                [
                    cart_ref[part, quarter * 16 + group * 8 : quarter * 16 + group * 8 + 8, :]
                    for quarter in range(4)
                ]
            )
            for part in range(parts)
        ]
        for j in range(4):
            start = group * 32 + 8 * j
            cosine = pixel_ref[0, start : start + 8, :]
            sine = pixel_ref[1, start : start + 8, :]
            real, imag = ordered[0][j], ordered[1][j]
            order_ref[pl.ds(2 * start, 8, stride=2), :] = cosine * real - sine * imag
            order_ref[pl.ds(2 * start + 1, 8, stride=2), :] = sine * real + cosine * imag
    out_ref[...] = order_ref[...].astype(jnp.bfloat16)


def blend_kernel(tile_ref, above_ref, height_ref, out_ref):
    def pair(ref, group):
        rows = ref[group * 16 : group * 16 + 16, :].astype(jnp.float32)
        return rows[0:8] + rows[8:16]

    for group in range(tile_ref.shape[0] // 16):
        height = height_ref[group * 8 : group * 8 + 8, :]
        value = (1.0 - height) * pair(tile_ref, group) + height * pair(above_ref, group)
        for core in range(2):
            lanes = slice((group * 2 + core) * LANES, (group * 2 + core + 1) * LANES)
            for row in range(out_ref.shape[0]):
                start = core * 4 + 2 * row
                out_ref[row, 0, :, lanes] = value[start : start + 2]


def body(
    polar_beams,
    band_start,
    band_weight,
    phase_rate,
    layer_wave,
    beam_map,
    range_map,
    pixel_frac,
    *,
    interpret=False,
):
    sub_index = lax.axis_index("sub")
    sub_count = lax.axis_size("sub")
    layers = lax.axis_size("hgt")
    beams = polar_beams.shape[2]
    range_count = polar_beams.shape[3]
    levels = band_start.shape[0]
    taps = band_weight.shape[-1]
    row_count, column_count = beam_map.shape
    members = sub_count // 2
    width = range_count // members
    halves = [[s for s in range(sub_count) if s >> 1 & 1 == half] for half in range(2)]
    place = sub_index.astype(jnp.int32).reshape(1)
    smem = pl.BlockSpec(memory_space=pltpu.SMEM)
    vmem = pl.BlockSpec(memory_space=pltpu.VMEM)
    shape = jax.ShapeDtypeStruct
    limit = pltpu.CompilerParams(vmem_limit_bytes=24 * 2**20)
    f32, bf16 = jnp.float32, jnp.bfloat16

    kept = shape if interpret else pltpu.VMEM

    def local(value):
        return value if interpret else pltpu.with_memory_space_constraint(value, pltpu.VMEM)

    slices = polar_beams.reshape(2, beams // 8, 8, members, width // LANES, LANES)
    slices = slices.transpose(3, 0, 1, 4, 2, 5)
    slices = lax.all_to_all(slices, "sub", 0, 0, axis_index_groups=halves, tiled=True)
    slices = slices.transpose(0, 1, 2, 4, 3, 5).reshape(members, 2, beams, width)
    slices = local(slices)
    trig, first, second, third, whole, real, pixel, height = pl.pallas_call(
        functools.partial(prepare_kernel, range_count=range_count),
        out_shape=[
            kept((10, 2, beams, width), f32),
            kept((4 * beams, 2 * beams), bf16),
            kept((2 * beams, 2 * beams), bf16),
            kept((4 * beams, 4 * beams), bf16),
            kept((3, row_count, LANES), jnp.int32),
            kept((2, row_count, LANES), f32),
            kept((2, row_count, LANES), f32),
            kept((4 * members, LANES), f32),
        ],
        grid_spec=pltpu.PrefetchScalarGridSpec(
            num_scalar_prefetch=1,
            grid=(1,),
            in_specs=[
                smem,
                pl.BlockSpec(band_start.shape, lambda i, p: (0, 0, 0, 0)),
                pl.BlockSpec((levels, 2, 2, taps, beams), lambda i, p: (0, 0, 0, 0, 0)),
                pl.BlockSpec(phase_rate.shape, lambda i, p: (0, 0, 0, 0)),
                pl.BlockSpec((row_count, LANES), lambda i, p: (0, block_of(p[0]))),
                pl.BlockSpec((row_count, LANES), lambda i, p: (0, block_of(p[0]))),
                pl.BlockSpec((2, row_count, LANES), lambda i, p: (0, 0, block_of(p[0]))),
                pl.BlockSpec((1, 16, column_count), lambda i, p: (2, p[0] >> 3, 0)),
            ],
            out_specs=[
                pl.BlockSpec((10, 2, beams, width), lambda i, p: (0, 0, 0, 0)),
                pl.BlockSpec((4 * beams, 2 * beams), lambda i, p: (0, 0)),
                pl.BlockSpec((2 * beams, 2 * beams), lambda i, p: (0, 0)),
                pl.BlockSpec((4 * beams, 4 * beams), lambda i, p: (0, 0)),
                pl.BlockSpec((3, row_count, LANES), lambda i, p: (0, 0, 0)),
                pl.BlockSpec((2, row_count, LANES), lambda i, p: (0, 0, 0)),
                pl.BlockSpec((2, row_count, LANES), lambda i, p: (0, 0, 0)),
                pl.BlockSpec((4 * members, LANES), lambda i, p: (0, 0)),
            ],
            scratch_shapes=[
                pltpu.VMEM((LANES, LANES), f32),
                pltpu.VMEM((members, 16, LANES), f32),
            ],
        ),
        interpret=interpret,
        name="prepare",
    )(
        place,
        layer_wave,
        band_start,
        band_weight.transpose(0, 1, 2, 4, 3),
        phase_rate,
        beam_map,
        range_map,
        pixel_frac,
        pixel_frac,
    )
    columns = pl.pallas_call(
        weights_kernel,
        out_shape=kept((row_count // 8 + 2, width, 4 * LANES), bf16),
        in_specs=[vmem, vmem],
        out_specs=vmem,
        compiler_params=limit,
        interpret=interpret,
        name="weights",
    )(local(whole), local(real))
    windows = pl.pallas_call(
        functools.partial(merge_kernel, groups=sub_count // 2**levels),
        out_shape=kept((members, PACKED, LANES), bf16),
        in_specs=[vmem] * 5 + [pl.BlockSpec(memory_space=pl.ANY)],
        out_specs=vmem,
        scratch_shapes=[
            pltpu.VMEM((2, 144, width), f32),
            pltpu.VMEM((members, PACKED, LANES), f32),
        ],
        compiler_params=limit,
        interpret=interpret,
        name="merge",
    )(slices, local(trig), local(first), local(second), local(third), local(columns))
    table = local(lax.all_to_all(windows, "sub", 0, 0, axis_index_groups=halves, tiled=True))
    cart = pl.pallas_call(
        sample_kernel,
        out_shape=kept((2 * row_count, LANES), bf16),
        in_specs=[vmem] * 5,
        out_specs=vmem,
        scratch_shapes=[
            pltpu.VMEM((members, PACKED, LANES), f32),
            pltpu.VMEM((members + 1, 2, WINDOW, width), f32),
            pltpu.VMEM((4, (members + 1) * 2 * QUARTER, width), bf16),
            pltpu.VMEM((2, row_count, LANES), f32),
            pltpu.VMEM((2 * row_count, LANES), f32),
        ],
        compiler_params=limit,
        interpret=interpret,
        name="sample",
    )(table, local(columns), local(whole), local(real), local(pixel))
    tile_rows = row_count // sub_count
    tiles = cart.reshape(sub_count, tile_rows * 2, LANES)
    tiles = lax.all_to_all(tiles, "sub", 0, 0, tiled=True)
    tiles = tiles.reshape(2 * row_count, LANES)
    above = lax.ppermute(tiles, "hgt", [(i, i - 1) for i in range(1, layers)])
    return pl.pallas_call(
        blend_kernel,
        out_shape=shape((tile_rows, 1, 2, column_count), f32),
        in_specs=[vmem] * 3,
        out_specs=vmem,
        interpret=interpret,
        name="blend",
    )(local(tiles), local(above), local(height))


def solution(mesh):
    in_specs = (P("hgt", None, "sub", None), P(), P(), P(), P("hgt"), P(), P(), P())
    out_specs = P("sub", "hgt", None, None)
    return jax.shard_map(body, mesh=mesh, in_specs=in_specs, out_specs=out_specs, check_vma=False)
```
